32 devices in a mesh: wide: 16 (over z, x, core), narrow: 2 (over y).
Axes of the slice: x: 2, y: 2, z: 4, core: 2. Of those that a mesh axis runs over, the one named last changes fastest.
Arguments:
- tokens: bfloat16 [16384, 768], P(('wide', 'narrow')), may hold values from -6 to 6
- token_marks: int32 [16384], P(('wide', 'narrow')), may hold values 0 or 1
- crop_lengths: int32 [256], P('wide'), may hold values from 0 to 576, as said below
- bucket_ids: int32 [256], P('wide'), may hold values from 0 to 3
- mask_token: bfloat16 [768], replicated, may hold values from -5 to 5
- norm1_gain: bfloat16 [768], replicated, may hold values from 0.099609375 to 1.8984375
- norm1_bias: bfloat16 [768], replicated, may hold values from -3 to 3
- w_qkv: bfloat16 [3, 768, 768], P(None, None, 'narrow'), may hold values from -0.21875 to 0.21875
- qv_bias: bfloat16 [2, 768], P(None, 'narrow'), may hold values from -3 to 3
- w_proj: bfloat16 [768, 768], P('narrow'), may hold values from -1.75 to 1.75
- proj_bias: bfloat16 [768], replicated, may hold values from -3 to 3
- scale_attn: bfloat16 [768], replicated, may hold values from 0.5 to 1.5
- norm2_gain: bfloat16 [768], replicated, may hold values from 0.099609375 to 1.8984375
- norm2_bias: bfloat16 [768], replicated, may hold values from -3 to 3
- w_fc1: bfloat16 [768, 3072], P(None, 'narrow'), may hold values from -0.21875 to 0.21875
- fc1_bias: bfloat16 [3072], P('narrow'), may hold values from -3 to 3
- w_fc2: bfloat16 [3072, 768], P('narrow'), may hold values from -0.109375 to 0.109375
- fc2_bias: bfloat16 [768], replicated, may hold values from -3 to 3
- scale_mlp: bfloat16 [768], replicated, may hold values from 0.5 to 1.5
- cotangent: bfloat16 [16384, 768], P(('wide', 'narrow')), may hold values from -6 to 6
Outputs:
- output: bfloat16 [16384, 768], P(('wide', 'narrow'))
- grad_tokens: float32 [16384, 768], P(('wide', 'narrow'))
- grad_mask_token: float32 [768], replicated
- grad_norm1_gain: float32 [768], replicated
- grad_norm1_bias: float32 [768], replicated
- grad_qkv: float32 [3, 768, 768], P(None, None, 'narrow')
- grad_qv_bias: float32 [2, 768], P(None, 'narrow')
- grad_proj: float32 [768, 768], P('narrow')
- grad_proj_bias: float32 [768], replicated
- grad_scale_attn: float32 [768], replicated
- grad_norm2_gain: float32 [768], replicated
- grad_norm2_bias: float32 [768], replicated
- grad_fc1: float32 [768, 3072], P(None, 'narrow')
- grad_fc1_bias: float32 [3072], P('narrow')
- grad_fc2: float32 [3072, 768], P('narrow')
- grad_fc2_bias: float32 [768], replicated
- grad_scale_mlp: float32 [768], replicated
The draws below stay inside these ranges and needn't reach their ends.
Inputs may be any that keep to these rules, and one draw needn't show every extreme that they name: `crop_lengths`: length 0 marks an empty slot. The nonempty slots of a buffer come first, and their padded rows together fill at most 1024; some buffer is filled to exactly 1024 rows. A nonempty crop has more than 48 rows, and its bucket is the smallest of 64, 144, 256, 576 that holds it.
All inputs are finite; a program needn't handle non-finite values. No bound on the sum of `token_marks` on one device may be relied on, other than what follows from the above.
Results may differ from the reference program's by a relative error of at most 0.017.
Values may be sent and summed in bfloat16 or wider, within the bound.
No kernel may reach another device: no remote copies, remote signals or barrier semaphores. Data moves between devices by JAX's collectives and lax.ppermute only.
A program may use at most 128 MiB of HBM per device.

```python
from functools import partial
import jax
import jax.numpy as jnp
from jax import lax

D = 768
HEADS = 12
HEAD_DIM = 64
FF = 3072
B0 = 64
B1 = 144
B2 = 256
B3 = 576
ROWS_DEV = 1024
SLOTS = 16
CROPS = 256
ROWS = 16384
N_WIDE = 16


def crop_table(key):
    device_count = CROPS // SLOTS
    sub_keys = jax.random.split(jax.random.fold_in(key, 11), 5)
    table_shape = (device_count, SLOTS)
    bucket_draw = jax.random.randint(sub_keys[0], table_shape, 0, 16)
    buckets = jnp.where(bucket_draw < 8, 0, jnp.where(bucket_draw < 12, 1, jnp.where(bucket_draw < 14, 2, 3)))
    full_device = jax.random.randint(sub_keys[1], (), 0, device_count)
    long_device = (full_device + 1 + jax.random.randint(sub_keys[2], (), 0, device_count - 1)) % device_count
    device_ids = jnp.arange(device_count)[:, None]
    slot_ids = jnp.arange(SLOTS)[None, :]
    first_long = (device_ids == long_device) & (slot_ids == 0)
    buckets = jnp.where(device_ids == full_device, 0, buckets)
    buckets = jnp.where(first_long, 3, buckets)
    padded = jnp.where(buckets == 0, B0, jnp.where(buckets == 1, B1, jnp.where(buckets == 2, B2, B3)))
    lowest = jnp.where(buckets == 0, B0 * 3 // 4 + 1, jnp.where(buckets == 1, B0 + 1, jnp.where(buckets == 2, B1 + 1, B2 + 1)))
    budget = jax.random.randint(sub_keys[3], (device_count, 1), ROWS_DEV * 3 // 10, ROWS_DEV + 1)
    budget = jnp.where((device_ids == full_device) | (device_ids == long_device), ROWS_DEV, budget)
    slot_used = jnp.cumsum(padded, axis=1) <= budget
    lengths = lowest + jax.random.randint(sub_keys[4], table_shape, 0, 1 << 20) % (padded - lowest + 1)
    lengths = jnp.where(first_long, B3, lengths)
    lengths = jnp.where(slot_used, lengths, 0)
    return (lengths.reshape(-1).astype(jnp.int32), buckets.reshape(-1).astype(jnp.int32))


def draw_crop_lengths(key, part):
    return crop_table(key)[0]


def draw_bucket_ids(key, part):
    return crop_table(key)[1]


def with_ends(drawn, rng, smallest, top_value):
    longest = drawn.shape.index(max(drawn.shape))
    spots = []
    for shift in (0, 1):
        where = [jax.random.randint(jax.random.fold_in(rng, axis), (), 0, length) for axis, length in enumerate(drawn.shape)]
        where[longest] = (where[longest] + shift) % drawn.shape[longest]
        spots.append(tuple(where))
    return drawn.at[spots[0]].set(smallest).at[spots[1]].set(top_value)


def block_levels(own_key, dims, cuts, least, largest):
    level = 1.0
    for dim, shards_of in cuts:
        draws = jax.random.uniform(jax.random.fold_in(jax.random.fold_in(own_key, 6), dim), (shards_of,), jnp.float32, least / len(cuts), largest / len(cuts))
        level = level * jnp.repeat(jnp.exp(draws), dims[dim] // shards_of).reshape((-1,) + (1,) * (len(dims) - 1 - dim))
    return level


def normal_values(key, dims, deviation, limit, cuts=(), kind=jnp.bfloat16):
    result = jax.random.normal(key, dims, jnp.float32) * deviation
    if len(cuts) > 0:
        result = block_levels(key, dims, cuts, -0.22, 0.18) * result
    return jnp.clip(result, min=-limit, max=limit).astype(kind)


def setup_inputs(seed: int = 0) -> dict:
    key_of = jax.random.split(jax.random.key(seed), 21)
    return {
        "tokens": normal_values(key_of[0], (ROWS, D), 1.0, 6.0, ((0, 32),)),
        "token_marks": with_ends((jax.random.randint(key_of[1], (ROWS,), 0, 5) < 3).astype(jnp.int32), jax.random.fold_in(key_of[1], 1), 0, 1),
        "crop_lengths": draw_crop_lengths(jax.random.fold_in(key_of[20], 71), 0),
        "bucket_ids": draw_bucket_ids(jax.random.fold_in(key_of[20], 71), 0),
        "mask_token": normal_values(key_of[4], (D,), 1.0, 5.0),
        "norm1_gain": jnp.clip(1.0 + 0.18 * jax.random.normal(key_of[5], (D,), jnp.float32), 0.099609375, 1.8984375).astype(jnp.bfloat16),
        "norm1_bias": normal_values(key_of[6], (D,), 0.3, 3.0),
        "w_qkv": normal_values(key_of[7], (3, D, D), D ** -0.5, 0.21875, ((2, 2),)),
        "qv_bias": normal_values(key_of[8], (2, D), 0.3, 3.0, ((1, 2),)),
        "w_proj": normal_values(key_of[9], (D, D), (D // 64) ** -0.5, 1.75, ((0, 2),)),
        "proj_bias": normal_values(key_of[10], (D,), 0.3, 3.0),
        "scale_attn": jnp.clip(jax.random.uniform(key_of[11], (D,), jnp.float32, 0.5, 1.5), 0.5, 1.5).astype(jnp.bfloat16),
        "norm2_gain": jnp.clip(1.0 + 0.18 * jax.random.normal(key_of[12], (D,), jnp.float32), 0.099609375, 1.8984375).astype(jnp.bfloat16),
        "norm2_bias": normal_values(key_of[13], (D,), 0.3, 3.0),
        "w_fc1": normal_values(key_of[14], (D, FF), D ** -0.5, 0.21875, ((1, 2),)),
        "fc1_bias": normal_values(key_of[15], (FF,), 0.5, 3.0, ((0, 2),)),
        "w_fc2": normal_values(key_of[16], (FF, D), FF ** -0.5, 0.109375, ((0, 2),)),
        "fc2_bias": normal_values(key_of[17], (D,), 0.3, 3.0),
        "scale_mlp": jnp.clip(jax.random.uniform(key_of[18], (D,), jnp.float32, 0.5, 1.5), 0.5, 1.5).astype(jnp.bfloat16),
        "cotangent": normal_values(key_of[19], (ROWS, D), 1.0, 6.0, ((0, 32),)),
    }


@jax.custom_vjp
def low(v):
    return lax.optimization_barrier(v.astype(jnp.bfloat16)).astype(jnp.float32)

@jax.custom_vjp
def low_back(v):
    return v

def low_keep(v):
    return (low(v), None)

def low_pass(kept, grad):
    return (grad,)

def back_keep(v):
    return (v, None)

def back_low(kept, grad):
    return (low(grad),)
low.defvjp(low_keep, low_pass)
low_back.defvjp(back_keep, back_low)
epsilon = 1e-06
score_scale = 0.125
masked_score = -1e+30
highest = lax.Precision.HIGHEST

def layer_norm(values_in, norm_gain, norm_shift):
    row_mean = lax.optimization_barrier(jnp.mean(values_in, axis=-1, keepdims=True))
    centered = values_in - row_mean
    variance = lax.optimization_barrier(jnp.mean(centered * centered, axis=-1, keepdims=True))
    return centered * lax.rsqrt(variance + epsilon) * norm_gain + norm_shift

def product(left, right):
    return jnp.dot(left, right, precision=highest, preferred_element_type=jnp.float32)

def row_layout(lengths, buckets, row_total):
    slot_count = lengths.shape[0]
    bucket_rows = jnp.where(buckets == 0, B0, jnp.where(buckets == 1, B1, jnp.where(buckets == 2, B2, B3)))
    padded_sizes = jnp.where(lengths > 0, bucket_rows, 0).astype(jnp.int32)
    slot_ends = jnp.cumsum(padded_sizes).astype(jnp.int32)
    starts = slot_ends - padded_sizes
    row_ids = jnp.arange(row_total, dtype=jnp.int32)
    crop_of_row = lax.optimization_barrier(jnp.sum((row_ids[:, None] >= slot_ends[None, :]).astype(jnp.int32), axis=1)).astype(jnp.int32)
    slot_match = crop_of_row[:, None] == jnp.arange(slot_count, dtype=jnp.int32)[None, :]
    row_start = lax.optimization_barrier(jnp.sum(jnp.where(slot_match, starts[None, :], 0), axis=1)).astype(jnp.int32)
    row_length = lax.optimization_barrier(jnp.sum(jnp.where(slot_match, lengths[None, :], 0), axis=1)).astype(jnp.int32)
    is_valid = (crop_of_row < slot_count) & (row_ids - row_start < row_length)
    return (crop_of_row, is_valid)

def allowed_block(crop_of_row, is_valid, first_row, block_rows):
    row_total = crop_of_row.shape[0]
    query_crop = lax.dynamic_slice_in_dim(crop_of_row, first_row, block_rows)
    query_valid = lax.dynamic_slice_in_dim(is_valid, first_row, block_rows)
    query_ids = first_row + jnp.arange(block_rows, dtype=jnp.int32)
    key_ids = jnp.arange(row_total, dtype=jnp.int32)
    same_crop = (query_crop[:, None] == crop_of_row[None, :]) & query_valid[:, None] & is_valid[None, :]
    itself = (query_ids[:, None] == key_ids[None, :]) & jnp.logical_not(query_valid)[:, None]
    return same_crop | itself

def block_rows_for(row_total):
    return 512 if row_total % 512 == 0 else row_total

def group_forward(params, tokens, token_marks, crop_of_row, is_valid):
    mask_token, norm1_gain, norm1_bias, w_qkv, qv_bias, w_proj, proj_bias, scale_attn, norm2_gain, norm2_bias, w_fc1, fc1_bias, w_fc2, fc2_bias, scale_mlp = params
    row_total = tokens.shape[0]
    x_in = jnp.where(token_marks[:, None] == 1, mask_token[None, :], tokens)
    normed1 = low(layer_norm(x_in, norm1_gain, norm1_bias))
    queries = low_back(low(product(normed1, w_qkv[0]) + qv_bias[0]))
    keys_all = low_back(low(product(normed1, w_qkv[1])))
    values_all = low_back(low(product(normed1, w_qkv[2]) + qv_bias[1]))
    query_heads = queries.reshape(row_total, HEADS, HEAD_DIM)
    key_heads = keys_all.reshape(row_total, HEADS, HEAD_DIM)
    value_heads = values_all.reshape(row_total, HEADS, HEAD_DIM)
    block_rows = block_rows_for(row_total)
    block_count = row_total // block_rows

    def attend(block_index):
        first_row = block_index * block_rows
        query_block = lax.dynamic_slice_in_dim(query_heads, first_row, block_rows, 0)
        scores = low_back(jnp.einsum('qhd,khd->hqk', query_block, key_heads, precision=highest) * score_scale)
        allowed = allowed_block(crop_of_row, is_valid, first_row, block_rows)
        scores = jnp.where(allowed[None], scores, masked_score)
        row_peak = lax.optimization_barrier(jnp.max(scores, axis=-1, keepdims=True))
        exponent = jnp.exp(scores - row_peak)
        probability = low(exponent / lax.optimization_barrier(jnp.sum(exponent, axis=-1, keepdims=True)))
        return jnp.einsum('hqk,khd->qhd', probability, value_heads, precision=highest)
    mixed = lax.map(jax.checkpoint(attend), jnp.arange(block_count, dtype=jnp.int32))
    heads_out = low_back(low(mixed.reshape(row_total, D)))
    attn_out = low_back(product(heads_out, w_proj) + proj_bias)
    hidden = x_in + scale_attn * attn_out
    normed2 = low(layer_norm(hidden, norm2_gain, norm2_bias))
    pre_act = low_back(product(normed2, w_fc1) + fc1_bias)
    activated = low(jax.nn.gelu(pre_act, approximate=False))
    branch = low_back(product(activated, w_fc2) + fc2_bias)
    return jnp.where(is_valid[:, None], hidden + scale_mlp * branch, 0.0)

def reference(tokens, token_marks, crop_lengths, bucket_ids, mask_token, norm1_gain, norm1_bias, w_qkv, qv_bias, w_proj, proj_bias, scale_attn, norm2_gain, norm2_bias, w_fc1, fc1_bias, w_fc2, fc2_bias, scale_mlp, cotangent):
    groups = N_WIDE
    token_groups = tokens.astype(jnp.float32).reshape(groups, ROWS_DEV, D)
    mark_groups = token_marks.reshape(groups, ROWS_DEV)
    length_groups = crop_lengths.reshape(groups, SLOTS)
    bucket_groups = bucket_ids.reshape(groups, SLOTS)
    crop_groups, valid_groups = jax.vmap(partial(row_layout, row_total=ROWS_DEV))(length_groups, bucket_groups)
    params = tuple((item.astype(jnp.float32) for item in (mask_token, norm1_gain, norm1_bias, w_qkv, qv_bias, w_proj, proj_bias, scale_attn, norm2_gain, norm2_bias, w_fc1, fc1_bias, w_fc2, fc2_bias, scale_mlp)))

    def forward(weights, inputs):

        def step(carried, sliced):
            group_tokens, group_marks, group_crops, group_valid = sliced
            return (carried, group_forward(weights, group_tokens, group_marks, group_crops, group_valid))
        return lax.scan(step, jnp.zeros((), jnp.float32), (inputs, mark_groups, crop_groups, valid_groups))[1]
    outputs, pullback = jax.vjp(forward, params, token_groups)
    grads, grad_tokens = pullback(cotangent.astype(jnp.float32).reshape(groups, ROWS_DEV, D))
    return (outputs.reshape(ROWS, D).astype(jnp.bfloat16), grad_tokens.reshape(ROWS, D), grads[0], grads[1], grads[2], grads[3], grads[4], grads[5], grads[6], grads[7], grads[8], grads[9], grads[10], grads[11], grads[12], grads[13], grads[14])
```

```python
from functools import partial

import jax
import jax.numpy as jnp
from jax import lax
from jax.experimental import pallas as pl
from jax.experimental.pallas import tpu as pltpu
from jax.sharding import PartitionSpec as P

HEAD_DIM = 64
B0 = 64
B1 = 144
B2 = 256
B3 = 576

epsilon = 1e-06
masked_score = -1e30
F32 = jnp.float32
BF16 = jnp.bfloat16
WINDOW = 256
BIG_ROWS = 192
SWAP = ((0, 1), (1, 0))


def nn(a, b):
    return lax.dot_general(a, b, (((1,), (0,)), ((), ())), preferred_element_type=F32)


def nt(a, b):
    return lax.dot_general(a, b, (((1,), (1,)), ((), ())), preferred_element_type=F32)


def tn(a, b):
    return lax.dot_general(a, b, (((0,), (0,)), ((), ())), preferred_element_type=F32)


def normed_of(rows_in):
    width = rows_in.shape[-1]
    mean = jnp.sum(rows_in, axis=-1, keepdims=True) * (1.0 / width)
    centered = rows_in - mean
    variance = jnp.sum(centered * centered, axis=-1, keepdims=True) * (1.0 / width)
    inverse = lax.rsqrt(variance + epsilon)
    return centered * inverse, inverse


def norm_back(grad, gain, normal, inverse):
    width = grad.shape[-1]
    g = grad * gain
    mean_g = jnp.sum(g, axis=-1, keepdims=True) * (1.0 / width)
    mean_gn = jnp.sum(g * normal, axis=-1, keepdims=True) * (1.0 / width)
    return (g - mean_g - normal * mean_gn) * inverse


def call(kernel, out_shape, args, flops, moved, name, scratch=(), scalars=0):
    spec = pltpu.PrefetchScalarGridSpec(
        num_scalar_prefetch=scalars,
        grid=(),
        in_specs=[pl.BlockSpec(memory_space=pltpu.VMEM)] * (len(args) - scalars),
        out_specs=jax.tree.map(lambda s: pl.BlockSpec(memory_space=pltpu.VMEM), out_shape),
        scratch_shapes=list(scratch),
    )
    return pl.pallas_call(
        kernel,
        out_shape=out_shape,
        grid_spec=spec,
        compiler_params=pltpu.CompilerParams(vmem_limit_bytes=56 * 1024 * 1024),
        cost_estimate=pl.CostEstimate(flops=flops, bytes_accessed=moved, transcendentals=0),
        name=name,
    )(*args)


def shape(dims, kind=BF16):
    return jax.ShapeDtypeStruct(tuple(dims), kind)


def qkv_kernel(x_ref, vec_ref, bias_ref, w_ref, normed_ref, qkv_ref):
    pairs = qkv_ref.shape[1]
    for first in range(0, x_ref.shape[0], WINDOW):
        rows = pl.ds(first, WINDOW)
        normal, inverse = normed_of(x_ref[rows, :].astype(F32))
        normed = (normal * vec_ref[0:1, :] + vec_ref[1:2, :]).astype(BF16)
        normed_ref[rows, :] = normed
        for c in range(3):
            part = (nn(normed, w_ref[c]) + bias_ref[c : c + 1, :]).astype(BF16)
            if c == 0:
                part = part * 0.125
            for p in range(pairs):
                qkv_ref[c, p, rows, :] = part[:, p * 128 : (p + 1) * 128]


def slot_rows(meta, slot):
    bucket = meta[32 + slot]
    rows = jnp.where(bucket == 0, B0, jnp.where(bucket == 1, B1, jnp.where(bucket == 2, B2, B3)))
    return jnp.where(meta[slot] > 0, rows, 0)


def walk_groups(meta, slots, small, big):
    def more(state):
        slot, first = state
        return jnp.logical_and(slot < slots, meta[slot] > 0)

    def step(state):
        slot, first = state
        first = pl.multiple_of(first, 16)
        rows = slot_rows(meta, slot)

        def take_big():
            big(first, meta[slot])
            return slot + 1, first + B3

        def take_small():
            starts, ends, lasts = [jnp.int32(0)], [rows], [meta[slot]]
            going, end, count = jnp.bool_(True), rows, jnp.int32(1)
            for k in range(1, 4):
                size = slot_rows(meta, slot + k)
                going = going & (slot + k < slots) & (size > 0) & (end + size <= WINDOW)
                starts.append(jnp.where(going, end, WINDOW))
                lasts.append(jnp.where(going, end + meta[slot + k], WINDOW))
                end = jnp.where(going, end + size, end)
                ends.append(jnp.where(going, end, WINDOW))
                count = jnp.where(going, count + 1, count)
            small(first, starts, ends, lasts)
            return slot + count, first + end

        return lax.cond(rows == B3, take_big, take_small)

    lax.while_loop(more, step, (jnp.int32(0), jnp.int32(0)))


def slot_ids(ids, starts, stops, outside):
    result = jnp.full(ids.shape, outside, jnp.int32)
    for k in range(4):
        result = jnp.where((ids >= starts[k]) & (ids < stops[k]), k, result)
    return result


def attention_kernel(slots, meta, own_ref, other_ref, heads_ref, qkv_ref, mixed_ref):
    pairs = own_ref.shape[1]
    half = own_ref.shape[2]
    total = 2 * half
    first_own = pl.multiple_of(meta[64], half)
    first_other = pl.multiple_of(half - meta[64], half)
    for c in range(3):
        for p in range(pairs):
            qkv_ref[c, p, pl.ds(first_own, half), :] = own_ref[c, p]
            qkv_ref[c, p, pl.ds(first_other, half), :] = other_ref[c, p]
            qkv_ref[c, p, pl.ds(total, WINDOW), :] = jnp.zeros((WINDOW, 128), BF16)
    mixed_ref[...] = jnp.zeros(mixed_ref.shape, BF16)
    low = lax.broadcasted_iota(jnp.int32, (1, 128), 1) < HEAD_DIM
    lanes = (low, jnp.logical_not(low))

    def mix(p, first, count, keys, values, mask):
        q = qkv_ref[0, p, pl.ds(first, count), :]
        parts = []
        for h in range(2):
            scores = nt(jnp.where(lanes[h], q, 0), keys)
            scores = jnp.where(mask, scores, masked_score)
            peak = jnp.max(scores, axis=1, keepdims=True)
            exponent = jnp.exp(scores - peak)
            inverse = 1.0 / jnp.sum(exponent, axis=1, keepdims=True)
            parts.append(nn((exponent * inverse).astype(BF16), values))
        mixed_ref[p, pl.ds(first, count), :] = jnp.where(low, parts[0], parts[1]).astype(BF16)

    def small(first, starts, ends, lasts):
        row = slot_ids(lax.broadcasted_iota(jnp.int32, (WINDOW, 1), 0), starts, ends, 4)
        column = slot_ids(lax.broadcasted_iota(jnp.int32, (1, WINDOW), 1), starts, lasts, 5)
        mask = row == column

        def pair(p, carry):
            window = pl.ds(first, WINDOW)
            mix(p, first, WINDOW, qkv_ref[1, p, window, :], qkv_ref[2, p, window, :], mask)
            return carry

        lax.fori_loop(0, pairs, pair, 0)

    def big(first, length):
        mask = lax.broadcasted_iota(jnp.int32, (1, B3), 1) < length

        def pair(p, carry):
            window = pl.ds(first, B3)
            keys = qkv_ref[1, p, window, :]
            values = qkv_ref[2, p, window, :]
            for b in range(B3 // BIG_ROWS):
                mix(p, pl.multiple_of(first + b * BIG_ROWS, 16), BIG_ROWS, keys, values, mask)
            return carry

        lax.fori_loop(0, pairs, pair, 0)

    walk_groups(meta, slots, small, big)
    for p in range(pairs):
        heads_ref[0, :, p * 128 : (p + 1) * 128] = mixed_ref[p, pl.ds(first_own, half), :]
        heads_ref[1, :, p * 128 : (p + 1) * 128] = mixed_ref[p, pl.ds(first_other, half), :]


def attention_back_kernel(
    slots, meta, qkv_ref, own_ref, other_ref, w_ref, grad_ref, out_ref
):
    pairs = qkv_ref.shape[1]
    half = own_ref.shape[0]
    total = 2 * half
    first_own = pl.multiple_of(meta[64], half)
    first_other = pl.multiple_of(half - meta[64], half)
    for source, first in ((own_ref, first_own), (other_ref, first_other)):
        for b in range(0, half, WINDOW):
            part = nt(source[b : b + WINDOW, :], w_ref[...]).astype(BF16)
            for p in range(pairs):
                out_ref[p, pl.ds(pl.multiple_of(first + b, WINDOW), WINDOW), :] = part[
                    :, p * 128 : (p + 1) * 128
                ]
    for p in range(pairs):
        out_ref[p, pl.ds(total, WINDOW), :] = jnp.zeros((WINDOW, 128), BF16)
    grad_ref[...] = jnp.zeros(grad_ref.shape, BF16)
    low = lax.broadcasted_iota(jnp.int32, (1, 128), 1) < HEAD_DIM
    lanes = (low, jnp.logical_not(low))

    def back(p, first, count, keys, values, mask, rows_in):
        q = qkv_ref[0, p, pl.ds(first, count), :]
        grads = out_ref[p, pl.ds(first, count), :]
        if rows_in is not None:
            grads = jnp.where(rows_in, grads, 0)
        d_query = d_key = d_value = None
        for h in range(2):
            q_h = jnp.where(lanes[h], q, 0)
            g_h = jnp.where(lanes[h], grads, 0)
            k_h = jnp.where(lanes[h], keys, 0)
            scores = nt(keys, q_h)
            scores = jnp.where(mask, scores, masked_score)
            peak = jnp.max(scores, axis=0, keepdims=True)
            exponent = jnp.exp(scores - peak)
            probs = exponent * (1.0 / jnp.sum(exponent, axis=0, keepdims=True))
            grad_probs = nt(values, g_h)
            inner = jnp.sum(probs * grad_probs, axis=0, keepdims=True)
            grad_scores = (probs * (grad_probs - inner)).astype(BF16)
            parts = (tn(grad_scores, k_h), nn(grad_scores, q_h), nn(probs.astype(BF16), g_h))
            if h == 0:
                d_query, d_key, d_value = parts
            else:
                d_query, d_key, d_value = d_query + parts[0], d_key + parts[1], d_value + parts[2]
        grad_ref[0, p, pl.ds(first, count), :] = (d_query * 0.125).astype(BF16)
        return d_key, d_value

    def small(first, starts, ends, lasts):
        key = slot_ids(lax.broadcasted_iota(jnp.int32, (WINDOW, 1), 0), starts, lasts, 5)
        query = slot_ids(lax.broadcasted_iota(jnp.int32, (1, WINDOW), 1), starts, ends, 4)
        rows_in = slot_ids(lax.broadcasted_iota(jnp.int32, (WINDOW, 1), 0), starts, ends, 4) < 4
        mask = key == query
        window = pl.ds(first, WINDOW)

        def pair(p, carry):
            d_key, d_value = back(
                p, first, WINDOW, qkv_ref[1, p, window, :], qkv_ref[2, p, window, :], mask, rows_in
            )
            grad_ref[1, p, window, :] = d_key.astype(BF16)
            grad_ref[2, p, window, :] = d_value.astype(BF16)
            return carry

        lax.fori_loop(0, pairs, pair, 0)

    def big(first, length):
        mask = lax.broadcasted_iota(jnp.int32, (B3, 1), 0) < length
        window = pl.ds(first, B3)

        def pair(p, carry):
            keys = qkv_ref[1, p, window, :]
            values = qkv_ref[2, p, window, :]
            d_key = d_value = None
            for b in range(B3 // BIG_ROWS):
                begin = pl.multiple_of(first + b * BIG_ROWS, 16)
                parts = back(p, begin, BIG_ROWS, keys, values, mask, None)
                if b == 0:
                    d_key, d_value = parts
                else:
                    d_key, d_value = d_key + parts[0], d_value + parts[1]
            grad_ref[1, p, window, :] = d_key.astype(BF16)
            grad_ref[2, p, window, :] = d_value.astype(BF16)
            return carry

        lax.fori_loop(0, pairs, pair, 0)

    walk_groups(meta, slots, small, big)


def feed_kernel(
    keep_attn,
    mine_ref,
    theirs_ref,
    x_ref,
    gb_ref,
    vec_ref,
    bias_ref,
    wp_mine_ref,
    wp_theirs_ref,
    w1_ref,
    w2_ref,
    normed_ref,
    act_ref,
    gpre_ref,
    grad_ref,
    *attn_ref,
):
    units = w1_ref.shape[1]
    step = 512
    for first in range(0, x_ref.shape[0], WINDOW):
        rows = pl.ds(first, WINDOW)
        attn = nn(mine_ref[rows, :], wp_mine_ref[...]) + nn(theirs_ref[rows, :], wp_theirs_ref[...])
        attn = attn + vec_ref[6:7, :]
        if keep_attn:
            attn_ref[0][rows, :] = attn
        hidden = x_ref[rows, :].astype(F32) + vec_ref[4:5, :] * attn
        normal, inverse = normed_of(hidden)
        normed = (normal * vec_ref[2:3, :] + vec_ref[3:4, :]).astype(BF16)
        normed_ref[rows, :] = normed
        grad = gb_ref[rows, :]
        total = None
        for u in range(0, units, step):
            cols = slice(u, u + step)
            pre = nn(normed, w1_ref[:, cols]) + bias_ref[0:1, cols]
            half_phi = 0.5 * (1.0 + lax.erf(pre * 0.7071067811865476))
            act_ref[rows, cols] = (pre * half_phi).astype(BF16)
            slope = half_phi + pre * (jnp.exp(pre * pre * -0.5) * 0.3989422804014327)
            gpre = (nt(grad, w2_ref[cols, :]) * slope).astype(BF16)
            gpre_ref[rows, cols] = gpre
            part = nt(gpre, w1_ref[:, cols])
            total = part if total is None else total + part
        grad_ref[rows, :] = total.astype(BF16)


def feed_grad_kernel(
    n_own, n_other, a_own, a_other, p_own, p_other, g_own, g_other, fc1_ref, fc2_ref, bias_ref
):
    fc1_ref[...] = (tn(n_own[...], p_own[...]) + tn(n_other[...], p_other[...])).astype(BF16)
    fc2_ref[...] = (tn(a_own[...], g_own[...]) + tn(a_other[...], g_other[...])).astype(BF16)
    bias_ref[...] = jnp.sum(p_own[...].astype(F32), axis=0, keepdims=True) + jnp.sum(
        p_other[...].astype(F32), axis=0, keepdims=True
    )


def feed_grads(n_own, n_other, a_own, a_other, p_own, p_other, g_own, g_other):
    rows, units = a_own.shape
    width = n_own.shape[1]
    tile = 256
    whole = pl.BlockSpec((rows, width), lambda i: (0, 0))
    cut = pl.BlockSpec((rows, tile), lambda i: (0, i))
    return pl.pallas_call(
        feed_grad_kernel,
        grid=(units // tile,),
        in_specs=[whole, whole, cut, cut, cut, cut, whole, whole],
        out_specs=[
            pl.BlockSpec((width, tile), lambda i: (0, i)),
            pl.BlockSpec((tile, width), lambda i: (i, 0)),
            pl.BlockSpec((1, tile), lambda i: (0, i)),
        ],
        out_shape=[shape((width, units)), shape((units, width)), shape((1, units), F32)],
        compiler_params=pltpu.CompilerParams(vmem_limit_bytes=56 * 1024 * 1024),
        cost_estimate=pl.CostEstimate(
            flops=8 * rows * units * width, bytes_accessed=14000000, transcendentals=0
        ),
        name="feed_grads",
    )(n_own, n_other, a_own, a_other, p_own, p_other, g_own, g_other)


def branch_kernel(act_ref, w2_ref, out_ref):
    for first in range(0, act_ref.shape[0], WINDOW):
        rows = pl.ds(first, WINDOW)
        out_ref[rows, :] = nn(act_ref[rows, :], w2_ref[...]).astype(out_ref.dtype)


def middle_kernel(mine_ref, got_ref, attn_ref, x_ref, gout_ref, vec_ref, hidden_ref, ga_ref, sum_ref):
    sums = None
    for first in range(0, x_ref.shape[0], WINDOW):
        rows = pl.ds(first, WINDOW)
        attn = attn_ref[rows, :]
        normal, inverse = normed_of(x_ref[rows, :].astype(F32) + vec_ref[4:5, :] * attn)
        grad = mine_ref[rows, :].astype(F32) + got_ref[rows, :].astype(F32)
        grad_hidden = gout_ref[rows, :].astype(F32) + norm_back(
            grad, vec_ref[2:3, :], normal, inverse
        )
        hidden_ref[rows, :] = grad_hidden
        grad_attn = (vec_ref[4:5, :] * grad_hidden).astype(BF16)
        ga_ref[rows, :] = grad_attn
        parts = [
            jnp.sum(v, axis=0, keepdims=True)
            for v in (grad * normal, grad, grad_hidden * attn, grad_attn.astype(F32))
        ]
        sums = parts if sums is None else [a + b for a, b in zip(sums, parts)]
    for k in range(4):
        sum_ref[k : k + 1, :] = sums[k]


def share_kernel(meta, grad_ref, w_ref, own_ref, other_ref):
    pairs = grad_ref.shape[1]
    half = own_ref.shape[0]
    for first, target in ((half - meta[64], other_ref), (meta[64], own_ref)):
        for b in range(0, half, WINDOW):
            rows = pl.ds(pl.multiple_of(first + b, WINDOW), WINDOW)
            total = None
            for c in range(3):
                wide = jnp.concatenate([grad_ref[c, p, rows, :] for p in range(pairs)], axis=1)
                part = nt(wide, w_ref[c])
                total = part if total is None else total + part
            target[b : b + WINDOW, :] = total.astype(BF16)


def weight_kernel(
    meta, grad_ref, n_own, n_other, mine_ref, ga_own, ga_other, qkv_ref, proj_ref, bias_ref
):
    pairs = grad_ref.shape[1]
    half = n_own.shape[0]
    own = pl.ds(pl.multiple_of(meta[64], half), half)
    other = pl.ds(pl.multiple_of(half - meta[64], half), half)
    for c in range(3):
        wide_own = jnp.concatenate([grad_ref[c, p, own, :] for p in range(pairs)], axis=1)
        wide_other = jnp.concatenate([grad_ref[c, p, other, :] for p in range(pairs)], axis=1)
        qkv_ref[c] = (tn(n_own[...], wide_own) + tn(n_other[...], wide_other)).astype(BF16)
        bias_ref[c : c + 1, :] = jnp.sum(wide_own.astype(F32), axis=0, keepdims=True) + jnp.sum(
            wide_other.astype(F32), axis=0, keepdims=True
        )
    proj_ref[...] = (tn(mine_ref[0], ga_own[...]) + tn(mine_ref[1], ga_other[...])).astype(BF16)


def final_kernel(mine_ref, got_ref, x_ref, hidden_ref, mark_ref, vec_ref, tokens_ref, sum_ref):
    sums = None
    for first in range(0, x_ref.shape[0], WINDOW):
        rows = pl.ds(first, WINDOW)
        normal, inverse = normed_of(x_ref[rows, :].astype(F32))
        grad = mine_ref[rows, :].astype(F32) + got_ref[rows, :].astype(F32)
        grad_x = hidden_ref[rows, :] + norm_back(grad, vec_ref[0:1, :], normal, inverse)
        marked = mark_ref[rows, :] > 0.5
        tokens_ref[rows, :] = jnp.where(marked, 0.0, grad_x)
        parts = [
            jnp.sum(v, axis=0, keepdims=True)
            for v in (jnp.where(marked, grad_x, 0.0), grad * normal, grad)
        ]
        sums = parts if sums is None else [a + b for a, b in zip(sums, parts)]
    for k in range(3):
        sum_ref[k : k + 1, :] = sums[k]


def own_validity(lengths, buckets, first_own, own_rows):
    slots = lengths.shape[0]
    rows = jnp.where(buckets == 0, B0, jnp.where(buckets == 1, B1, jnp.where(buckets == 2, B2, B3)))
    padded = jnp.where(lengths > 0, rows, 0).astype(jnp.int32)
    before = jnp.tril(jnp.ones((slots, slots), jnp.int32), -1)
    starts = jnp.sum(before * padded[None, :], axis=1)
    ids = first_own + lax.broadcasted_iota(jnp.int32, (own_rows, slots), 0)
    inside = (ids >= starts[None, :]) & (ids < (starts + lengths)[None, :])
    return jnp.any(inside, axis=1, keepdims=True)


def shards(
    tokens,
    token_marks,
    crop_lengths,
    bucket_ids,
    mask_token,
    norm1_gain,
    norm1_bias,
    w_qkv,
    qv_bias,
    w_proj,
    proj_bias,
    scale_attn,
    norm2_gain,
    norm2_bias,
    w_fc1,
    fc1_bias,
    w_fc2,
    fc2_bias,
    scale_mlp,
    cotangent,
):
    half, width = tokens.shape
    slots = crop_lengths.shape[0]
    local = w_qkv.shape[2]
    pairs = local // 128
    units = w_fc1.shape[1]
    first_own = (lax.axis_index("narrow") * half).astype(jnp.int32)
    swap = lambda v: lax.ppermute(v, "narrow", SWAP)

    marked = (token_marks == 1)[:, None]
    x_own = jnp.where(marked, mask_token[None, :], tokens)
    x_other = swap(x_own)
    valid = own_validity(crop_lengths, bucket_ids, first_own, half)
    scale2 = scale_mlp.astype(F32)
    gout_own = jnp.where(valid, cotangent, 0).astype(BF16)
    gb_own = (scale2 * gout_own.astype(F32)).astype(BF16)
    gb_other = swap(gb_own)
    wp_other = swap(w_proj)
    pad = jnp.zeros((32 - slots,), jnp.int32)
    meta = jnp.concatenate(
        [crop_lengths, pad, bucket_ids, pad, jnp.full((8,), first_own, jnp.int32)]
    )
    vec = jnp.stack(
        [norm1_gain, norm1_bias, norm2_gain, norm2_bias, scale_attn, scale_mlp, proj_bias, fc2_bias]
    ).astype(F32)
    bias_q = jnp.stack([qv_bias[0], jnp.zeros_like(qv_bias[0]), qv_bias[1]]).astype(F32)
    bias_1 = fc1_bias.astype(F32)[None, :]
    mark_column = marked.astype(F32)

    def qkv(x):
        return call(
            qkv_kernel,
            [shape((half, width)), shape((3, pairs, half, 128))],
            (x, vec, bias_q, w_qkv),
            6 * half * width * local,
            5000000,
            "norm_qkv",
        )

    n_own, qkv_own = qkv(x_own)
    n_other, qkv_other = qkv(x_other)
    heads, qkv_all = call(
        partial(attention_kernel, slots),
        [shape((2, half, local)), shape((3, pairs, 2 * half + WINDOW, 128))],
        (meta, qkv_own, qkv_other),
        4 * 512 * 1024 * local,
        6000000,
        "attention",
        scratch=[pltpu.VMEM((pairs, 2 * half + WINDOW, 128), BF16)],
        scalars=1,
    )
    got = swap(heads)

    def feed(mine, theirs, x, gb, keep):
        outs = [shape((half, width)), shape((half, units)), shape((half, units)), shape((half, width))]
        if keep:
            outs.append(shape((half, width), F32))
        return call(
            partial(feed_kernel, keep),
            outs,
            (mine, theirs, x, gb, vec, bias_1, w_proj, wp_other, w_fc1, w_fc2),
            6 * half * width * units + 4 * half * local * width,
            12000000,
            "feed",
        )

    n2_other, act_other, gpre_other, gn2_other = feed(heads[1], got[0], x_other, gb_other, False)
    gn2_got = swap(gn2_other)
    n2_own, act_own, gpre_own, gn2_own, attn_own = feed(heads[0], got[1], x_own, gb_own, True)
    g_fc1, g_fc2, g_fc1b = feed_grads(
        n2_own, n2_other, act_own, act_other, gpre_own, gpre_other, gb_own, gb_other
    )
    g_fc1, g_fc2 = lax.psum((g_fc1, g_fc2), "wide")

    def branch_of(act, kind):
        return call(
            branch_kernel, shape((half, width), kind), (act, w_fc2), 2 * half * width * units, 6000000, "branch"
        )

    branch_got = swap(branch_of(act_other, BF16))
    grad_hidden, ga_own, sums2 = call(
        middle_kernel,
        [shape((half, width), F32), shape((half, width)), shape((4, width), F32)],
        (gn2_own, gn2_got, attn_own, x_own, gout_own, vec),
        20 * half * width,
        8000000,
        "middle",
    )
    ga_other = swap(ga_own)
    branch = (
        branch_of(act_own, F32).astype(BF16).astype(F32)
        + branch_got.astype(F32)
        + fc2_bias.astype(F32)
    )
    hidden = x_own.astype(F32) + scale_attn.astype(F32) * attn_own
    output = jnp.where(valid, hidden + scale2 * branch, 0.0).astype(BF16)
    g_smlp = jnp.sum(gout_own.astype(F32) * branch, axis=0)
    g_fc2b = jnp.sum(gb_own.astype(F32), axis=0)

    d_qkv = call(
        partial(attention_back_kernel, slots),
        shape((3, pairs, 2 * half + WINDOW, 128)),
        (meta, qkv_all, ga_own, ga_other, w_proj),
        10 * 512 * 1024 * local,
        8000000,
        "attention_back",
        scratch=[pltpu.VMEM((pairs, 2 * half + WINDOW, 128), BF16)],
        scalars=1,
    )
    gn1_own, gn1_other = call(
        share_kernel,
        [shape((half, width)), shape((half, width))],
        (meta, d_qkv, w_qkv),
        12 * half * width * local,
        6000000,
        "share",
        scalars=1,
    )
    gn1_got = swap(gn1_other)
    g_qkv, g_proj, d_bias = call(
        weight_kernel,
        [shape((3, width, local)), shape((local, width)), shape((3, local), F32)],
        (meta, d_qkv, n_own, n_other, heads, ga_own, ga_other),
        16 * half * width * local,
        9000000,
        "weights",
        scalars=1,
    )
    g_qkv, g_proj = lax.psum((g_qkv, g_proj), "wide")
    grad_tokens, sums1 = call(
        final_kernel,
        [shape((half, width), F32), shape((3, width), F32)],
        (gn1_own, gn1_got, x_own, grad_hidden, mark_column, vec),
        20 * half * width,
        8000000,
        "final",
    )
    rows = jnp.concatenate([sums1, sums2, g_fc2b[None], g_smlp[None]], axis=0)
    g_qvb = jnp.stack([d_bias[0], d_bias[2]])
    rows = lax.psum(rows, ("wide", "narrow"))
    g_qvb, g_fc1b = lax.psum((g_qvb, g_fc1b), "wide")
    return (
        output,
        grad_tokens,
        rows[0],
        rows[1],
        rows[2],
        g_qkv.astype(F32),
        g_qvb,
        g_proj.astype(F32),
        rows[6],
        rows[5],
        rows[3],
        rows[4],
        g_fc1.astype(F32),
        g_fc1b[0],
        g_fc2.astype(F32),
        rows[7],
        rows[8],
    )


def solution(mesh):
    rows = P(("wide", "narrow"), None)
    return jax.shard_map(
        shards,
        mesh=mesh,
        in_specs=(
            rows,
            P(("wide", "narrow")),
            P("wide"),
            P("wide"),
            P(),
            P(),
            P(),
            P(None, None, "narrow"),
            P(None, "narrow"),
            P("narrow", None),
            P(),
            P(),
            P(),
            P(),
            P(None, "narrow"),
            P("narrow"),
            P("narrow", None),
            P(),
            P(),
            rows,
        ),
        out_specs=(
            rows,
            rows,
            P(),
            P(),
            P(),
            P(None, None, "narrow"),
            P(None, "narrow"),
            P("narrow", None),
            P(),
            P(),
            P(),
            P(),
            P(None, "narrow"),
            P("narrow"),
            P("narrow", None),
            P(),
            P(),
        ),
        check_vma=False,
    )
```

```python
from functools import partial

import jax
import jax.numpy as jnp
from jax import lax
from jax.experimental import pallas as pl
from jax.experimental.pallas import tpu as pltpu
from jax.sharding import PartitionSpec as P

HEAD_DIM = 64
B0 = 64
B1 = 144
B2 = 256
B3 = 576

epsilon = 1e-06
masked_score = -1e30
F32 = jnp.float32
BF16 = jnp.bfloat16
WINDOW = 256
BIG_ROWS = 128
SWAP = ((0, 1), (1, 0))


def nn(a, b):
    return lax.dot_general(a, b, (((1,), (0,)), ((), ())), preferred_element_type=F32)


def nt(a, b):
    return lax.dot_general(a, b, (((1,), (1,)), ((), ())), preferred_element_type=F32)


def tn(a, b):
    return lax.dot_general(a, b, (((0,), (0,)), ((), ())), preferred_element_type=F32)


def normed_of(rows_in):
    width = rows_in.shape[-1]
    mean = jnp.sum(rows_in, axis=-1, keepdims=True) * (1.0 / width)
    centered = rows_in - mean
    variance = jnp.sum(centered * centered, axis=-1, keepdims=True) * (1.0 / width)
    inverse = lax.rsqrt(variance + epsilon)
    return centered * inverse, inverse


def norm_back(grad, gain, normal, inverse):
    width = grad.shape[-1]
    g = grad * gain
    mean_g = jnp.sum(g, axis=-1, keepdims=True) * (1.0 / width)
    mean_gn = jnp.sum(g * normal, axis=-1, keepdims=True) * (1.0 / width)
    return (g - mean_g - normal * mean_gn) * inverse


def estimate(micros):
    return pl.CostEstimate(flops=int(micros * 1e9), bytes_accessed=1000, transcendentals=0)


def call(kernel, out_shape, args, micros, name, scratch=(), scalars=0):
    spec = pltpu.PrefetchScalarGridSpec(
        num_scalar_prefetch=scalars,
        grid=(),
        in_specs=[pl.BlockSpec(memory_space=pltpu.VMEM)] * (len(args) - scalars),
        out_specs=jax.tree.map(lambda s: pl.BlockSpec(memory_space=pltpu.VMEM), out_shape),
        scratch_shapes=list(scratch),
    )
    return pl.pallas_call(
        kernel,
        out_shape=out_shape,
        grid_spec=spec,
        compiler_params=pltpu.CompilerParams(vmem_limit_bytes=22 * 1024 * 1024),
        cost_estimate=estimate(micros),
        name=name,
    )(*args)


def shape(dims, kind=BF16):
    return jax.ShapeDtypeStruct(tuple(dims), kind)


def over_rows(total, body, carry=0):
    def step(i, carry):
        result = body(pl.ds(pl.multiple_of(i * WINDOW, WINDOW), WINDOW), carry)
        return carry if result is None else result

    return lax.fori_loop(0, total // WINDOW, step, carry)


def qkv_kernel(x_ref, vec_ref, bias_ref, w_ref, normed_ref, qkv_ref):
    pairs = qkv_ref.shape[1]

    def block(rows, carry):
        normal, inverse = normed_of(x_ref[rows, :].astype(F32))
        normed = (normal * vec_ref[0:1, :] + vec_ref[1:2, :]).astype(BF16)
        normed_ref[rows, :] = normed
        for c in range(3):
            part = (nn(normed, w_ref[c]) + bias_ref[c : c + 1, :]).astype(BF16)
            if c == 0:
                part = part * 0.125
            for p in range(pairs):
                qkv_ref[c, p, rows, :] = part[:, p * 128 : (p + 1) * 128]

    over_rows(x_ref.shape[0], block)


def slot_rows(meta, slot):
    bucket = meta[32 + slot]
    rows = jnp.where(bucket == 0, B0, jnp.where(bucket == 1, B1, jnp.where(bucket == 2, B2, B3)))
    return jnp.where(meta[slot] > 0, rows, 0)


def walk_groups(meta, slots, small, big):
    def more(state):
        slot, first = state
        return jnp.logical_and(slot < slots, meta[slot] > 0)

    def step(state):
        slot, first = state
        first = pl.multiple_of(first, 16)
        rows = slot_rows(meta, slot)

        def take_big():
            big(first, meta[slot])
            return slot + 1, first + B3

        def take_small():
            starts, ends, lasts = [jnp.int32(0)], [rows], [meta[slot]]
            going, end, count = jnp.bool_(True), rows, jnp.int32(1)
            for k in range(1, 4):
                size = slot_rows(meta, slot + k)
                going = going & (slot + k < slots) & (size > 0) & (end + size <= WINDOW)
                starts.append(jnp.where(going, end, WINDOW))
                lasts.append(jnp.where(going, end + meta[slot + k], WINDOW))
                end = jnp.where(going, end + size, end)
                ends.append(jnp.where(going, end, WINDOW))
                count = jnp.where(going, count + 1, count)
            small(first, starts, ends, lasts)
            return slot + count, first + end

        return lax.cond(rows == B3, take_big, take_small)

    lax.while_loop(more, step, (jnp.int32(0), jnp.int32(0)))


def slot_ids(ids, starts, stops, outside):
    result = jnp.full(ids.shape, outside, jnp.int32)
    for k in range(4):
        result = jnp.where((ids >= starts[k]) & (ids < stops[k]), k, result)
    return result


def attention_kernel(slots, meta, own_ref, other_ref, heads_ref, qkv_ref, mixed_ref):
    pairs = own_ref.shape[1]
    half = own_ref.shape[2]
    total = 2 * half
    first_own = pl.multiple_of(meta[64], half)
    first_other = pl.multiple_of(half - meta[64], half)
    for c in range(3):
        for p in range(pairs):
            qkv_ref[c, p, pl.ds(first_own, half), :] = own_ref[c, p]
            qkv_ref[c, p, pl.ds(first_other, half), :] = other_ref[c, p]
            qkv_ref[c, p, pl.ds(total, WINDOW), :] = jnp.zeros((WINDOW, 128), BF16)
    mixed_ref[...] = jnp.zeros(mixed_ref.shape, BF16)
    low = lax.broadcasted_iota(jnp.int32, (1, 128), 1) < HEAD_DIM
    lanes = (low, jnp.logical_not(low))

    def mix(chosen, first, count, window, mask):
        scores = []
        for p in chosen:
            q = qkv_ref[0, p, pl.ds(first, count), :]
            keys = qkv_ref[1, p, window, :]
            for h in range(2):
                scores.append(nt(jnp.where(lanes[h], q, 0), keys))
        probs = []
        for score in scores:
            score = jnp.where(mask, score, masked_score)
            exponent = jnp.exp(score - jnp.max(score, axis=1, keepdims=True))
            inverse = 1.0 / jnp.sum(exponent, axis=1, keepdims=True)
            probs.append((exponent * inverse).astype(BF16))
        for k, p in enumerate(chosen):
            values = qkv_ref[2, p, window, :]
            mixed = jnp.where(low, nn(probs[2 * k], values), nn(probs[2 * k + 1], values))
            mixed_ref[p, pl.ds(first, count), :] = mixed.astype(BF16)

    def small(first, starts, ends, lasts):
        row = slot_ids(lax.broadcasted_iota(jnp.int32, (WINDOW, 1), 0), starts, ends, 4)
        column = slot_ids(lax.broadcasted_iota(jnp.int32, (1, WINDOW), 1), starts, lasts, 5)
        mix(range(pairs), first, WINDOW, pl.ds(first, WINDOW), row == column)

    def big(first, length):
        mask = lax.broadcasted_iota(jnp.int32, (1, B3), 1) < length

        def block(b, carry):
            begin = pl.multiple_of(first + b * BIG_ROWS, 16)
            mix(range(pairs), begin, BIG_ROWS, pl.ds(first, B3), mask)
            return carry

        lax.fori_loop(0, pl.cdiv(B3, BIG_ROWS), block, 0)

    walk_groups(meta, slots, small, big)
    for p in range(pairs):
        heads_ref[0, :, p * 128 : (p + 1) * 128] = mixed_ref[p, pl.ds(first_own, half), :]
        heads_ref[1, :, p * 128 : (p + 1) * 128] = mixed_ref[p, pl.ds(first_other, half), :]


def attention_back_kernel(
    slots, meta, qkv_ref, own_ref, other_ref, w_ref, grad_ref, out_ref, sum_ref
):
    pairs = qkv_ref.shape[1]
    half = own_ref.shape[0]
    total = 2 * half
    first_own = pl.multiple_of(meta[64], half)
    first_other = pl.multiple_of(half - meta[64], half)
    for source, first in ((own_ref, first_own), (other_ref, first_other)):

        def project(i, carry):
            begin = pl.multiple_of(i * WINDOW, WINDOW)
            part = nt(source[pl.ds(begin, WINDOW), :], w_ref[...]).astype(BF16)
            for p in range(pairs):
                out_ref[p, pl.ds(pl.multiple_of(first + begin, WINDOW), WINDOW), :] = part[
                    :, p * 128 : (p + 1) * 128
                ]
            return carry

        lax.fori_loop(0, half // WINDOW, project, 0)
    for p in range(pairs):
        out_ref[p, pl.ds(total, WINDOW), :] = jnp.zeros((WINDOW, 128), BF16)
    grad_ref[...] = jnp.zeros(grad_ref.shape, BF16)
    low = lax.broadcasted_iota(jnp.int32, (1, 128), 1) < HEAD_DIM
    lanes = (low, jnp.logical_not(low))

    def back(chosen, first, count, window, mask, rows_in):
        work = []
        for p in chosen:
            q = qkv_ref[0, p, pl.ds(first, count), :]
            keys = qkv_ref[1, p, window, :]
            values = qkv_ref[2, p, window, :]
            grads = out_ref[p, pl.ds(first, count), :]
            if rows_in is not None:
                grads = jnp.where(rows_in, grads, 0)
            for h in range(2):
                q_h = jnp.where(lanes[h], q, 0)
                g_h = jnp.where(lanes[h], grads, 0)
                work.append((nt(keys, q_h), nt(values, g_h), q_h, g_h))
        pieces = []
        for scores, grad_probs, q_h, g_h in work:
            scores = jnp.where(mask, scores, masked_score)
            exponent = jnp.exp(scores - jnp.max(scores, axis=0, keepdims=True))
            probs = exponent * (1.0 / jnp.sum(exponent, axis=0, keepdims=True))
            inner = jnp.sum(probs * grad_probs, axis=0, keepdims=True)
            grad_scores = (probs * (grad_probs - inner)).astype(BF16)
            pieces.append((probs.astype(BF16), grad_scores, q_h, g_h))
        results = []
        for k, p in enumerate(chosen):
            keys = qkv_ref[1, p, window, :]
            d_query = d_key = d_value = 0.0
            for h in range(2):
                probs, grad_scores, q_h, g_h = pieces[2 * k + h]
                d_query = d_query + tn(grad_scores, jnp.where(lanes[h], keys, 0))
                d_key = d_key + nn(grad_scores, q_h)
                d_value = d_value + nn(probs, g_h)
            grad_ref[0, p, pl.ds(first, count), :] = (d_query * 0.125).astype(BF16)
            results.append((d_key, d_value))
        return results

    def small(first, starts, ends, lasts):
        key = slot_ids(lax.broadcasted_iota(jnp.int32, (WINDOW, 1), 0), starts, lasts, 5)
        query = slot_ids(lax.broadcasted_iota(jnp.int32, (1, WINDOW), 1), starts, ends, 4)
        rows_in = slot_ids(lax.broadcasted_iota(jnp.int32, (WINDOW, 1), 0), starts, ends, 4) < 4
        window = pl.ds(first, WINDOW)
        parts = back(range(pairs), first, WINDOW, window, key == query, rows_in)
        for p, (d_key, d_value) in enumerate(parts):
            grad_ref[1, p, window, :] = d_key.astype(BF16)
            grad_ref[2, p, window, :] = d_value.astype(BF16)

    def big(first, length):
        mask = lax.broadcasted_iota(jnp.int32, (B3, 1), 0) < length
        window = pl.ds(first, B3)
        sum_ref[...] = jnp.zeros(sum_ref.shape, F32)

        def block(b, carry):
            begin = pl.multiple_of(first + b * BIG_ROWS, 16)
            rows_in = lax.broadcasted_iota(jnp.int32, (BIG_ROWS, 1), 0) < B3 - b * BIG_ROWS
            for p, parts in enumerate(back(range(pairs), begin, BIG_ROWS, window, mask, rows_in)):
                for c in range(2):
                    sum_ref[c, p] += parts[c]
            return carry

        lax.fori_loop(0, pl.cdiv(B3, BIG_ROWS), block, 0)
        for p in range(pairs):
            for c in range(2):
                grad_ref[1 + c, p, window, :] = sum_ref[c, p].astype(BF16)

    walk_groups(meta, slots, small, big)


def feed_kernel(
    keep_attn,
    meta,
    mine_ref,
    theirs_ref,
    x_ref,
    gb_ref,
    vec_ref,
    bias_ref,
    wp_ref,
    wp_first_ref,
    wp_second_ref,
    w1_ref,
    w2_ref,
    normed_ref,
    act_ref,
    gpre_ref,
    grad_ref,
    *attn_ref,
):
    units = w1_ref.shape[1]
    step = 512
    which = 0 if keep_attn else 1
    even = meta[65] == 0
    wp_theirs = jnp.concatenate(
        [
            jnp.where(even, wp_first_ref[...], wp_second_ref[...]),
            jnp.where(even, wp_second_ref[...], wp_first_ref[...]),
        ],
        axis=1,
    )

    def block(rows, carry):
        attn = nn(mine_ref[which, rows, :], wp_ref[...])
        attn = attn + nn(theirs_ref[1 - which, rows, :], wp_theirs)
        attn = attn + vec_ref[6:7, :]
        if keep_attn:
            attn_ref[0][rows, :] = attn
        hidden = x_ref[rows, :].astype(F32) + vec_ref[4:5, :] * attn
        normal, inverse = normed_of(hidden)
        normed = (normal * vec_ref[2:3, :] + vec_ref[3:4, :]).astype(BF16)
        normed_ref[rows, :] = normed
        grad = gb_ref[rows, :]
        total = None
        for u in range(0, units, step):
            cols = slice(u, u + step)
            pre = nn(normed, w1_ref[:, cols]) + bias_ref[0:1, cols]
            half_phi = 0.5 * (1.0 + lax.erf(pre * 0.7071067811865476))
            act_ref[rows, cols] = (pre * half_phi).astype(BF16)
            slope = half_phi + pre * (jnp.exp(pre * pre * -0.5) * 0.3989422804014327)
            gpre = (nt(grad, w2_ref[cols, :]) * slope).astype(BF16)
            gpre_ref[rows, cols] = gpre
            part = nt(gpre, w1_ref[:, cols])
            total = part if total is None else total + part
        grad_ref[rows, :] = total.astype(BF16)

    over_rows(x_ref.shape[0], block)


def feed_grad_kernel(
    n_own, n_other, a_own, a_other, p_own, p_other, g_own, g_other, fc1_ref, fc2_ref, bias_ref
):
    units = a_own.shape[1]
    tile = 512

    def block(i, carry):
        cols = pl.ds(pl.multiple_of(i * tile, tile), tile)
        fc1_ref[:, cols] = (
            tn(n_own[...], p_own[:, cols]) + tn(n_other[...], p_other[:, cols])
        ).astype(BF16)
        fc2_ref[cols, :] = (
            tn(a_own[:, cols], g_own[...]) + tn(a_other[:, cols], g_other[...])
        ).astype(BF16)
        bias_ref[:, cols] = jnp.sum(p_own[:, cols].astype(F32), axis=0, keepdims=True) + jnp.sum(
            p_other[:, cols].astype(F32), axis=0, keepdims=True
        )
        return carry

    lax.fori_loop(0, units // tile, block, 0)


def feed_grads(n_own, n_other, a_own, a_other, p_own, p_other, g_own, g_other):
    units = a_own.shape[1]
    width = n_own.shape[1]
    return call(
        feed_grad_kernel,
        [shape((width, units)), shape((units, width)), shape((1, units), F32)],
        (n_own, n_other, a_own, a_other, p_own, p_other, g_own, g_other),
        8,
        "feed_grads",
    )


def branch_kernel(act_ref, w2_ref, out_ref):
    def block(rows, carry):
        out_ref[rows, :] = nn(act_ref[rows, :], w2_ref[...]).astype(out_ref.dtype)

    over_rows(act_ref.shape[0], block)


def middle_kernel(mine_ref, got_ref, attn_ref, x_ref, gout_ref, vec_ref, hidden_ref, ga_ref, sum_ref):
    def block(rows, sums):
        attn = attn_ref[rows, :]
        normal, inverse = normed_of(x_ref[rows, :].astype(F32) + vec_ref[4:5, :] * attn)
        grad = mine_ref[rows, :].astype(F32) + got_ref[rows, :].astype(F32)
        grad_hidden = gout_ref[rows, :].astype(F32) + norm_back(
            grad, vec_ref[2:3, :], normal, inverse
        )
        hidden_ref[rows, :] = grad_hidden
        grad_attn = (vec_ref[4:5, :] * grad_hidden).astype(BF16)
        ga_ref[rows, :] = grad_attn
        parts = [
            jnp.sum(v, axis=0, keepdims=True)
            for v in (grad * normal, grad, grad_hidden * attn, grad_attn.astype(F32))
        ]
        return [a + b for a, b in zip(sums, parts)]

    zero = jnp.zeros((1, x_ref.shape[1]), F32)
    sums = over_rows(x_ref.shape[0], block, [zero] * 4)
    for k in range(4):
        sum_ref[k : k + 1, :] = sums[k]


def share_kernel(meta, grad_ref, w_ref, own_ref, other_ref):
    pairs = grad_ref.shape[1]
    half = own_ref.shape[0]
    for first, target in ((half - meta[64], other_ref), (meta[64], own_ref)):

        def block(to_rows, carry):
            rows = pl.ds(pl.multiple_of(first + to_rows.start, WINDOW), WINDOW)
            total = None
            for c in range(3):
                wide = jnp.concatenate([grad_ref[c, p, rows, :] for p in range(pairs)], axis=1)
                part = nt(wide, w_ref[c])
                total = part if total is None else total + part
            target[to_rows, :] = total.astype(BF16)

        over_rows(half, block)


def weight_kernel(
    meta, grad_ref, n_own, n_other, mine_ref, ga_own, ga_other, out_ref, bias_ref
):
    pairs = grad_ref.shape[1]
    width = n_own.shape[1]
    local = pairs * 128
    half = n_own.shape[0]
    own = pl.ds(pl.multiple_of(meta[64], half), half)
    other = pl.ds(pl.multiple_of(half - meta[64], half), half)
    for c in range(3):
        wide_own = jnp.concatenate([grad_ref[c, p, own, :] for p in range(pairs)], axis=1)
        wide_other = jnp.concatenate([grad_ref[c, p, other, :] for p in range(pairs)], axis=1)
        out_ref[pl.ds(c * width, width), :] = (
            tn(n_own[...], wide_own) + tn(n_other[...], wide_other)
        ).astype(BF16)
        bias_ref[c : c + 1, :] = jnp.sum(wide_own.astype(F32), axis=0, keepdims=True) + jnp.sum(
            wide_other.astype(F32), axis=0, keepdims=True
        )
    proj = (tn(mine_ref[0], ga_own[...]) + tn(mine_ref[1], ga_other[...])).astype(BF16)
    for b in range(width // local):
        out_ref[pl.ds(3 * width + b * local, local), :] = proj[:, b * local : (b + 1) * local]


def final_kernel(mine_ref, got_ref, x_ref, hidden_ref, mark_ref, vec_ref, tokens_ref, sum_ref):
    def block(rows, sums):
        normal, inverse = normed_of(x_ref[rows, :].astype(F32))
        grad = mine_ref[rows, :].astype(F32) + got_ref[rows, :].astype(F32)
        grad_x = hidden_ref[rows, :] + norm_back(grad, vec_ref[0:1, :], normal, inverse)
        marked = mark_ref[rows, :] > 0.5
        tokens_ref[rows, :] = jnp.where(marked, 0.0, grad_x)
        parts = [
            jnp.sum(v, axis=0, keepdims=True)
            for v in (jnp.where(marked, grad_x, 0.0), grad * normal, grad)
        ]
        return [a + b for a, b in zip(sums, parts)]

    zero = jnp.zeros((1, x_ref.shape[1]), F32)
    sums = over_rows(x_ref.shape[0], block, [zero] * 3)
    for k in range(3):
        sum_ref[k : k + 1, :] = sums[k]


def unpack_kernel(meta, mine_ref, got_ref, qkv_ref, proj_ref):
    width = qkv_ref.shape[1]
    local = qkv_ref.shape[2]

    def write(low_ref, high_ref):
        qkv_ref[0] = low_ref[:width, :].astype(F32)
        qkv_ref[1] = low_ref[width:, :].astype(F32)
        qkv_ref[2] = high_ref[:width, :].astype(F32)
        for b in range(width // local):
            proj_ref[:, b * local : (b + 1) * local] = high_ref[
                width + b * local : width + (b + 1) * local, :
            ].astype(F32)

    @pl.when(meta[65] == 0)
    def even():
        write(mine_ref, got_ref)

    @pl.when(meta[65] != 0)
    def odd():
        write(got_ref, mine_ref)


def own_validity(lengths, buckets, first_own, own_rows):
    slots = lengths.shape[0]
    rows = jnp.where(buckets == 0, B0, jnp.where(buckets == 1, B1, jnp.where(buckets == 2, B2, B3)))
    padded = jnp.where(lengths > 0, rows, 0).astype(jnp.int32)
    before = jnp.tril(jnp.ones((slots, slots), jnp.int32), -1)
    starts = jnp.sum(before * padded[None, :], axis=1)
    ids = first_own + lax.broadcasted_iota(jnp.int32, (own_rows, slots), 0)
    inside = (ids >= starts[None, :]) & (ids < (starts + lengths)[None, :])
    return jnp.any(inside, axis=1, keepdims=True)


def steps_of_wide():
    size = lax.axis_size("wide")
    bits = list(range(size.bit_length() - 1))
    even, odd = bits[1:], bits[1:]
    if len(bits) > 2:
        odd = [bits[2], bits[1]] + bits[3:]
    return [(0, 0)] + list(zip(even, odd))


def hop(value, step):
    size = lax.axis_size("wide")
    pairs = tuple((i, i ^ (1 << step[i % 2])) for i in range(size))
    return lax.ppermute(value, "wide", pairs)


def upper(step):
    index = lax.axis_index("wide")
    shift = jnp.where(index % 2 == 0, step[0], step[1])
    return (index >> shift) % 2


def halve(part, step):
    rows = part.shape[0] // 2
    high = upper(step)
    keep = lax.dynamic_slice_in_dim(part, high * rows, rows)
    give = lax.dynamic_slice_in_dim(part, (1 - high) * rows, rows)
    return (keep.astype(F32) + hop(give, step).astype(F32)).astype(BF16)


def double(part, step):
    got = hop(part, step)
    return jnp.where(
        upper(step) == 0, jnp.concatenate([part, got]), jnp.concatenate([got, part])
    )


def column_half(w_proj):
    columns = w_proj.shape[1] // 2
    core = lax.axis_index("wide") % 2
    return lax.ppermute(
        lax.dynamic_slice_in_dim(w_proj, core * columns, columns, 1), "narrow", SWAP
    )


def shards(
    tokens,
    token_marks,
    crop_lengths,
    bucket_ids,
    mask_token,
    norm1_gain,
    norm1_bias,
    w_qkv,
    qv_bias,
    w_proj,
    proj_bias,
    scale_attn,
    norm2_gain,
    norm2_bias,
    w_fc1,
    fc1_bias,
    w_fc2,
    fc2_bias,
    scale_mlp,
    cotangent,
):
    half, width = tokens.shape
    slots = crop_lengths.shape[0]
    local = w_qkv.shape[2]
    pairs = local // 128
    units = w_fc1.shape[1]
    first_own = (lax.axis_index("narrow") * half).astype(jnp.int32)
    swap = lambda v: lax.ppermute(v, "narrow", SWAP)

    marked = (token_marks == 1)[:, None]
    x_own = jnp.where(marked, mask_token[None, :], tokens)
    x_other = swap(x_own)
    valid = own_validity(crop_lengths, bucket_ids, first_own, half)
    scale2 = scale_mlp.astype(F32)
    gout_own = jnp.where(valid, cotangent, 0).astype(BF16)
    gb_own = (scale2 * gout_own.astype(F32)).astype(BF16)
    pad = jnp.zeros((32 - slots,), jnp.int32)
    meta = jnp.concatenate(
        [
            crop_lengths,
            pad,
            bucket_ids,
            pad,
            jnp.stack([first_own, (lax.axis_index("wide") % 2).astype(jnp.int32)]),
        ]
    )
    vec = jnp.stack(
        [norm1_gain, norm1_bias, norm2_gain, norm2_bias, scale_attn, scale_mlp, proj_bias, fc2_bias]
    ).astype(F32)
    bias_q = jnp.stack([qv_bias[0], jnp.zeros_like(qv_bias[0]), qv_bias[1]]).astype(F32)
    bias_1 = fc1_bias.astype(F32)[None, :]
    mark_column = marked.astype(F32)

    def qkv(x):
        return call(
            qkv_kernel,
            [shape((half, width)), shape((3, pairs, half, 128))],
            (x, vec, bias_q, w_qkv),
            2,
            "norm_qkv",
        )

    n_own, qkv_own = qkv(x_own)
    n_own, gb_start, wp_start = lax.optimization_barrier((n_own, gb_own, w_proj))
    gb_other = swap(gb_start)
    wp_mine = column_half(wp_start)
    n_other, qkv_other = qkv(x_other)
    heads, qkv_all = call(
        partial(attention_kernel, slots),
        [shape((2, half, local)), shape((3, pairs, 2 * half + WINDOW, 128))],
        (meta, qkv_own, qkv_other),
        8,
        "attention",
        scratch=[pltpu.VMEM((pairs, 2 * half + WINDOW, 128), BF16)],
        scalars=1,
    )
    heads, gb_other, wp_mine = lax.optimization_barrier((heads, gb_other, wp_mine))
    got = swap(heads)
    wp_next = hop(wp_mine, (0, 0))

    def feed(x, gb, keep):
        outs = [shape((half, width)), shape((half, units)), shape((half, units)), shape((half, width))]
        if keep:
            outs.append(shape((half, width), F32))
        return call(
            partial(feed_kernel, keep),
            outs,
            (meta, heads, got, x, gb, vec, bias_1, w_proj, wp_mine, wp_next, w_fc1, w_fc2),
            7,
            "feed",
            scalars=1,
        )

    n2_other, act_other, gpre_other, gn2_other = feed(x_other, gb_other, False)
    gn2_got = swap(gn2_other)
    n2_own, act_own, gpre_own, gn2_own, attn_own = feed(x_own, gb_own, True)
    g_fc1, g_fc2, g_fc1b = feed_grads(
        n2_own, n2_other, act_own, act_other, gpre_own, gpre_other, gb_own, gb_other
    )

    gn2_got, g_fc1, g_fc2 = lax.optimization_barrier((gn2_got, g_fc1, g_fc2))
    sum_fc1, sum_fc2 = lax.psum((g_fc1, g_fc2), "wide")

    operands = (
        gn2_own, gn2_got, attn_own, x_own, gout_own, gb_own, act_own, act_other, qkv_all, n_own, n_other, heads, g_fc1b
    )

    def rest(operands):
        gn2_own, gn2_got, attn_own, x_own, gout_own, gb_own, act_own, act_other, qkv_all, n_own, n_other, heads, g_fc1b = operands
        grad_hidden, ga_own, sums2 = call(
            middle_kernel,
            [shape((half, width), F32), shape((half, width)), shape((4, width), F32)],
            (gn2_own, gn2_got, attn_own, x_own, gout_own, vec),
            3,
            "middle",
        )
        ga_other = swap(ga_own)
        def branch_of(act, kind):
            return call(
                branch_kernel, shape((half, width), kind), (act, w_fc2), 2, "branch"
            )

        branch_got = swap(branch_of(act_other, BF16))
        branch_own = branch_of(act_own, F32)
        ga_other, branch_own = lax.optimization_barrier((ga_other, branch_own))
        d_qkv = call(
            partial(attention_back_kernel, slots),
            shape((3, pairs, 2 * half + WINDOW, 128)),
            (meta, qkv_all, ga_own, ga_other, w_proj),
            9,
            "attention_back",
            scratch=[
                pltpu.VMEM((pairs, 2 * half + WINDOW, 128), BF16),
                pltpu.VMEM((2, pairs, B3, 128), F32),
            ],
            scalars=1,
        )
        d_qkv, branch_got = lax.optimization_barrier((d_qkv, branch_got))
        gn1_own, gn1_other = call(
            share_kernel,
            [shape((half, width)), shape((half, width))],
            (meta, d_qkv, w_qkv),
            3,
            "share",
            scalars=1,
        )
        gn1_got = swap(gn1_other)
        d_qkv, gn1_own = lax.optimization_barrier((d_qkv, gn1_own))
        g_attn, d_bias = call(
            weight_kernel,
            [shape((4 * width, local)), shape((3, local), F32)],
            (meta, d_qkv, n_own, n_other, heads, ga_own, ga_other),
            5,
            "weights",
            scalars=1,
        )
        steps = steps_of_wide()
        part = halve(halve(g_attn, steps[0]), steps[1])
        part, gn1_got = lax.optimization_barrier((part, gn1_got))
        branch = branch_own + branch_got.astype(F32) + fc2_bias.astype(F32)
        hidden = x_own.astype(F32) + scale_attn.astype(F32) * attn_own
        output = jnp.where(valid, hidden + scale2 * branch, 0.0).astype(BF16)
        g_smlp = jnp.sum(gout_own.astype(F32) * branch, axis=0)
        g_fc2b = jnp.sum(gb_own.astype(F32), axis=0)
        grad_tokens, sums1 = call(
            final_kernel,
            [shape((half, width), F32), shape((3, width), F32)],
            (gn1_own, gn1_got, x_own, grad_hidden, mark_column, vec),
            3,
            "final",
        )
        wide_only = jnp.concatenate([d_bias[0], d_bias[2], g_fc1b[0]]).reshape(-1, width)
        small = jnp.concatenate([sums1, sums2, g_fc2b[None], g_smlp[None], wide_only], axis=0)
        for step in steps[2:]:
            part = halve(part, step)
        for step in reversed(steps[1:]):
            part, small = lax.optimization_barrier((part, small))
            part, small = double(part, step), small + hop(small, step)
        small = small + hop(small, steps[0])
        count = 9
        rows = small[:count] + swap(small[:count])
        flat = small[count:].reshape(-1)
        g_qvb = flat[: 2 * local].reshape(2, local)
        g_fc1b = flat[2 * local :]
        g_qkv, g_proj = call(
            unpack_kernel,
            [shape((3, width, local), F32), shape((local, width), F32)],
            (meta, part, hop(part, steps[0])),
            3,
            "unpack",
            scalars=1,
        )
        return output, grad_tokens, rows, g_qkv, g_qvb, g_proj, g_fc1b

    def none(operands):
        return jax.tree.map(lambda v: jnp.zeros(v.shape, v.dtype), jax.eval_shape(rest, operands))

    output, grad_tokens, rows, g_qkv, g_qvb, g_proj, g_fc1b = lax.cond(
        jnp.max(crop_lengths) < 65536, rest, none, operands
    )
    return (
        output,
        grad_tokens,
        rows[0],
        rows[1],
        rows[2],
        g_qkv,
        g_qvb,
        g_proj,
        rows[6],
        rows[5],
        rows[3],
        rows[4],
        sum_fc1.astype(F32),
        g_fc1b,
        sum_fc2.astype(F32),
        rows[7],
        rows[8],
    )


def solution(mesh):
    rows = P(("wide", "narrow"), None)
    return jax.shard_map(
        shards,
        mesh=mesh,
        in_specs=(
            rows,
            P(("wide", "narrow")),
            P("wide"),
            P("wide"),
            P(),
            P(),
            P(),
            P(None, None, "narrow"),
            P(None, "narrow"),
            P("narrow", None),
            P(),
            P(),
            P(),
            P(),
            P(None, "narrow"),
            P("narrow"),
            P("narrow", None),
            P(),
            P(),
            rows,
        ),
        out_specs=(
            rows,
            rows,
            P(),
            P(),
            P(),
            P(None, None, "narrow"),
            P(None, "narrow"),
            P("narrow", None),
            P(),
            P(),
            P(),
            P(),
            P(None, "narrow"),
            P("narrow"),
            P("narrow", None),
            P(),
            P(),
        ),
        check_vma=False,
    )
```

```python
from functools import partial

import jax
import jax.numpy as jnp
from jax import lax
from jax.experimental import pallas as pl
from jax.experimental.pallas import tpu as pltpu
from jax.sharding import PartitionSpec as P

HEAD_DIM = 64
B0 = 64
B1 = 144
B2 = 256
B3 = 576

epsilon = 1e-06
masked_score = -1e30
F32 = jnp.float32
BF16 = jnp.bfloat16
WINDOW = 256
BIG_ROWS = 128
SWAP = ((0, 1), (1, 0))


def nn(a, b):
    return lax.dot_general(a, b, (((1,), (0,)), ((), ())), preferred_element_type=F32)


def nt(a, b):
    return lax.dot_general(a, b, (((1,), (1,)), ((), ())), preferred_element_type=F32)


def tn(a, b):
    return lax.dot_general(a, b, (((0,), (0,)), ((), ())), preferred_element_type=F32)


def normed_of(rows_in):
    width = rows_in.shape[-1]
    mean = jnp.sum(rows_in, axis=-1, keepdims=True) * (1.0 / width)
    centered = rows_in - mean
    variance = jnp.sum(centered * centered, axis=-1, keepdims=True) * (1.0 / width)
    inverse = lax.rsqrt(variance + epsilon)
    return centered * inverse, inverse


def norm_back(grad, gain, normal, inverse):
    width = grad.shape[-1]
    g = grad * gain
    mean_g = jnp.sum(g, axis=-1, keepdims=True) * (1.0 / width)
    mean_gn = jnp.sum(g * normal, axis=-1, keepdims=True) * (1.0 / width)
    return (g - mean_g - normal * mean_gn) * inverse


def estimate(micros):
    return pl.CostEstimate(flops=int(micros * 1e9), bytes_accessed=1000, transcendentals=0)


def call(kernel, out_shape, args, micros, name, scratch=(), scalars=0):
    spec = pltpu.PrefetchScalarGridSpec(
        num_scalar_prefetch=scalars,
        grid=(),
        in_specs=[pl.BlockSpec(memory_space=pltpu.VMEM)] * (len(args) - scalars),
        out_specs=jax.tree.map(lambda s: pl.BlockSpec(memory_space=pltpu.VMEM), out_shape),
        scratch_shapes=list(scratch),
    )
    return pl.pallas_call(
        kernel,
        out_shape=out_shape,
        grid_spec=spec,
        compiler_params=pltpu.CompilerParams(vmem_limit_bytes=22 * 1024 * 1024),
        cost_estimate=estimate(micros),
        name=name,
    )(*args)


def shape(dims, kind=BF16):
    return jax.ShapeDtypeStruct(tuple(dims), kind)


def row_of(ref, k):
    return ref[k : k + 1, :].astype(F32)


def over_rows(total, body, carry=0):
    def step(i, carry):
        result = body(pl.ds(pl.multiple_of(i * WINDOW, WINDOW), WINDOW), carry)
        return carry if result is None else result

    return lax.fori_loop(0, total // WINDOW, step, carry)


def qkv_kernel(tokens_ref, mark_ref, vec_ref, w_ref, normed_ref, qkv_ref, x_ref):
    pairs = qkv_ref.shape[1]
    local = pairs * 128

    def block(rows, carry):
        x = jnp.where(mark_ref[rows, :] > 0.5, vec_ref[8:9, :], tokens_ref[rows, :])
        x_ref[rows, :] = x
        normal, inverse = normed_of(x.astype(F32))
        normed = (normal * row_of(vec_ref, 0) + row_of(vec_ref, 1)).astype(BF16)
        normed_ref[rows, :] = normed
        for c in range(3):
            part = nn(normed, w_ref[c])
            if c != 1:
                start = 0 if c == 0 else local
                part = part + vec_ref[9:10, start : start + local].astype(F32)
            part = part.astype(BF16)
            if c == 0:
                part = part * 0.125
            for p in range(pairs):
                qkv_ref[c, p, rows, :] = part[:, p * 128 : (p + 1) * 128]

    for first in range(0, x_ref.shape[0], WINDOW):
        block(pl.ds(first, WINDOW), 0)


def slot_rows(meta, slot):
    bucket = meta[32 + slot]
    rows = jnp.where(bucket == 0, B0, jnp.where(bucket == 1, B1, jnp.where(bucket == 2, B2, B3)))
    return jnp.where(meta[slot] > 0, rows, 0)


def walk_groups(meta, slots, small, big):
    def more(state):
        slot, first = state
        return jnp.logical_and(slot < slots, meta[slot] > 0)

    def step(state):
        slot, first = state
        first = pl.multiple_of(first, 16)
        rows = slot_rows(meta, slot)

        def take_big():
            big(first, meta[slot])
            return slot + 1, first + B3

        def take_small():
            starts, ends, lasts = [jnp.int32(0)], [rows], [meta[slot]]
            going, end, count = jnp.bool_(True), rows, jnp.int32(1)
            for k in range(1, 4):
                size = slot_rows(meta, slot + k)
                going = going & (slot + k < slots) & (size > 0) & (end + size <= WINDOW)
                starts.append(jnp.where(going, end, WINDOW))
                lasts.append(jnp.where(going, end + meta[slot + k], WINDOW))
                end = jnp.where(going, end + size, end)
                ends.append(jnp.where(going, end, WINDOW))
                count = jnp.where(going, count + 1, count)
            small(first, starts, ends, lasts)
            return slot + count, first + end

        return lax.cond(rows == B3, take_big, take_small)

    lax.while_loop(more, step, (jnp.int32(0), jnp.int32(0)))


def slot_ids(ids, starts, stops, outside):
    result = jnp.full(ids.shape, outside, jnp.int32)
    for k in range(4):
        result = jnp.where((ids >= starts[k]) & (ids < stops[k]), k, result)
    return result


def attention_kernel(
    slots, meta, own_ref, other_ref, heads_own_ref, heads_other_ref, qkv_ref, mixed_ref
):
    pairs = own_ref.shape[1]
    half = own_ref.shape[2]
    total = 2 * half
    first_own = pl.multiple_of(meta[64], half)
    first_other = pl.multiple_of(half - meta[64], half)
    for c in range(3):
        for p in range(pairs):
            qkv_ref[c, p, pl.ds(first_own, half), :] = own_ref[c, p]
            qkv_ref[c, p, pl.ds(first_other, half), :] = other_ref[c, p]
            qkv_ref[c, p, pl.ds(total, WINDOW), :] = jnp.zeros((WINDOW, 128), BF16)
    mixed_ref[...] = jnp.zeros(mixed_ref.shape, BF16)
    low = lax.broadcasted_iota(jnp.int32, (1, 128), 1) < HEAD_DIM
    lanes = (low, jnp.logical_not(low))

    def mix(chosen, first, count, window, mask):
        scores = []
        for p in chosen:
            q = qkv_ref[0, p, pl.ds(first, count), :]
            keys = qkv_ref[1, p, window, :]
            for h in range(2):
                scores.append(nt(jnp.where(lanes[h], q, 0), keys))
        probs = []
        for score in scores:
            score = jnp.where(mask, score, masked_score)
            exponent = jnp.exp(score - jnp.max(score, axis=1, keepdims=True))
            inverse = 1.0 / jnp.sum(exponent, axis=1, keepdims=True)
            probs.append((exponent * inverse).astype(BF16))
        for k, p in enumerate(chosen):
            values = qkv_ref[2, p, window, :]
            mixed = jnp.where(low, nn(probs[2 * k], values), nn(probs[2 * k + 1], values))
            mixed_ref[p, pl.ds(first, count), :] = mixed.astype(BF16)

    def small(first, starts, ends, lasts):
        row = slot_ids(lax.broadcasted_iota(jnp.int32, (WINDOW, 1), 0), starts, ends, 4)
        column = slot_ids(lax.broadcasted_iota(jnp.int32, (1, WINDOW), 1), starts, lasts, 5)
        mix(range(pairs), first, WINDOW, pl.ds(first, WINDOW), row == column)

    def big(first, length):
        mask = lax.broadcasted_iota(jnp.int32, (1, B3), 1) < length

        def block(b, carry):
            begin = pl.multiple_of(first + b * BIG_ROWS, 16)
            mix(range(pairs), begin, BIG_ROWS, pl.ds(first, B3), mask)
            return carry

        lax.fori_loop(0, pl.cdiv(B3, BIG_ROWS), block, 0)

    walk_groups(meta, slots, small, big)
    for p in range(pairs):
        heads_own_ref[:, p * 128 : (p + 1) * 128] = mixed_ref[p, pl.ds(first_own, half), :]
        heads_other_ref[:, p * 128 : (p + 1) * 128] = mixed_ref[p, pl.ds(first_other, half), :]


def attention_back_kernel(
    slots, meta, qkv_ref, own_0, own_1, other_0, other_1, w_ref, grad_ref, out_ref, sum_ref
):
    pairs = qkv_ref.shape[1]
    half = 2 * own_0.shape[0]
    total = 2 * half
    first_own = pl.multiple_of(meta[64], half)
    first_other = pl.multiple_of(half - meta[64], half)
    for source, first in (
        (own_0, first_own),
        (own_1, first_own + WINDOW),
        (other_0, first_other),
        (other_1, first_other + WINDOW),
    ):
        part = nt(source[...], w_ref[...]).astype(BF16)
        for p in range(pairs):
            out_ref[p, pl.ds(pl.multiple_of(first, WINDOW), WINDOW), :] = part[
                :, p * 128 : (p + 1) * 128
            ]
    for p in range(pairs):
        out_ref[p, pl.ds(total, WINDOW), :] = jnp.zeros((WINDOW, 128), BF16)
    grad_ref[...] = jnp.zeros(grad_ref.shape, BF16)
    low = lax.broadcasted_iota(jnp.int32, (1, 128), 1) < HEAD_DIM
    lanes = (low, jnp.logical_not(low))

    def back(chosen, first, count, window, mask, rows_in):
        work = []
        for p in chosen:
            q = qkv_ref[0, p, pl.ds(first, count), :]
            keys = qkv_ref[1, p, window, :]
            values = qkv_ref[2, p, window, :]
            grads = out_ref[p, pl.ds(first, count), :]
            if rows_in is not None:
                grads = jnp.where(rows_in, grads, 0)
            for h in range(2):
                q_h = jnp.where(lanes[h], q, 0)
                g_h = jnp.where(lanes[h], grads, 0)
                work.append((nt(keys, q_h), nt(values, g_h), q_h, g_h))
        pieces = []
        for scores, grad_probs, q_h, g_h in work:
            scores = jnp.where(mask, scores, masked_score)
            exponent = jnp.exp(scores - jnp.max(scores, axis=0, keepdims=True))
            probs = exponent * (1.0 / jnp.sum(exponent, axis=0, keepdims=True))
            inner = jnp.sum(probs * grad_probs, axis=0, keepdims=True)
            grad_scores = (probs * (grad_probs - inner)).astype(BF16)
            pieces.append((probs.astype(BF16), grad_scores, q_h, g_h))
        results = []
        for k, p in enumerate(chosen):
            keys = qkv_ref[1, p, window, :]
            d_query = d_key = d_value = 0.0
            for h in range(2):
                probs, grad_scores, q_h, g_h = pieces[2 * k + h]
                d_query = d_query + tn(grad_scores, jnp.where(lanes[h], keys, 0))
                d_key = d_key + nn(grad_scores, q_h)
                d_value = d_value + nn(probs, g_h)
            grad_ref[0, p, pl.ds(first, count), :] = (d_query * 0.125).astype(BF16)
            results.append((d_key, d_value))
        return results

    def small(first, starts, ends, lasts):
        key = slot_ids(lax.broadcasted_iota(jnp.int32, (WINDOW, 1), 0), starts, lasts, 5)
        query = slot_ids(lax.broadcasted_iota(jnp.int32, (1, WINDOW), 1), starts, ends, 4)
        rows_in = slot_ids(lax.broadcasted_iota(jnp.int32, (WINDOW, 1), 0), starts, ends, 4) < 4
        window = pl.ds(first, WINDOW)
        parts = back(range(pairs), first, WINDOW, window, key == query, rows_in)
        for p, (d_key, d_value) in enumerate(parts):
            grad_ref[1, p, window, :] = d_key.astype(BF16)
            grad_ref[2, p, window, :] = d_value.astype(BF16)

    def big(first, length):
        mask = lax.broadcasted_iota(jnp.int32, (B3, 1), 0) < length
        window = pl.ds(first, B3)
        sum_ref[...] = jnp.zeros(sum_ref.shape, F32)

        def block(b, carry):
            begin = pl.multiple_of(first + b * BIG_ROWS, 16)
            rows_in = lax.broadcasted_iota(jnp.int32, (BIG_ROWS, 1), 0) < B3 - b * BIG_ROWS
            for p, parts in enumerate(back(range(pairs), begin, BIG_ROWS, window, mask, rows_in)):
                for c in range(2):
                    sum_ref[c, p] += parts[c]
            return carry

        lax.fori_loop(0, pl.cdiv(B3, BIG_ROWS), block, 0)
        for p in range(pairs):
            for c in range(2):
                grad_ref[1 + c, p, window, :] = sum_ref[c, p].astype(BF16)

    walk_groups(meta, slots, small, big)


def feed_kernel(
    keep_attn,
    meta,
    mine_ref,
    theirs_ref,
    x_ref,
    gb_ref,
    vec_ref,
    wp_ref,
    wp_first_ref,
    wp_second_ref,
    w1_ref,
    w2_ref,
    normed_ref,
    act_ref,
    gpre_ref,
    grad_ref,
    *more,
):
    units = w1_ref.shape[1]
    step = x_ref.shape[1]
    sum_ref = more[-1]
    even = meta[65] == 0
    wp_theirs = jnp.concatenate(
        [
            jnp.where(even, wp_first_ref[...], wp_second_ref[...]),
            jnp.where(even, wp_second_ref[...], wp_first_ref[...]),
        ],
        axis=1,
    )

    def block(rows, carry):
        attn = nn(mine_ref[rows, :], wp_ref[...]) + nn(theirs_ref[rows, :], wp_theirs)
        attn = attn + row_of(vec_ref, 6)
        if keep_attn:
            more[0][rows, :] = attn
        hidden = x_ref[rows, :].astype(F32) + row_of(vec_ref, 4) * attn
        normal, inverse = normed_of(hidden)
        normed = (normal * row_of(vec_ref, 2) + row_of(vec_ref, 3)).astype(BF16)
        normed_ref[rows, :] = normed
        sum_ref[...] = jnp.zeros(sum_ref.shape, F32)

        def chunk(u, carry):
            cols = pl.ds(pl.multiple_of(u * step, step), step)
            shift = row_of(vec_ref, 10)
            for k in range(1, units // step):
                shift = jnp.where(u == k, row_of(vec_ref, 10 + k), shift)
            pre = nn(normed_ref[rows, :], w1_ref[:, cols]) + shift
            half_phi = 0.5 * (1.0 + lax.erf(pre * 0.7071067811865476))
            act_ref[rows, cols] = (pre * half_phi).astype(BF16)
            slope = half_phi + pre * (jnp.exp(pre * pre * -0.5) * 0.3989422804014327)
            gpre = (nt(gb_ref[rows, :], w2_ref[cols, :]) * slope).astype(BF16)
            gpre_ref[rows, cols] = gpre
            sum_ref[...] += nt(gpre, w1_ref[:, cols])
            return carry

        lax.fori_loop(0, units // step, chunk, 0)
        grad_ref[rows, :] = sum_ref[...].astype(BF16)

    over_rows(x_ref.shape[0], block)


def feed_grad_kernel(
    n_own, n_other, a_own, a_other, p_own, p_other, g_own, g_other, fc1_ref, fc2_ref, bias_ref
):
    units = a_own.shape[1]
    tile = 512

    def block(i, carry):
        cols = pl.ds(pl.multiple_of(i * tile, tile), tile)
        fc1_ref[:, cols] = (
            tn(n_own[...], p_own[:, cols]) + tn(n_other[...], p_other[:, cols])
        ).astype(BF16)
        fc2_ref[cols, :] = (
            tn(a_own[:, cols], g_own[...]) + tn(a_other[:, cols], g_other[...])
        ).astype(BF16)
        bias_ref[:, cols] = jnp.sum(p_own[:, cols].astype(F32), axis=0, keepdims=True) + jnp.sum(
            p_other[:, cols].astype(F32), axis=0, keepdims=True
        )
        return carry

    lax.fori_loop(0, units // tile, block, 0)


def feed_grads(n_own, n_other, a_own, a_other, p_own, p_other, g_own, g_other):
    units = a_own.shape[1]
    width = n_own.shape[1]
    return call(
        feed_grad_kernel,
        [shape((width, units)), shape((units, width)), shape((1, units), F32)],
        (n_own, n_other, a_own, a_other, p_own, p_other, g_own, g_other),
        8,
        "feed_grads",
    )


def branch_kernel(act_ref, w2_ref, out_ref):
    def block(rows, carry):
        out_ref[rows, :] = nn(act_ref[rows, :], w2_ref[...]).astype(out_ref.dtype)

    over_rows(act_ref.shape[0], block)


def middle_kernel(
    begin, mine_ref, got_ref, attn_ref, x_ref, gout_ref, vec_ref, hidden_ref, ga_ref, sum_ref
):
    rows = pl.ds(begin, got_ref.shape[0])
    attn = attn_ref[rows, :]
    normal, inverse = normed_of(x_ref[rows, :].astype(F32) + row_of(vec_ref, 4) * attn)
    grad = mine_ref[rows, :].astype(F32) + got_ref[...].astype(F32)
    grad_hidden = gout_ref[rows, :].astype(F32) + norm_back(grad, row_of(vec_ref, 2), normal, inverse)
    hidden_ref[...] = grad_hidden
    grad_attn = (row_of(vec_ref, 4) * grad_hidden).astype(BF16)
    ga_ref[...] = grad_attn
    sums = [
        jnp.sum(v, axis=0, keepdims=True)
        for v in (grad * normal, grad, grad_hidden * attn, grad_attn.astype(F32))
    ]
    for k in range(4):
        sum_ref[k : k + 1, :] = sums[k]


def share_kernel(meta, grad_ref, w_ref, own_ref, other_ref):
    pairs = grad_ref.shape[1]
    half = own_ref.shape[0]
    for first, target in ((half - meta[64], other_ref), (meta[64], own_ref)):

        def block(to_rows, carry):
            rows = pl.ds(pl.multiple_of(first + to_rows.start, WINDOW), WINDOW)
            total = None
            for c in range(3):
                wide = jnp.concatenate([grad_ref[c, p, rows, :] for p in range(pairs)], axis=1)
                part = nt(wide, w_ref[c])
                total = part if total is None else total + part
            target[to_rows, :] = total.astype(BF16)

        over_rows(half, block)


def weight_kernel(
    meta, grad_ref, n_own, n_other, h_own, h_other, g_0, g_1, g_2, g_3, keep_ref, give_ref, bias_ref
):
    pairs = grad_ref.shape[1]
    half = n_own.shape[0]
    local = pairs * 128
    own = pl.ds(pl.multiple_of(meta[64], half), half)
    other = pl.ds(pl.multiple_of(half - meta[64], half), half)
    grads = []
    for c in range(3):
        wide_own = jnp.concatenate([grad_ref[c, p, own, :] for p in range(pairs)], axis=1)
        wide_other = jnp.concatenate([grad_ref[c, p, other, :] for p in range(pairs)], axis=1)
        bias_ref[c : c + 1, :] = jnp.sum(wide_own.astype(F32), axis=0, keepdims=True) + jnp.sum(
            wide_other.astype(F32), axis=0, keepdims=True
        )
        grads.append((wide_own, wide_other))
    for k, out_ref in enumerate((keep_ref, give_ref)):
        half_id = meta[65] if k == 0 else 1 - meta[65]
        columns = pl.ds(pl.multiple_of(half_id * local, local), local)
        for c in range(3):
            part = tn(n_own[:, columns], grads[c][0]) + tn(n_other[:, columns], grads[c][1])
            out_ref[pl.ds(c * local, local), :] = part.astype(BF16)
        ga_own = jnp.concatenate([g_0[:, columns], g_1[:, columns]], axis=0)
        ga_other = jnp.concatenate([g_2[:, columns], g_3[:, columns]], axis=0)
        part = tn(h_own[...], ga_own) + tn(h_other[...], ga_other)
        out_ref[pl.ds(3 * local, local), :] = part.astype(BF16)


def final_kernel(
    mine_ref, got_ref, x_ref, hidden_0, hidden_1, mark_ref, vec_ref, tokens_ref, sum_ref
):
    sums = [jnp.zeros((1, x_ref.shape[1]), F32)] * 3
    for k, hidden_ref in enumerate((hidden_0, hidden_1)):
        rows = pl.ds(k * WINDOW, WINDOW)
        normal, inverse = normed_of(x_ref[rows, :].astype(F32))
        grad = mine_ref[rows, :].astype(F32) + got_ref[rows, :].astype(F32)
        grad_x = hidden_ref[...] + norm_back(grad, row_of(vec_ref, 0), normal, inverse)
        marked = mark_ref[rows, :] > 0.5
        tokens_ref[rows, :] = jnp.where(marked, 0.0, grad_x)
        parts = [
            jnp.sum(v, axis=0, keepdims=True)
            for v in (jnp.where(marked, grad_x, 0.0), grad * normal, grad)
        ]
        sums = [a + b for a, b in zip(sums, parts)]
    for k in range(3):
        sum_ref[k : k + 1, :] = sums[k]


def unpack_kernel(meta, mine_ref, across_ref, beside_ref, corner_ref, qkv_ref, proj_ref):
    local = qkv_ref.shape[2]
    pieces = ((mine_ref, 0, 0), (across_ref, 1, 0), (beside_ref, 0, 1), (corner_ref, 1, 1))
    for ref, core_flip, side_flip in pieces:
        begin = pl.ds(pl.multiple_of((meta[65] ^ core_flip) * local, local), local)
        upper = (meta[66] ^ side_flip) == 1

        @pl.when(jnp.logical_not(upper))
        def first(ref=ref, begin=begin):
            qkv_ref[0, begin, :] = ref[:local, :].astype(F32)
            qkv_ref[1, begin, :] = ref[local:, :].astype(F32)

        @pl.when(upper)
        def second(ref=ref, begin=begin):
            qkv_ref[2, begin, :] = ref[:local, :].astype(F32)
            proj_ref[:, begin] = ref[local:, :].astype(F32)


def own_validity(lengths, buckets, first_own, own_rows):
    slots = lengths.shape[0]
    rows = jnp.where(buckets == 0, B0, jnp.where(buckets == 1, B1, jnp.where(buckets == 2, B2, B3)))
    padded = jnp.where(lengths > 0, rows, 0).astype(jnp.int32)
    before = jnp.tril(jnp.ones((slots, slots), jnp.int32), -1)
    starts = jnp.sum(before * padded[None, :], axis=1)
    ids = first_own + lax.broadcasted_iota(jnp.int32, (own_rows, slots), 0)
    inside = (ids >= starts[None, :]) & (ids < (starts + lengths)[None, :])
    return jnp.any(inside, axis=1, keepdims=True)


def chip_bits():
    return list(range(1, lax.axis_size("wide").bit_length() - 1))


def hop(value, flip):
    size = lax.axis_size("wide")
    return lax.ppermute(value, "wide", tuple((i, i ^ flip) for i in range(size)))


def bits_at(shift, count=1):
    return ((lax.axis_index("wide") >> shift) % (1 << count)).astype(jnp.int32)


def fold_kernel(parts, place, meta, mine_ref, got_ref, *out_refs):
    rows = out_refs[0].shape[0]
    for flip, out_ref in enumerate(out_refs):
        start = pl.multiple_of((meta[place] ^ flip) * rows, rows)
        total = mine_ref[pl.ds(start, rows), :].astype(F32) + got_ref[pl.ds(start, rows), :].astype(F32)
        out_ref[...] = total.astype(BF16)


def fold(meta, mine, got, parts, place, index):
    rows = mine.shape[0] // parts
    if rows % 32:
        total = (mine.astype(F32) + got.astype(F32)).astype(BF16)
        return [
            lax.dynamic_slice_in_dim(total, (index ^ flip) * rows, rows) for flip in range(parts)
        ]
    return call(
        partial(fold_kernel, parts, place),
        [shape((rows, mine.shape[1]))] * parts,
        (meta, mine, got),
        1,
        "fold",
        scalars=1,
    )


def gather_kernel(place, meta, *refs):
    out_ref = refs[-1]
    rows = refs[0].shape[0]
    for flip, ref in enumerate(refs[:-1]):
        start = pl.multiple_of((meta[place] ^ flip) * rows, rows)
        out_ref[pl.ds(start, rows), :] = ref[...]


def gather(meta, pieces, place, index):
    rows, columns = pieces[0].shape
    if rows % 32:
        total = jnp.zeros((rows * len(pieces), columns), pieces[0].dtype)
        for flip, piece in enumerate(pieces):
            total = lax.dynamic_update_slice_in_dim(total, piece, (index ^ flip) * rows, 0)
        return total
    return call(
        partial(gather_kernel, place),
        shape((rows * len(pieces), columns)),
        (meta, *pieces),
        1,
        "gather",
        scalars=1,
    )


def column_half(w_proj):
    columns = w_proj.shape[1] // 2
    core = lax.axis_index("wide") % 2
    return lax.ppermute(
        lax.dynamic_slice_in_dim(w_proj, core * columns, columns, 1), "narrow", SWAP
    )


def shards(
    tokens,
    token_marks,
    crop_lengths,
    bucket_ids,
    mask_token,
    norm1_gain,
    norm1_bias,
    w_qkv,
    qv_bias,
    w_proj,
    proj_bias,
    scale_attn,
    norm2_gain,
    norm2_bias,
    w_fc1,
    fc1_bias,
    w_fc2,
    fc2_bias,
    scale_mlp,
    cotangent,
):
    half, width = tokens.shape
    slots = crop_lengths.shape[0]
    local = w_qkv.shape[2]
    pairs = local // 128
    units = w_fc1.shape[1]
    first_own = (lax.axis_index("narrow") * half).astype(jnp.int32)
    swap = lambda v: lax.ppermute(v, "narrow", SWAP)
    singles = chip_bits()

    tokens_other = swap(tokens)
    marks_other = swap(token_marks)
    valid = own_validity(crop_lengths, bucket_ids, first_own, half)
    scale2 = scale_mlp.astype(F32)
    gout_own = jnp.where(valid, cotangent, 0).astype(BF16)
    gb_own = (scale2 * gout_own.astype(F32)).astype(BF16)
    pad = jnp.zeros((32 - slots,), jnp.int32)
    meta = jnp.concatenate(
        [
            crop_lengths,
            pad,
            bucket_ids,
            pad,
            jnp.stack(
                [first_own, bits_at(0)] + [bits_at(bit) for bit in singles]
            ),
        ]
    )
    table = [
        norm1_gain,
        norm1_bias,
        norm2_gain,
        norm2_bias,
        scale_attn,
        scale_mlp,
        proj_bias,
        fc2_bias,
        mask_token,
        qv_bias.reshape(width),
    ] + [fc1_bias[k * width : (k + 1) * width] for k in range(units // width)]
    lines = lax.broadcasted_iota(jnp.int32, (len(table), width), 0)
    vec = jnp.zeros((len(table), width), BF16)
    for k, line in enumerate(table):
        vec = jnp.where(lines == k, line[None, :], vec)

    def qkv(rows, marks):
        return call(
            qkv_kernel,
            [shape((half, width)), shape((3, pairs, half, 128)), shape((half, width))],
            (rows, marks, vec, w_qkv),
            2,
            "norm_qkv",
        )

    mark_column = (token_marks == 1).astype(F32)[:, None]
    n_own, qkv_own, x_own = qkv(tokens, mark_column)
    n_own, gb_start, wp_start = lax.optimization_barrier((n_own, gb_own, w_proj))
    gb_other = swap(gb_start)
    wp_mine = column_half(wp_start)
    n_other, qkv_other, x_other = qkv(tokens_other, (marks_other == 1).astype(F32)[:, None])
    heads_own, heads_other, qkv_all = call(
        partial(attention_kernel, slots),
        [shape((half, local)), shape((half, local)), shape((3, pairs, 2 * half + WINDOW, 128))],
        (meta, qkv_own, qkv_other),
        8,
        "attention",
        scratch=[pltpu.VMEM((pairs, 2 * half + WINDOW, 128), BF16)],
        scalars=1,
    )
    heads_own, heads_other, gb_other, wp_mine = lax.optimization_barrier(
        (heads_own, heads_other, gb_other, wp_mine)
    )
    got_other = swap(heads_own)
    got_own = swap(heads_other)
    wp_next = hop(wp_mine, 1)

    def feed(mine, theirs, x, gb, keep):
        outs = [shape((half, width)), shape((half, units)), shape((half, units)), shape((half, width))]
        if keep:
            outs.append(shape((half, width), F32))
        return call(
            partial(feed_kernel, keep),
            outs,
            (meta, mine, theirs, x, gb, vec, w_proj, wp_mine, wp_next, w_fc1, w_fc2),
            7,
            "feed",
            scratch=[pltpu.VMEM((WINDOW, width), F32)],
            scalars=1,
        )

    n2_other, act_other, gpre_other, gn2_other = feed(
        heads_other, got_other, x_other, gb_other, False
    )
    gn2_got = [swap(gn2_other[:WINDOW]), swap(gn2_other[WINDOW:])]
    n2_own, act_own, gpre_own, gn2_own, attn_own = feed(
        heads_own, got_own, x_own, gb_own, True
    )
    def middle(k, *arrays):
        return call(
            partial(middle_kernel, k * WINDOW),
            [shape((WINDOW, width), F32), shape((WINDOW, width)), shape((4, width), F32)],
            (*arrays, vec),
            2,
            "middle",
        )

    hidden_0, ga_own_0, sums_0 = middle(0, gn2_own, gn2_got[0], attn_own, x_own, gout_own)
    ga_other_0 = swap(ga_own_0)
    act_own, ga_own_0 = lax.optimization_barrier((act_own, ga_own_0))
    g_fc1, g_fc2, g_fc1b = feed_grads(
        n2_own, n2_other, act_own, act_other, gpre_own, gpre_other, gb_own, gb_other
    )

    gn2_got_1, g_fc1, g_fc2, ga_other_0 = lax.optimization_barrier(
        (gn2_got[1], g_fc1, g_fc2, ga_other_0)
    )
    sum_fc1, sum_fc2 = lax.psum((g_fc1, g_fc2), "wide")

    operands = (
        gn2_own, gn2_got_1, attn_own, x_own, gout_own, gb_own, act_own, act_other, qkv_all, n_own, n_other,
        heads_own, heads_other, g_fc1b, hidden_0, ga_own_0, ga_other_0, sums_0
    )

    def rest(operands):
        (
            gn2_own, gn2_got_1, attn_own, x_own, gout_own, gb_own, act_own, act_other, qkv_all, n_own, n_other, heads_own, heads_other, g_fc1b, hidden_0, ga_own_0, ga_other_0, sums_0
        ) = operands
        hidden_1, ga_own_1, sums_1 = middle(1, gn2_own, gn2_got_1, attn_own, x_own, gout_own)
        ga_other_1 = swap(ga_own_1)
        sums2 = sums_0 + sums_1
        def branch_of(act, kind):
            return call(
                branch_kernel, shape((half, width), kind), (act, w_fc2), 2, "branch"
            )

        branch_got = swap(branch_of(act_other, BF16))
        branch_own = branch_of(act_own, F32)
        ga_other_1, branch_own = lax.optimization_barrier((ga_other_1, branch_own))
        ga = (ga_own_0, ga_own_1, ga_other_0, ga_other_1)
        d_qkv = call(
            partial(attention_back_kernel, slots),
            shape((3, pairs, 2 * half + WINDOW, 128)),
            (meta, qkv_all, *ga, w_proj),
            9,
            "attention_back",
            scratch=[
                pltpu.VMEM((pairs, 2 * half + WINDOW, 128), BF16),
                pltpu.VMEM((2, pairs, B3, 128), F32),
            ],
            scalars=1,
        )
        d_qkv, branch_got = lax.optimization_barrier((d_qkv, branch_got))
        keep, give, d_bias = call(
            weight_kernel,
            [shape((2 * width, local)), shape((2 * width, local)), shape((3, local), F32)],
            (meta, d_qkv, n_own, n_other, heads_own, heads_other, *ga),
            4,
            "weights",
            scalars=1,
        )
        d_qkv, keep, give = lax.optimization_barrier((d_qkv, keep, give))
        got = hop(give, 1)
        gn1_own, gn1_other = call(
            share_kernel,
            [shape((half, width)), shape((half, width))],
            (meta, d_qkv, w_qkv),
            3,
            "share",
            scalars=1,
        )
        gn1_got = swap(gn1_other)
        got, gn1_own = lax.optimization_barrier((got, gn1_own))
        branch = branch_own + branch_got.astype(F32) + fc2_bias.astype(F32)
        hidden = x_own.astype(F32) + scale_attn.astype(F32) * attn_own
        output = jnp.where(valid, hidden + scale2 * branch, 0.0).astype(BF16)
        g_smlp = jnp.sum(gout_own.astype(F32) * branch, axis=0)
        g_fc2b = jnp.sum(gb_own.astype(F32), axis=0)
        for k, bit in enumerate(singles):
            keep, give = fold(meta, keep, got, 2, 66 + k, bits_at(bit))
            got = hop(give, 1 << bit)
            if k == 0:
                got, output, g_smlp, g_fc2b = lax.optimization_barrier((got, output, g_smlp, g_fc2b))
        keep, gn1_got = lax.optimization_barrier((keep, gn1_got))
        grad_tokens, sums1 = call(
            final_kernel,
            [shape((half, width), F32), shape((3, width), F32)],
            (gn1_own, gn1_got, x_own, hidden_0, hidden_1, mark_column, vec),
            3,
            "final",
        )
        got, grad_tokens = lax.optimization_barrier((got, grad_tokens))
        part = (keep.astype(F32) + got.astype(F32)).astype(BF16)
        wide_only = jnp.concatenate([d_bias[0], d_bias[2], g_fc1b[0]]).reshape(-1, width)
        small = jnp.concatenate([sums1, sums2, g_fc2b[None], g_smlp[None], wide_only], axis=0)
        for k in range(len(singles) - 1, 0, -1):
            part, small = lax.optimization_barrier((part, small))
            pieces = [part, hop(part, 1 << singles[k])]
            small = small + hop(small, 1 << singles[k])
            part = gather(meta, pieces, 66 + k, bits_at(singles[k]))
        return output, grad_tokens, part, small

    def none(operands):
        return jax.tree.map(lambda v: jnp.zeros(v.shape, v.dtype), jax.eval_shape(rest, operands))

    output, grad_tokens, part, small = lax.cond(
        jnp.max(crop_lengths) < 65536, rest, none, operands
    )
    beside = hop(part, 1 << singles[0])
    small = small + hop(small, 1 << singles[0])
    across = hop(part, 1)
    beside, across, small = lax.optimization_barrier((beside, across, small))
    corner = hop(beside, 1)
    small = small + hop(small, 1)
    corner, small, sum_fc1, sum_fc2 = lax.optimization_barrier(
        (corner, small, sum_fc1.astype(F32), sum_fc2.astype(F32))
    )
    count = 9
    rows = small[:count] + swap(small[:count])
    flat = small[count:].reshape(-1)
    g_qvb = flat[: 2 * local].reshape(2, local)
    g_fc1b = flat[2 * local :]
    g_qkv, g_proj = call(
        unpack_kernel,
        [shape((3, width, local), F32), shape((local, width), F32)],
        (meta, part, across, beside, corner),
        3,
        "unpack",
        scalars=1,
    )
    return (
        output,
        grad_tokens,
        rows[0],
        rows[1],
        rows[2],
        g_qkv,
        g_qvb,
        g_proj,
        rows[6],
        rows[5],
        rows[3],
        rows[4],
        sum_fc1,
        g_fc1b,
        sum_fc2,
        rows[7],
        rows[8],
    )


def solution(mesh):
    rows = P(("wide", "narrow"), None)
    return jax.shard_map(
        shards,
        mesh=mesh,
        in_specs=(
            rows,
            P(("wide", "narrow")),
            P("wide"),
            P("wide"),
            P(),
            P(),
            P(),
            P(None, None, "narrow"),
            P(None, "narrow"),
            P("narrow", None),
            P(),
            P(),
            P(),
            P(),
            P(None, "narrow"),
            P("narrow"),
            P("narrow", None),
            P(),
            P(),
            rows,
        ),
        out_specs=(
            rows,
            rows,
            P(),
            P(),
            P(),
            P(None, None, "narrow"),
            P(None, "narrow"),
            P("narrow", None),
            P(),
            P(),
            P(),
            P(),
            P(None, "narrow"),
            P("narrow"),
            P("narrow", None),
            P(),
            P(),
        ),
        check_vma=False,
    )
```

```python
from functools import partial

import jax
import jax.numpy as jnp
from jax import lax
from jax.experimental import pallas as pl
from jax.experimental.pallas import tpu as pltpu
from jax.sharding import PartitionSpec as P

HEAD_DIM = 64
B0 = 64
B1 = 144
B2 = 256
B3 = 576

epsilon = 1e-06
masked_score = -1e30
F32 = jnp.float32
BF16 = jnp.bfloat16
WINDOW = 256
BIG_ROWS = 128
SWAP = ((0, 1), (1, 0))


def nn(a, b):
    return lax.dot_general(a, b, (((1,), (0,)), ((), ())), preferred_element_type=F32)


def nt(a, b):
    return lax.dot_general(a, b, (((1,), (1,)), ((), ())), preferred_element_type=F32)


def tn(a, b):
    return lax.dot_general(a, b, (((0,), (0,)), ((), ())), preferred_element_type=F32)


def normed_of(rows_in):
    width = rows_in.shape[-1]
    mean = jnp.sum(rows_in, axis=-1, keepdims=True) * (1.0 / width)
    centered = rows_in - mean
    variance = jnp.sum(centered * centered, axis=-1, keepdims=True) * (1.0 / width)
    inverse = lax.rsqrt(variance + epsilon)
    return centered * inverse, inverse


def norm_back(grad, gain, normal, inverse):
    width = grad.shape[-1]
    g = grad * gain
    mean_g = jnp.sum(g, axis=-1, keepdims=True) * (1.0 / width)
    mean_gn = jnp.sum(g * normal, axis=-1, keepdims=True) * (1.0 / width)
    return (g - mean_g - normal * mean_gn) * inverse


def estimate(micros):
    return pl.CostEstimate(flops=int(micros * 1e9), bytes_accessed=1000, transcendentals=0)


def call(kernel, out_shape, args, micros, name, scratch=(), scalars=0):
    spec = pltpu.PrefetchScalarGridSpec(
        num_scalar_prefetch=scalars,
        grid=(),
        in_specs=[pl.BlockSpec(memory_space=pltpu.VMEM)] * (len(args) - scalars),
        out_specs=jax.tree.map(lambda s: pl.BlockSpec(memory_space=pltpu.VMEM), out_shape),
        scratch_shapes=list(scratch),
    )
    return pl.pallas_call(
        kernel,
        out_shape=out_shape,
        grid_spec=spec,
        compiler_params=pltpu.CompilerParams(vmem_limit_bytes=22 * 1024 * 1024),
        cost_estimate=estimate(micros),
        name=name,
    )(*args)


def shape(dims, kind=BF16):
    return jax.ShapeDtypeStruct(tuple(dims), kind)


def row_of(ref, k):
    return ref[k : k + 1, :].astype(F32)


def over_rows(total, body, carry=0):
    def step(i, carry):
        result = body(pl.ds(pl.multiple_of(i * WINDOW, WINDOW), WINDOW), carry)
        return carry if result is None else result

    return lax.fori_loop(0, total // WINDOW, step, carry)


def project_rows(tokens_ref, mark_ref, vec_ref, w_ref, normed_ref, x_ref, store):
    local = w_ref.shape[2]
    count = x_ref.shape[0]
    for first in range(0, count, count):
        rows = pl.ds(first, count)
        x = jnp.where(mark_ref[rows, :] > 0.5, vec_ref[8:9, :], tokens_ref[rows, :])
        x_ref[rows, :] = x
        normal, inverse = normed_of(x.astype(F32))
        normed = (normal * row_of(vec_ref, 0) + row_of(vec_ref, 1)).astype(BF16)
        normed_ref[rows, :] = normed
        for c in range(3):
            part = nn(normed, w_ref[c])
            if c != 1:
                start = 0 if c == 0 else local
                part = part + vec_ref[9:10, start : start + local].astype(F32)
            part = part.astype(BF16)
            if c == 0:
                part = part * 0.125
            for p in range(local // 128):
                store(c, p, first, part[:, p * 128 : (p + 1) * 128])


def qkv_kernel(tokens_ref, mark_ref, vec_ref, w_ref, normed_ref, qkv_ref, x_ref):
    def store(c, p, first, value):
        qkv_ref[c, p, pl.ds(first, value.shape[0]), :] = value

    project_rows(tokens_ref, mark_ref, vec_ref, w_ref, normed_ref, x_ref, store)


def slot_rows(meta, slot):
    bucket = meta[32 + slot]
    rows = jnp.where(bucket == 0, B0, jnp.where(bucket == 1, B1, jnp.where(bucket == 2, B2, B3)))
    return jnp.where(meta[slot] > 0, rows, 0)


def walk_groups(meta, slots, small, big):
    def more(state):
        slot, first = state
        return jnp.logical_and(slot < slots, meta[slot] > 0)

    def step(state):
        slot, first = state
        first = pl.multiple_of(first, 16)
        rows = slot_rows(meta, slot)

        def take_big():
            big(first, meta[slot])
            return slot + 1, first + B3

        def take_small():
            starts, ends, lasts = [jnp.int32(0)], [rows], [meta[slot]]
            going, end, count = jnp.bool_(True), rows, jnp.int32(1)
            for k in range(1, 4):
                size = slot_rows(meta, slot + k)
                going = going & (slot + k < slots) & (size > 0) & (end + size <= WINDOW)
                starts.append(jnp.where(going, end, WINDOW))
                lasts.append(jnp.where(going, end + meta[slot + k], WINDOW))
                end = jnp.where(going, end + size, end)
                ends.append(jnp.where(going, end, WINDOW))
                count = jnp.where(going, count + 1, count)
            small(first, starts, ends, lasts)
            return slot + count, first + end

        return lax.cond(rows == B3, take_big, take_small)

    lax.while_loop(more, step, (jnp.int32(0), jnp.int32(0)))


def slot_ids(ids, starts, stops, outside):
    result = jnp.full(ids.shape, outside, jnp.int32)
    for k in range(4):
        result = jnp.where((ids >= starts[k]) & (ids < stops[k]), k, result)
    return result


def attention_kernel(
    slots,
    meta,
    own_ref,
    tokens_ref,
    mark_ref,
    vec_ref,
    w_ref,
    heads_own_ref,
    heads_other_ref,
    qkv_ref,
    normed_ref,
    x_ref,
    mixed_ref,
):
    pairs = own_ref.shape[1]
    half = own_ref.shape[2]
    total = 2 * half
    first_own = pl.multiple_of(meta[64], half)
    first_other = pl.multiple_of(half - meta[64], half)

    def store(c, p, first, value):
        begin = pl.multiple_of(first_other + first, WINDOW)
        qkv_ref[c, p, pl.ds(begin, value.shape[0]), :] = value

    project_rows(tokens_ref, mark_ref, vec_ref, w_ref, normed_ref, x_ref, store)
    for c in range(3):
        for p in range(pairs):
            qkv_ref[c, p, pl.ds(first_own, half), :] = own_ref[c, p]
            qkv_ref[c, p, pl.ds(total, WINDOW), :] = jnp.zeros((WINDOW, 128), BF16)
    mixed_ref[...] = jnp.zeros(mixed_ref.shape, BF16)
    low = lax.broadcasted_iota(jnp.int32, (1, 128), 1) < HEAD_DIM
    lanes = (low, jnp.logical_not(low))

    def mix(chosen, first, count, window, mask):
        scores = []
        for p in chosen:
            q = qkv_ref[0, p, pl.ds(first, count), :]
            keys = qkv_ref[1, p, window, :]
            for h in range(2):
                scores.append(nt(jnp.where(lanes[h], q, 0), keys))
        probs = []
        for score in scores:
            score = jnp.where(mask, score, masked_score)
            exponent = jnp.exp(score - jnp.max(score, axis=1, keepdims=True))
            inverse = 1.0 / jnp.sum(exponent, axis=1, keepdims=True)
            probs.append((exponent * inverse).astype(BF16))
        for k, p in enumerate(chosen):
            values = qkv_ref[2, p, window, :]
            mixed = jnp.where(low, nn(probs[2 * k], values), nn(probs[2 * k + 1], values))
            mixed_ref[p, pl.ds(first, count), :] = mixed.astype(BF16)

    def small(first, starts, ends, lasts):
        row = slot_ids(lax.broadcasted_iota(jnp.int32, (WINDOW, 1), 0), starts, ends, 4)
        column = slot_ids(lax.broadcasted_iota(jnp.int32, (1, WINDOW), 1), starts, lasts, 5)
        mix(range(pairs), first, WINDOW, pl.ds(first, WINDOW), row == column)

    def big(first, length):
        mask = lax.broadcasted_iota(jnp.int32, (1, B3), 1) < length

        def block(b, carry):
            begin = pl.multiple_of(first + b * BIG_ROWS, 16)
            mix(range(pairs), begin, BIG_ROWS, pl.ds(first, B3), mask)
            return carry

        lax.fori_loop(0, pl.cdiv(B3, BIG_ROWS), block, 0)

    walk_groups(meta, slots, small, big)
    for p in range(pairs):
        heads_own_ref[:, p * 128 : (p + 1) * 128] = mixed_ref[p, pl.ds(first_own, half), :]
        heads_other_ref[:, p * 128 : (p + 1) * 128] = mixed_ref[p, pl.ds(first_other, half), :]


def attention_back_kernel(
    slots, meta, qkv_ref, own_0, own_1, other_0, other_1, w_ref, grad_ref, out_ref, sum_ref
):
    pairs = qkv_ref.shape[1]
    half = 2 * own_0.shape[0]
    total = 2 * half
    first_own = pl.multiple_of(meta[64], half)
    first_other = pl.multiple_of(half - meta[64], half)
    for source, first in (
        (own_0, first_own),
        (own_1, first_own + WINDOW),
        (other_0, first_other),
        (other_1, first_other + WINDOW),
    ):
        part = nt(source[...], w_ref[...]).astype(BF16)
        for p in range(pairs):
            out_ref[p, pl.ds(pl.multiple_of(first, WINDOW), WINDOW), :] = part[
                :, p * 128 : (p + 1) * 128
            ]
    for p in range(pairs):
        out_ref[p, pl.ds(total, WINDOW), :] = jnp.zeros((WINDOW, 128), BF16)
    grad_ref[...] = jnp.zeros(grad_ref.shape, BF16)
    low = lax.broadcasted_iota(jnp.int32, (1, 128), 1) < HEAD_DIM
    lanes = (low, jnp.logical_not(low))

    def back(chosen, first, count, window, mask, rows_in):
        work = []
        for p in chosen:
            q = qkv_ref[0, p, pl.ds(first, count), :]
            keys = qkv_ref[1, p, window, :]
            values = qkv_ref[2, p, window, :]
            grads = out_ref[p, pl.ds(first, count), :]
            if rows_in is not None:
                grads = jnp.where(rows_in, grads, 0)
            for h in range(2):
                q_h = jnp.where(lanes[h], q, 0)
                g_h = jnp.where(lanes[h], grads, 0)
                work.append((nt(keys, q_h), nt(values, g_h), q_h, g_h))
        pieces = []
        for scores, grad_probs, q_h, g_h in work:
            scores = jnp.where(mask, scores, masked_score)
            exponent = jnp.exp(scores - jnp.max(scores, axis=0, keepdims=True))
            probs = exponent * (1.0 / jnp.sum(exponent, axis=0, keepdims=True))
            inner = jnp.sum(probs * grad_probs, axis=0, keepdims=True)
            grad_scores = (probs * (grad_probs - inner)).astype(BF16)
            pieces.append((probs.astype(BF16), grad_scores, q_h, g_h))
        results = []
        for k, p in enumerate(chosen):
            keys = qkv_ref[1, p, window, :]
            d_query = d_key = d_value = 0.0
            for h in range(2):
                probs, grad_scores, q_h, g_h = pieces[2 * k + h]
                d_query = d_query + tn(grad_scores, jnp.where(lanes[h], keys, 0))
                d_key = d_key + nn(grad_scores, q_h)
                d_value = d_value + nn(probs, g_h)
            grad_ref[0, p, pl.ds(first, count), :] = (d_query * 0.125).astype(BF16)
            results.append((d_key, d_value))
        return results

    def small(first, starts, ends, lasts):
        key = slot_ids(lax.broadcasted_iota(jnp.int32, (WINDOW, 1), 0), starts, lasts, 5)
        query = slot_ids(lax.broadcasted_iota(jnp.int32, (1, WINDOW), 1), starts, ends, 4)
        rows_in = slot_ids(lax.broadcasted_iota(jnp.int32, (WINDOW, 1), 0), starts, ends, 4) < 4
        window = pl.ds(first, WINDOW)
        parts = back(range(pairs), first, WINDOW, window, key == query, rows_in)
        for p, (d_key, d_value) in enumerate(parts):
            grad_ref[1, p, window, :] = d_key.astype(BF16)
            grad_ref[2, p, window, :] = d_value.astype(BF16)

    def big(first, length):
        mask = lax.broadcasted_iota(jnp.int32, (B3, 1), 0) < length
        window = pl.ds(first, B3)
        sum_ref[...] = jnp.zeros(sum_ref.shape, F32)

        def block(b, carry):
            begin = pl.multiple_of(first + b * BIG_ROWS, 16)
            rows_in = lax.broadcasted_iota(jnp.int32, (BIG_ROWS, 1), 0) < B3 - b * BIG_ROWS
            for p, parts in enumerate(back(range(pairs), begin, BIG_ROWS, window, mask, rows_in)):
                for c in range(2):
                    sum_ref[c, p] += parts[c]
            return carry

        lax.fori_loop(0, pl.cdiv(B3, BIG_ROWS), block, 0)
        for p in range(pairs):
            for c in range(2):
                grad_ref[1 + c, p, window, :] = sum_ref[c, p].astype(BF16)

    walk_groups(meta, slots, small, big)


def feed_kernel(
    keep_attn,
    meta,
    mine_ref,
    theirs_ref,
    x_ref,
    gb_ref,
    vec_ref,
    wp_ref,
    wp_first_ref,
    wp_second_ref,
    w1_ref,
    w2_ref,
    normed_ref,
    act_ref,
    gpre_ref,
    grad_ref,
    *more,
):
    units = w1_ref.shape[1]
    step = x_ref.shape[1]
    sum_ref = more[-1]
    even = meta[65] == 0
    wp_theirs = jnp.concatenate(
        [
            jnp.where(even, wp_first_ref[...], wp_second_ref[...]),
            jnp.where(even, wp_second_ref[...], wp_first_ref[...]),
        ],
        axis=1,
    )

    def block(rows, carry):
        attn = nn(mine_ref[rows, :], wp_ref[...]) + nn(theirs_ref[rows, :], wp_theirs)
        attn = attn + row_of(vec_ref, 6)
        if keep_attn:
            more[0][rows, :] = attn
        hidden = x_ref[rows, :].astype(F32) + row_of(vec_ref, 4) * attn
        normal, inverse = normed_of(hidden)
        normed = (normal * row_of(vec_ref, 2) + row_of(vec_ref, 3)).astype(BF16)
        normed_ref[rows, :] = normed
        sum_ref[...] = jnp.zeros(sum_ref.shape, F32)

        def chunk(u, carry):
            cols = pl.ds(pl.multiple_of(u * step, step), step)
            shift = row_of(vec_ref, 10)
            for k in range(1, units // step):
                shift = jnp.where(u == k, row_of(vec_ref, 10 + k), shift)
            pre = nn(normed_ref[rows, :], w1_ref[:, cols]) + shift
            half_phi = 0.5 * (1.0 + lax.erf(pre * 0.7071067811865476))
            act_ref[rows, cols] = (pre * half_phi).astype(BF16)
            slope = half_phi + pre * (jnp.exp(pre * pre * -0.5) * 0.3989422804014327)
            gpre = (nt(gb_ref[rows, :], w2_ref[cols, :]) * slope).astype(BF16)
            gpre_ref[rows, cols] = gpre
            sum_ref[...] += nt(gpre, w1_ref[:, cols])
            return carry

        lax.fori_loop(0, units // step, chunk, 0)
        grad_ref[rows, :] = sum_ref[...].astype(BF16)

    block(pl.ds(0, x_ref.shape[0]), 0)


def feed_grad_kernel(
    n_own, n_other, a_own, a_other, p_own, p_other, g_own, g_other, fc1_ref, fc2_ref, bias_ref
):
    units = a_own.shape[1]
    tile = 512

    def block(i, carry):
        cols = pl.ds(pl.multiple_of(i * tile, tile), tile)
        fc1_ref[:, cols] = (
            tn(n_own[...], p_own[:, cols]) + tn(n_other[...], p_other[:, cols])
        ).astype(BF16)
        fc2_ref[cols, :] = (
            tn(a_own[:, cols], g_own[...]) + tn(a_other[:, cols], g_other[...])
        ).astype(BF16)
        bias_ref[:, cols] = jnp.sum(p_own[:, cols].astype(F32), axis=0, keepdims=True) + jnp.sum(
            p_other[:, cols].astype(F32), axis=0, keepdims=True
        )
        return carry

    lax.fori_loop(0, units // tile, block, 0)


def feed_grads(n_own, n_other, a_own, a_other, p_own, p_other, g_own, g_other):
    units = a_own.shape[1]
    width = n_own.shape[1]
    return call(
        feed_grad_kernel,
        [shape((width, units)), shape((units, width)), shape((1, units), F32)],
        (n_own, n_other, a_own, a_other, p_own, p_other, g_own, g_other),
        8,
        "feed_grads",
    )


def branch_kernel(act_ref, w2_ref, out_ref):
    def block(rows, carry):
        out_ref[rows, :] = nn(act_ref[rows, :], w2_ref[...]).astype(out_ref.dtype)

    over_rows(act_ref.shape[0], block)


def middle_kernel(
    begin, mine_ref, got_ref, attn_ref, x_ref, gout_ref, vec_ref, hidden_ref, ga_ref, sum_ref
):
    rows = pl.ds(begin, got_ref.shape[0])
    attn = attn_ref[rows, :]
    normal, inverse = normed_of(x_ref[rows, :].astype(F32) + row_of(vec_ref, 4) * attn)
    grad = mine_ref[rows, :].astype(F32) + got_ref[...].astype(F32)
    grad_hidden = gout_ref[rows, :].astype(F32) + norm_back(grad, row_of(vec_ref, 2), normal, inverse)
    hidden_ref[...] = grad_hidden
    grad_attn = (row_of(vec_ref, 4) * grad_hidden).astype(BF16)
    ga_ref[...] = grad_attn
    sums = [
        jnp.sum(v, axis=0, keepdims=True)
        for v in (grad * normal, grad, grad_hidden * attn, grad_attn.astype(F32))
    ]
    for k in range(4):
        sum_ref[k : k + 1, :] = sums[k]


def share_kernel(meta, grad_ref, w_ref, own_ref, other_ref):
    pairs = grad_ref.shape[1]
    half = own_ref.shape[0]
    for first, target in ((half - meta[64], other_ref), (meta[64], own_ref)):

        def block(to_rows, carry):
            rows = pl.ds(pl.multiple_of(first + to_rows.start, WINDOW), WINDOW)
            total = None
            for c in range(3):
                wide = jnp.concatenate([grad_ref[c, p, rows, :] for p in range(pairs)], axis=1)
                part = nt(wide, w_ref[c])
                total = part if total is None else total + part
            target[to_rows, :] = total.astype(BF16)

        over_rows(half, block)


def weight_kernel(
    meta, grad_ref, n_own, n_other, h_own, h_other, g_0, g_1, g_2, g_3, keep_ref, give_ref, bias_ref
):
    pairs = grad_ref.shape[1]
    half = n_own.shape[0]
    local = pairs * 128
    own = pl.ds(pl.multiple_of(meta[64], half), half)
    other = pl.ds(pl.multiple_of(half - meta[64], half), half)
    grads = []
    for c in range(3):
        wide_own = jnp.concatenate([grad_ref[c, p, own, :] for p in range(pairs)], axis=1)
        wide_other = jnp.concatenate([grad_ref[c, p, other, :] for p in range(pairs)], axis=1)
        bias_ref[c : c + 1, :] = jnp.sum(wide_own.astype(F32), axis=0, keepdims=True) + jnp.sum(
            wide_other.astype(F32), axis=0, keepdims=True
        )
        grads.append((wide_own, wide_other))
    for k, out_ref in enumerate((keep_ref, give_ref)):
        half_id = meta[65] if k == 0 else 1 - meta[65]
        columns = pl.ds(pl.multiple_of(half_id * local, local), local)
        for c in range(3):
            part = tn(n_own[:, columns], grads[c][0]) + tn(n_other[:, columns], grads[c][1])
            out_ref[pl.ds(c * local, local), :] = part.astype(BF16)
        ga_own = jnp.concatenate([g_0[:, columns], g_1[:, columns]], axis=0)
        ga_other = jnp.concatenate([g_2[:, columns], g_3[:, columns]], axis=0)
        part = tn(h_own[...], ga_own) + tn(h_other[...], ga_other)
        out_ref[pl.ds(3 * local, local), :] = part.astype(BF16)


def final_kernel(
    mine_ref, got_ref, x_ref, hidden_0, hidden_1, mark_ref, vec_ref, tokens_ref, sum_ref
):
    sums = [jnp.zeros((1, x_ref.shape[1]), F32)] * 3
    for k, hidden_ref in enumerate((hidden_0, hidden_1)):
        rows = pl.ds(k * WINDOW, WINDOW)
        normal, inverse = normed_of(x_ref[rows, :].astype(F32))
        grad = mine_ref[rows, :].astype(F32) + got_ref[rows, :].astype(F32)
        grad_x = hidden_ref[...] + norm_back(grad, row_of(vec_ref, 0), normal, inverse)
        marked = mark_ref[rows, :] > 0.5
        tokens_ref[rows, :] = jnp.where(marked, 0.0, grad_x)
        parts = [
            jnp.sum(v, axis=0, keepdims=True)
            for v in (jnp.where(marked, grad_x, 0.0), grad * normal, grad)
        ]
        sums = [a + b for a, b in zip(sums, parts)]
    for k in range(3):
        sum_ref[k : k + 1, :] = sums[k]


def unpack_kernel(meta, *refs):
    qkv_ref, proj_ref = refs[-2:]
    local = qkv_ref.shape[2]
    for k, ref in enumerate(refs[:-2]):
        begin = pl.ds(pl.multiple_of((meta[65] ^ (k % 2)) * local, local), local)
        block = (meta[66] ^ (k // 2 % 2)) * 2 + (meta[67] ^ (k // 4))

        @pl.when(block < 3)
        def first(ref=ref, begin=begin, block=block):
            qkv_ref[block, begin, :] = ref[...].astype(F32)

        @pl.when(block == 3)
        def second(ref=ref, begin=begin):
            proj_ref[:, begin] = ref[...].astype(F32)


def own_validity(lengths, buckets, first_own, own_rows):
    slots = lengths.shape[0]
    rows = jnp.where(buckets == 0, B0, jnp.where(buckets == 1, B1, jnp.where(buckets == 2, B2, B3)))
    padded = jnp.where(lengths > 0, rows, 0).astype(jnp.int32)
    before = jnp.tril(jnp.ones((slots, slots), jnp.int32), -1)
    starts = jnp.sum(before * padded[None, :], axis=1)
    ids = first_own + lax.broadcasted_iota(jnp.int32, (own_rows, slots), 0)
    inside = (ids >= starts[None, :]) & (ids < (starts + lengths)[None, :])
    return jnp.any(inside, axis=1, keepdims=True)


def chip_bits():
    return list(range(1, lax.axis_size("wide").bit_length() - 1))


def hop(value, flip):
    size = lax.axis_size("wide")
    return lax.ppermute(value, "wide", tuple((i, i ^ flip) for i in range(size)))


def bits_at(shift, count=1):
    return ((lax.axis_index("wide") >> shift) % (1 << count)).astype(jnp.int32)


def fold_kernel(parts, place, meta, mine_ref, got_ref, *out_refs):
    rows = out_refs[0].shape[0]
    for flip, out_ref in enumerate(out_refs):
        start = pl.multiple_of((meta[place] ^ flip) * rows, rows)
        total = mine_ref[pl.ds(start, rows), :].astype(F32) + got_ref[pl.ds(start, rows), :].astype(F32)
        out_ref[...] = total.astype(BF16)


def fold(meta, mine, got, parts, place, index):
    rows = mine.shape[0] // parts
    if rows % 32:
        total = (mine.astype(F32) + got.astype(F32)).astype(BF16)
        return [
            lax.dynamic_slice_in_dim(total, (index ^ flip) * rows, rows) for flip in range(parts)
        ]
    return call(
        partial(fold_kernel, parts, place),
        [shape((rows, mine.shape[1]))] * parts,
        (meta, mine, got),
        1,
        "fold",
        scalars=1,
    )


def gather_kernel(place, meta, *refs):
    out_ref = refs[-1]
    rows = refs[0].shape[0]
    for flip, ref in enumerate(refs[:-1]):
        start = pl.multiple_of((meta[place] ^ flip) * rows, rows)
        out_ref[pl.ds(start, rows), :] = ref[...]


def gather(meta, pieces, place, index):
    rows, columns = pieces[0].shape
    if rows % 32:
        total = jnp.zeros((rows * len(pieces), columns), pieces[0].dtype)
        for flip, piece in enumerate(pieces):
            total = lax.dynamic_update_slice_in_dim(total, piece, (index ^ flip) * rows, 0)
        return total
    return call(
        partial(gather_kernel, place),
        shape((rows * len(pieces), columns)),
        (meta, *pieces),
        1,
        "gather",
        scalars=1,
    )


def quarter(w_proj, bit):
    rows, columns = w_proj.shape[0] // 2, w_proj.shape[1] // 2
    part = lax.dynamic_slice(w_proj, (bits_at(bit) * rows, bits_at(0) * columns), (rows, columns))
    return lax.ppermute(part, "narrow", SWAP)


def shards(
    tokens,
    token_marks,
    crop_lengths,
    bucket_ids,
    mask_token,
    norm1_gain,
    norm1_bias,
    w_qkv,
    qv_bias,
    w_proj,
    proj_bias,
    scale_attn,
    norm2_gain,
    norm2_bias,
    w_fc1,
    fc1_bias,
    w_fc2,
    fc2_bias,
    scale_mlp,
    cotangent,
):
    half, width = tokens.shape
    slots = crop_lengths.shape[0]
    local = w_qkv.shape[2]
    pairs = local // 128
    units = w_fc1.shape[1]
    first_own = (lax.axis_index("narrow") * half).astype(jnp.int32)
    swap = lambda v: lax.ppermute(v, "narrow", SWAP)
    singles = chip_bits()

    tokens_other = swap(tokens)
    marks_other = swap(token_marks)
    valid = own_validity(crop_lengths, bucket_ids, first_own, half)
    scale2 = scale_mlp.astype(F32)
    gout_own = jnp.where(valid, cotangent, 0).astype(BF16)
    gb_own = (scale2 * gout_own.astype(F32)).astype(BF16)
    pad = jnp.zeros((32 - slots,), jnp.int32)
    meta = jnp.concatenate(
        [
            crop_lengths,
            pad,
            bucket_ids,
            pad,
            jnp.stack(
                [first_own, bits_at(0)] + [bits_at(bit) for bit in singles]
            ),
        ]
    )
    table = [
        norm1_gain,
        norm1_bias,
        norm2_gain,
        norm2_bias,
        scale_attn,
        scale_mlp,
        proj_bias,
        fc2_bias,
        mask_token,
        qv_bias.reshape(width),
    ] + [fc1_bias[k * width : (k + 1) * width] for k in range(units // width)]
    lines = lax.broadcasted_iota(jnp.int32, (len(table), width), 0)
    vec = jnp.zeros((len(table), width), BF16)
    for k, line in enumerate(table):
        vec = jnp.where(lines == k, line[None, :], vec)

    def qkv(rows, marks):
        return call(
            qkv_kernel,
            [shape((half, width)), shape((3, pairs, half, 128)), shape((half, width))],
            (rows, marks, vec, w_qkv),
            2,
            "norm_qkv",
        )

    mark_column = (token_marks == 1).astype(F32)[:, None]
    n_own, qkv_own, x_own = qkv(tokens, mark_column)
    n_own, wp_start = lax.optimization_barrier((n_own, w_proj))
    wp_mine = quarter(wp_start, singles[0])
    tokens_other, gb_start = lax.optimization_barrier((tokens_other, gb_own))
    gb_other = swap(gb_start)
    heads_own, heads_other, qkv_all, n_other, x_other = call(
        partial(attention_kernel, slots),
        [
            shape((half, local)),
            shape((half, local)),
            shape((3, pairs, 2 * half + WINDOW, 128)),
            shape((half, width)),
            shape((half, width)),
        ],
        (meta, qkv_own, tokens_other, (marks_other == 1).astype(F32)[:, None], vec, w_qkv),
        12,
        "attention",
        scratch=[pltpu.VMEM((pairs, 2 * half + WINDOW, 128), BF16)],
        scalars=1,
    )
    heads_own, heads_other, wp_mine = lax.optimization_barrier((heads_own, heads_other, wp_mine))
    wp_side = hop(wp_mine, 1 << singles[0])
    heads_own, heads_other, gb_other, wp_side = lax.optimization_barrier(
        (heads_own, heads_other, gb_other, wp_side)
    )
    got_other = swap(heads_own)
    got_own = swap(heads_other)
    wp_mine = gather(meta, [wp_mine, wp_side], 66, bits_at(singles[0]))
    wp_next = hop(wp_mine, 1)

    def feed(mine, theirs, x, gb, keep):
        outs = [shape((half, width)), shape((half, units)), shape((half, units)), shape((half, width))]
        if keep:
            outs.append(shape((half, width), F32))
        return call(
            partial(feed_kernel, keep),
            outs,
            (meta, mine, theirs, x, gb, vec, w_proj, wp_mine, wp_next, w_fc1, w_fc2),
            7,
            "feed",
            scratch=[pltpu.VMEM((half, width), F32)],
            scalars=1,
        )

    n2_other, act_other, gpre_other, gn2_other = feed(
        heads_other, got_other, x_other, gb_other, False
    )
    gn2_got = [swap(gn2_other[:WINDOW]), swap(gn2_other[WINDOW:])]
    n2_own, act_own, gpre_own, gn2_own, attn_own = feed(
        heads_own, got_own, x_own, gb_own, True
    )
    def middle(k, *arrays):
        return call(
            partial(middle_kernel, k * WINDOW),
            [shape((WINDOW, width), F32), shape((WINDOW, width)), shape((4, width), F32)],
            (*arrays, vec),
            2,
            "middle",
        )

    hidden_0, ga_own_0, sums_0 = middle(0, gn2_own, gn2_got[0], attn_own, x_own, gout_own)
    ga_other_0 = swap(ga_own_0)
    act_own, ga_own_0 = lax.optimization_barrier((act_own, ga_own_0))
    g_fc1, g_fc2, g_fc1b = feed_grads(
        n2_own, n2_other, act_own, act_other, gpre_own, gpre_other, gb_own, gb_other
    )

    gn2_got_1, g_fc1, g_fc2, ga_other_0 = lax.optimization_barrier(
        (gn2_got[1], g_fc1, g_fc2, ga_other_0)
    )
    sum_fc1, sum_fc2 = lax.psum((g_fc1, g_fc2), "wide")

    operands = (
        gn2_own, gn2_got_1, attn_own, x_own, gout_own, gb_own, act_own, act_other, qkv_all, n_own, n_other,
        heads_own, heads_other, g_fc1b, hidden_0, ga_own_0, ga_other_0, sums_0
    )

    def rest(operands):
        (
            gn2_own, gn2_got_1, attn_own, x_own, gout_own, gb_own, act_own, act_other, qkv_all, n_own, n_other, heads_own, heads_other, g_fc1b, hidden_0, ga_own_0, ga_other_0, sums_0
        ) = operands
        hidden_1, ga_own_1, sums_1 = middle(1, gn2_own, gn2_got_1, attn_own, x_own, gout_own)
        ga_other_1 = swap(ga_own_1)
        sums2 = sums_0 + sums_1
        def branch_of(act, kind):
            return call(
                branch_kernel, shape((half, width), kind), (act, w_fc2), 2, "branch"
            )

        branch_got = swap(branch_of(act_other, BF16))
        branch_own = branch_of(act_own, F32)
        ga_other_1, branch_own = lax.optimization_barrier((ga_other_1, branch_own))
        ga = (ga_own_0, ga_own_1, ga_other_0, ga_other_1)
        d_qkv = call(
            partial(attention_back_kernel, slots),
            shape((3, pairs, 2 * half + WINDOW, 128)),
            (meta, qkv_all, *ga, w_proj),
            9,
            "attention_back",
            scratch=[
                pltpu.VMEM((pairs, 2 * half + WINDOW, 128), BF16),
                pltpu.VMEM((2, pairs, B3, 128), F32),
            ],
            scalars=1,
        )
        d_qkv, branch_got = lax.optimization_barrier((d_qkv, branch_got))
        keep, give, d_bias = call(
            weight_kernel,
            [shape((2 * width, local)), shape((2 * width, local)), shape((3, local), F32)],
            (meta, d_qkv, n_own, n_other, heads_own, heads_other, *ga),
            4,
            "weights",
            scalars=1,
        )
        d_qkv, keep, give = lax.optimization_barrier((d_qkv, keep, give))
        got = hop(give, 1)
        gn1_own, gn1_other = call(
            share_kernel,
            [shape((half, width)), shape((half, width))],
            (meta, d_qkv, w_qkv),
            3,
            "share",
            scalars=1,
        )
        gn1_got = swap(gn1_other)
        got, gn1_own = lax.optimization_barrier((got, gn1_own))
        branch = branch_own + branch_got.astype(F32) + fc2_bias.astype(F32)
        hidden = x_own.astype(F32) + scale_attn.astype(F32) * attn_own
        output = jnp.where(valid, hidden + scale2 * branch, 0.0).astype(BF16)
        g_smlp = jnp.sum(gout_own.astype(F32) * branch, axis=0)
        g_fc2b = jnp.sum(gb_own.astype(F32), axis=0)
        for k, bit in enumerate(singles):
            keep, give = fold(meta, keep, got, 2, 66 + k, bits_at(bit))
            got = hop(give, 1 << bit)
            if k == 0:
                got, output, g_smlp, g_fc2b = lax.optimization_barrier((got, output, g_smlp, g_fc2b))
        keep, gn1_got = lax.optimization_barrier((keep, gn1_got))
        grad_tokens, sums1 = call(
            final_kernel,
            [shape((half, width), F32), shape((3, width), F32)],
            (gn1_own, gn1_got, x_own, hidden_0, hidden_1, mark_column, vec),
            3,
            "final",
        )
        got, grad_tokens = lax.optimization_barrier((got, grad_tokens))
        part = (keep.astype(F32) + got.astype(F32)).astype(BF16)
        wide_only = jnp.concatenate([d_bias[0], d_bias[2], g_fc1b[0]]).reshape(-1, width)
        small = jnp.concatenate([sums1, sums2, g_fc2b[None], g_smlp[None], wide_only], axis=0)
        for k in range(len(singles) - 1, 1, -1):
            part, small = lax.optimization_barrier((part, small))
            pieces = [part, hop(part, 1 << singles[k])]
            small = small + hop(small, 1 << singles[k])
            part = gather(meta, pieces, 66 + k, bits_at(singles[k]))
        part, small = lax.optimization_barrier((part, small))
        side, near = 1 << singles[0], 1 << singles[1]
        next_part, beside, across = hop(part, near), hop(part, side), hop(part, 1)
        small = small + hop(small, near)
        next_part, beside, across, small = lax.optimization_barrier((next_part, beside, across, small))
        next_beside, next_across, corner = hop(next_part, side), hop(next_part, 1), hop(beside, 1)
        small = small + hop(small, side)
        next_beside, next_across, corner, small = lax.optimization_barrier(
            (next_beside, next_across, corner, small)
        )
        next_corner = hop(next_beside, 1)
        small = small + hop(small, 1)
        count = 9
        rows = small[:count] + swap(small[:count])
        g_qkv, g_proj = call(
            unpack_kernel,
            [shape((3, width, local), F32), shape((local, width), F32)],
            (meta, part, across, beside, corner, next_part, next_across, next_beside, next_corner),
            3,
            "unpack",
            scalars=1,
        )
        return output, grad_tokens, rows, small[count:], g_qkv, g_proj

    def none(operands):
        return jax.tree.map(lambda v: jnp.zeros(v.shape, v.dtype), jax.eval_shape(rest, operands))

    output, grad_tokens, rows, flat, g_qkv, g_proj = lax.cond(
        jnp.max(crop_lengths) < 65536, rest, none, operands
    )
    flat = flat.reshape(-1)
    g_qvb = flat[: 2 * local].reshape(2, local)
    g_fc1b = flat[2 * local :]
    return (
        output,
        grad_tokens,
        rows[0],
        rows[1],
        rows[2],
        g_qkv,
        g_qvb,
        g_proj,
        rows[6],
        rows[5],
        rows[3],
        rows[4],
        sum_fc1.astype(F32),
        g_fc1b,
        sum_fc2.astype(F32),
        rows[7],
        rows[8],
    )


def solution(mesh):
    rows = P(("wide", "narrow"), None)
    return jax.shard_map(
        shards,
        mesh=mesh,
        in_specs=(
            rows,
            P(("wide", "narrow")),
            P("wide"),
            P("wide"),
            P(),
            P(),
            P(),
            P(None, None, "narrow"),
            P(None, "narrow"),
            P("narrow", None),
            P(),
            P(),
            P(),
            P(),
            P(None, "narrow"),
            P("narrow"),
            P("narrow", None),
            P(),
            P(),
            rows,
        ),
        out_specs=(
            rows,
            rows,
            P(),
            P(),
            P(),
            P(None, None, "narrow"),
            P(None, "narrow"),
            P("narrow", None),
            P(),
            P(),
            P(),
            P(),
            P(None, "narrow"),
            P("narrow"),
            P("narrow", None),
            P(),
            P(),
        ),
        check_vma=False,
    )
```

```python
from functools import partial

import jax
import jax.numpy as jnp
from jax import lax
from jax.experimental import pallas as pl
from jax.experimental.pallas import tpu as pltpu
from jax.sharding import PartitionSpec as P

HEAD_DIM = 64
B0 = 64
B1 = 144
B2 = 256
B3 = 576

epsilon = 1e-06
masked_score = -1e30
F32 = jnp.float32
BF16 = jnp.bfloat16
WINDOW = 256
BIG_ROWS = 128
SWAP = ((0, 1), (1, 0))


def nn(a, b):
    return lax.dot_general(a, b, (((1,), (0,)), ((), ())), preferred_element_type=F32)


def nt(a, b):
    return lax.dot_general(a, b, (((1,), (1,)), ((), ())), preferred_element_type=F32)


def tn(a, b):
    return lax.dot_general(a, b, (((0,), (0,)), ((), ())), preferred_element_type=F32)


def normed_of(rows_in):
    width = rows_in.shape[-1]
    mean = jnp.sum(rows_in, axis=-1, keepdims=True) * (1.0 / width)
    centered = rows_in - mean
    variance = jnp.sum(centered * centered, axis=-1, keepdims=True) * (1.0 / width)
    inverse = lax.rsqrt(variance + epsilon)
    return centered * inverse, inverse


def norm_back(grad, gain, normal, inverse):
    width = grad.shape[-1]
    g = grad * gain
    mean_g = jnp.sum(g, axis=-1, keepdims=True) * (1.0 / width)
    mean_gn = jnp.sum(g * normal, axis=-1, keepdims=True) * (1.0 / width)
    return (g - mean_g - normal * mean_gn) * inverse


def estimate(micros):
    return pl.CostEstimate(flops=int(micros * 1e9), bytes_accessed=1000, transcendentals=0)


def call(kernel, out_shape, args, micros, name, scratch=(), scalars=0):
    spec = pltpu.PrefetchScalarGridSpec(
        num_scalar_prefetch=scalars,
        grid=(),
        in_specs=[pl.BlockSpec(memory_space=pltpu.VMEM)] * (len(args) - scalars),
        out_specs=jax.tree.map(lambda s: pl.BlockSpec(memory_space=pltpu.VMEM), out_shape),
        scratch_shapes=list(scratch),
    )
    return pl.pallas_call(
        kernel,
        out_shape=out_shape,
        grid_spec=spec,
        compiler_params=pltpu.CompilerParams(vmem_limit_bytes=22 * 1024 * 1024),
        cost_estimate=estimate(micros),
        name=name,
    )(*args)


def shape(dims, kind=BF16):
    return jax.ShapeDtypeStruct(tuple(dims), kind)


def row_of(ref, k):
    return ref[k : k + 1, :].astype(F32)


def over_rows(total, body, carry=0):
    def step(i, carry):
        result = body(pl.ds(pl.multiple_of(i * WINDOW, WINDOW), WINDOW), carry)
        return carry if result is None else result

    return lax.fori_loop(0, total // WINDOW, step, carry)


def project_rows(tokens_ref, mark_ref, vec_ref, w_ref, normed_ref, x_ref, store):
    local = w_ref.shape[2]
    count = x_ref.shape[0]
    for first in range(0, count, count):
        rows = pl.ds(first, count)
        x = jnp.where(mark_ref[rows, :] > 0.5, vec_ref[8:9, :], tokens_ref[rows, :])
        x_ref[rows, :] = x
        normal, inverse = normed_of(x.astype(F32))
        normed = (normal * row_of(vec_ref, 0) + row_of(vec_ref, 1)).astype(BF16)
        normed_ref[rows, :] = normed
        for c in range(3):
            part = nn(normed, w_ref[c])
            if c != 1:
                start = 0 if c == 0 else local
                part = part + vec_ref[9:10, start : start + local].astype(F32)
            part = part.astype(BF16)
            if c == 0:
                part = part * 0.125
            for p in range(local // 128):
                store(c, p, first, part[:, p * 128 : (p + 1) * 128])


def qkv_kernel(tokens_ref, mark_ref, vec_ref, w_ref, normed_ref, qkv_ref, x_ref):
    def store(c, p, first, value):
        qkv_ref[c, p, pl.ds(first, value.shape[0]), :] = value

    project_rows(tokens_ref, mark_ref, vec_ref, w_ref, normed_ref, x_ref, store)


def slot_rows(meta, slot):
    bucket = meta[32 + slot]
    rows = jnp.where(bucket == 0, B0, jnp.where(bucket == 1, B1, jnp.where(bucket == 2, B2, B3)))
    return jnp.where(meta[slot] > 0, rows, 0)


def walk_groups(meta, slots, small, big):
    def more(state):
        slot, first = state
        return jnp.logical_and(slot < slots, meta[slot] > 0)

    def step(state):
        slot, first = state
        first = pl.multiple_of(first, 16)
        rows = slot_rows(meta, slot)

        def take_big():
            big(first, meta[slot])
            return slot + 1, first + B3

        def take_small():
            starts, ends, lasts = [jnp.int32(0)], [rows], [meta[slot]]
            going, end, count = jnp.bool_(True), rows, jnp.int32(1)
            for k in range(1, 4):
                size = slot_rows(meta, slot + k)
                going = going & (slot + k < slots) & (size > 0) & (end + size <= WINDOW)
                starts.append(jnp.where(going, end, WINDOW))
                lasts.append(jnp.where(going, end + meta[slot + k], WINDOW))
                end = jnp.where(going, end + size, end)
                ends.append(jnp.where(going, end, WINDOW))
                count = jnp.where(going, count + 1, count)
            small(first, starts, ends, lasts)
            return slot + count, first + end

        return lax.cond(rows == B3, take_big, take_small)

    lax.while_loop(more, step, (jnp.int32(0), jnp.int32(0)))


def slot_ids(ids, starts, stops, outside):
    result = jnp.full(ids.shape, outside, jnp.int32)
    for k in range(4):
        result = jnp.where((ids >= starts[k]) & (ids < stops[k]), k, result)
    return result


def attention_kernel(
    slots,
    meta,
    own_ref,
    tokens_ref,
    mark_ref,
    vec_ref,
    w_ref,
    heads_own_ref,
    heads_other_ref,
    qkv_ref,
    normed_ref,
    x_ref,
    mixed_ref,
):
    pairs = own_ref.shape[1]
    half = own_ref.shape[2]
    total = 2 * half
    first_own = pl.multiple_of(meta[64], half)
    first_other = pl.multiple_of(half - meta[64], half)

    def store(c, p, first, value):
        begin = pl.multiple_of(first_other + first, WINDOW)
        qkv_ref[c, p, pl.ds(begin, value.shape[0]), :] = value

    project_rows(tokens_ref, mark_ref, vec_ref, w_ref, normed_ref, x_ref, store)
    for c in range(3):
        for p in range(pairs):
            qkv_ref[c, p, pl.ds(first_own, half), :] = own_ref[c, p]
            qkv_ref[c, p, pl.ds(total, WINDOW), :] = jnp.zeros((WINDOW, 128), BF16)
    mixed_ref[...] = jnp.zeros(mixed_ref.shape, BF16)
    low = lax.broadcasted_iota(jnp.int32, (1, 128), 1) < HEAD_DIM
    lanes = (low, jnp.logical_not(low))

    def mix(chosen, first, count, window, mask):
        scores = []
        for p in chosen:
            q = qkv_ref[0, p, pl.ds(first, count), :]
            keys = qkv_ref[1, p, window, :]
            for h in range(2):
                scores.append(nt(jnp.where(lanes[h], q, 0), keys))
        probs = []
        for score in scores:
            score = jnp.where(mask, score, masked_score)
            exponent = jnp.exp(score - jnp.max(score, axis=1, keepdims=True))
            inverse = 1.0 / jnp.sum(exponent, axis=1, keepdims=True)
            probs.append((exponent * inverse).astype(BF16))
        for k, p in enumerate(chosen):
            values = qkv_ref[2, p, window, :]
            mixed = jnp.where(low, nn(probs[2 * k], values), nn(probs[2 * k + 1], values))
            mixed_ref[p, pl.ds(first, count), :] = mixed.astype(BF16)

    def small(first, starts, ends, lasts):
        row = slot_ids(lax.broadcasted_iota(jnp.int32, (WINDOW, 1), 0), starts, ends, 4)
        column = slot_ids(lax.broadcasted_iota(jnp.int32, (1, WINDOW), 1), starts, lasts, 5)
        mix(range(pairs), first, WINDOW, pl.ds(first, WINDOW), row == column)

    def big(first, length):
        mask = lax.broadcasted_iota(jnp.int32, (1, B3), 1) < length

        def block(b, carry):
            begin = pl.multiple_of(first + b * BIG_ROWS, 16)
            mix(range(pairs), begin, BIG_ROWS, pl.ds(first, B3), mask)
            return carry

        lax.fori_loop(0, pl.cdiv(B3, BIG_ROWS), block, 0)

    walk_groups(meta, slots, small, big)
    for p in range(pairs):
        heads_own_ref[:, p * 128 : (p + 1) * 128] = mixed_ref[p, pl.ds(first_own, half), :]
        heads_other_ref[:, p * 128 : (p + 1) * 128] = mixed_ref[p, pl.ds(first_other, half), :]


def attention_back_kernel(
    slots, meta, qkv_ref, own_ref, other_ref, w_ref, grad_ref, out_ref, sum_ref
):
    pairs = qkv_ref.shape[1]
    half = own_ref.shape[0]
    total = 2 * half
    first_own = pl.multiple_of(meta[64], half)
    first_other = pl.multiple_of(half - meta[64], half)
    for source, first in ((own_ref, first_own), (other_ref, first_other)):
        part = nt(source[...], w_ref[...]).astype(BF16)
        for p in range(pairs):
            out_ref[p, pl.ds(first, half), :] = part[:, p * 128 : (p + 1) * 128]
    for p in range(pairs):
        out_ref[p, pl.ds(total, WINDOW), :] = jnp.zeros((WINDOW, 128), BF16)
    grad_ref[...] = jnp.zeros(grad_ref.shape, BF16)
    low = lax.broadcasted_iota(jnp.int32, (1, 128), 1) < HEAD_DIM
    lanes = (low, jnp.logical_not(low))

    def back(chosen, first, count, window, mask, rows_in):
        work = []
        for p in chosen:
            q = qkv_ref[0, p, pl.ds(first, count), :]
            keys = qkv_ref[1, p, window, :]
            values = qkv_ref[2, p, window, :]
            grads = out_ref[p, pl.ds(first, count), :]
            if rows_in is not None:
                grads = jnp.where(rows_in, grads, 0)
            for h in range(2):
                q_h = jnp.where(lanes[h], q, 0)
                g_h = jnp.where(lanes[h], grads, 0)
                work.append((nt(keys, q_h), nt(values, g_h), q_h, g_h))
        pieces = []
        for scores, grad_probs, q_h, g_h in work:
            scores = jnp.where(mask, scores, masked_score)
            exponent = jnp.exp(scores - jnp.max(scores, axis=0, keepdims=True))
            probs = exponent * (1.0 / jnp.sum(exponent, axis=0, keepdims=True))
            inner = jnp.sum(probs * grad_probs, axis=0, keepdims=True)
            grad_scores = (probs * (grad_probs - inner)).astype(BF16)
            pieces.append((probs.astype(BF16), grad_scores, q_h, g_h))
        results = []
        for k, p in enumerate(chosen):
            keys = qkv_ref[1, p, window, :]
            d_query = d_key = d_value = 0.0
            for h in range(2):
                probs, grad_scores, q_h, g_h = pieces[2 * k + h]
                d_query = d_query + tn(grad_scores, jnp.where(lanes[h], keys, 0))
                d_key = d_key + nn(grad_scores, q_h)
                d_value = d_value + nn(probs, g_h)
            grad_ref[0, p, pl.ds(first, count), :] = (d_query * 0.125).astype(BF16)
            results.append((d_key, d_value))
        return results

    def small(first, starts, ends, lasts):
        key = slot_ids(lax.broadcasted_iota(jnp.int32, (WINDOW, 1), 0), starts, lasts, 5)
        query = slot_ids(lax.broadcasted_iota(jnp.int32, (1, WINDOW), 1), starts, ends, 4)
        rows_in = slot_ids(lax.broadcasted_iota(jnp.int32, (WINDOW, 1), 0), starts, ends, 4) < 4
        window = pl.ds(first, WINDOW)
        parts = back(range(pairs), first, WINDOW, window, key == query, rows_in)
        for p, (d_key, d_value) in enumerate(parts):
            grad_ref[1, p, window, :] = d_key.astype(BF16)
            grad_ref[2, p, window, :] = d_value.astype(BF16)

    def big(first, length):
        mask = lax.broadcasted_iota(jnp.int32, (B3, 1), 0) < length
        window = pl.ds(first, B3)
        sum_ref[...] = jnp.zeros(sum_ref.shape, F32)

        def block(b, carry):
            begin = pl.multiple_of(first + b * BIG_ROWS, 16)
            rows_in = lax.broadcasted_iota(jnp.int32, (BIG_ROWS, 1), 0) < B3 - b * BIG_ROWS
            for p, parts in enumerate(back(range(pairs), begin, BIG_ROWS, window, mask, rows_in)):
                for c in range(2):
                    sum_ref[c, p] += parts[c]
            return carry

        lax.fori_loop(0, pl.cdiv(B3, BIG_ROWS), block, 0)
        for p in range(pairs):
            for c in range(2):
                grad_ref[1 + c, p, window, :] = sum_ref[c, p].astype(BF16)

    walk_groups(meta, slots, small, big)


def feed_kernel(
    keep_attn,
    meta,
    mine_ref,
    theirs_ref,
    x_ref,
    gb_ref,
    vec_ref,
    wp_ref,
    wp_first_ref,
    wp_second_ref,
    w1_ref,
    w2_ref,
    normed_ref,
    act_ref,
    gpre_ref,
    grad_ref,
    *more,
):
    units = w1_ref.shape[1]
    step = x_ref.shape[1]
    sum_ref = more[-1]
    even = meta[65] == 0
    wp_theirs = jnp.concatenate(
        [
            jnp.where(even, wp_first_ref[...], wp_second_ref[...]),
            jnp.where(even, wp_second_ref[...], wp_first_ref[...]),
        ],
        axis=1,
    )

    def block(rows, carry):
        attn = nn(mine_ref[rows, :], wp_ref[...]) + nn(theirs_ref[rows, :], wp_theirs)
        attn = attn + row_of(vec_ref, 6)
        if keep_attn:
            more[0][rows, :] = attn
        hidden = x_ref[rows, :].astype(F32) + row_of(vec_ref, 4) * attn
        normal, inverse = normed_of(hidden)
        normed = (normal * row_of(vec_ref, 2) + row_of(vec_ref, 3)).astype(BF16)
        normed_ref[rows, :] = normed
        sum_ref[...] = jnp.zeros(sum_ref.shape, F32)

        def chunk(u, carry):
            cols = pl.ds(pl.multiple_of(u * step, step), step)
            shift = row_of(vec_ref, 10)
            for k in range(1, units // step):
                shift = jnp.where(u == k, row_of(vec_ref, 10 + k), shift)
            pre = nn(normed_ref[rows, :], w1_ref[:, cols]) + shift
            half_phi = 0.5 * (1.0 + lax.erf(pre * 0.7071067811865476))
            act_ref[rows, cols] = (pre * half_phi).astype(BF16)
            slope = half_phi + pre * (jnp.exp(pre * pre * -0.5) * 0.3989422804014327)
            gpre = (nt(gb_ref[rows, :], w2_ref[cols, :]) * slope).astype(BF16)
            gpre_ref[rows, cols] = gpre
            sum_ref[...] += nt(gpre, w1_ref[:, cols])
            return carry

        lax.fori_loop(0, units // step, chunk, 0)
        grad_ref[rows, :] = sum_ref[...].astype(BF16)

    block(pl.ds(0, x_ref.shape[0]), 0)


def feed_grad_kernel(
    n_own, n_other, a_own, a_other, p_own, p_other, g_own, g_other, fc1_ref, fc2_ref, bias_ref
):
    units = a_own.shape[1]
    tile = 512

    def block(i, carry):
        cols = pl.ds(pl.multiple_of(i * tile, tile), tile)
        fc1_ref[:, cols] = (
            tn(n_own[...], p_own[:, cols]) + tn(n_other[...], p_other[:, cols])
        ).astype(BF16)
        fc2_ref[cols, :] = (
            tn(a_own[:, cols], g_own[...]) + tn(a_other[:, cols], g_other[...])
        ).astype(BF16)
        bias_ref[:, cols] = jnp.sum(p_own[:, cols].astype(F32), axis=0, keepdims=True) + jnp.sum(
            p_other[:, cols].astype(F32), axis=0, keepdims=True
        )
        return carry

    lax.fori_loop(0, units // tile, block, 0)


def feed_grads(n_own, n_other, a_own, a_other, p_own, p_other, g_own, g_other):
    units = a_own.shape[1]
    width = n_own.shape[1]
    return call(
        feed_grad_kernel,
        [shape((width, units)), shape((units, width)), shape((1, units), F32)],
        (n_own, n_other, a_own, a_other, p_own, p_other, g_own, g_other),
        0.3,
        "feed_grads",
    )


def branch_kernel(act_ref, w2_ref, out_ref):
    def block(rows, carry):
        out_ref[rows, :] = nn(act_ref[rows, :], w2_ref[...]).astype(out_ref.dtype)

    over_rows(act_ref.shape[0], block)


def middle_kernel(
    begin, mine_ref, got_ref, attn_ref, x_ref, gout_ref, vec_ref, hidden_ref, ga_ref, sum_ref
):
    rows = pl.ds(begin, got_ref.shape[0])
    attn = attn_ref[rows, :]
    normal, inverse = normed_of(x_ref[rows, :].astype(F32) + row_of(vec_ref, 4) * attn)
    grad = mine_ref[rows, :].astype(F32) + got_ref[...].astype(F32)
    grad_hidden = gout_ref[rows, :].astype(F32) + norm_back(grad, row_of(vec_ref, 2), normal, inverse)
    hidden_ref[...] = grad_hidden
    grad_attn = (row_of(vec_ref, 4) * grad_hidden).astype(BF16)
    ga_ref[...] = grad_attn
    sums = [
        jnp.sum(v, axis=0, keepdims=True)
        for v in (grad * normal, grad, grad_hidden * attn, grad_attn.astype(F32))
    ]
    for k in range(4):
        sum_ref[k : k + 1, :] = sums[k]


def share_kernel(meta, grad_ref, w_ref, own_ref, other_ref):
    pairs = grad_ref.shape[1]
    half = own_ref.shape[0]
    for first, target in ((half - meta[64], other_ref), (meta[64], own_ref)):

        def block(to_rows, carry):
            rows = pl.ds(pl.multiple_of(first + to_rows.start, WINDOW), WINDOW)
            total = None
            for c in range(3):
                wide = jnp.concatenate([grad_ref[c, p, rows, :] for p in range(pairs)], axis=1)
                part = nt(wide, w_ref[c])
                total = part if total is None else total + part
            target[to_rows, :] = total.astype(BF16)

        over_rows(half, block)


def weight_kernel(
    meta, grad_ref, n_own, n_other, h_own, h_other, g_own, g_other, keep_ref, give_ref, bias_ref
):
    pairs = grad_ref.shape[1]
    half = n_own.shape[0]
    local = pairs * 128
    own = pl.ds(pl.multiple_of(meta[64], half), half)
    other = pl.ds(pl.multiple_of(half - meta[64], half), half)
    grads = []
    for c in range(3):
        wide_own = jnp.concatenate([grad_ref[c, p, own, :] for p in range(pairs)], axis=1)
        wide_other = jnp.concatenate([grad_ref[c, p, other, :] for p in range(pairs)], axis=1)
        bias_ref[c : c + 1, :] = jnp.sum(wide_own.astype(F32), axis=0, keepdims=True) + jnp.sum(
            wide_other.astype(F32), axis=0, keepdims=True
        )
        grads.append((wide_own, wide_other))
    for k, out_ref in enumerate((keep_ref, give_ref)):
        half_id = meta[65] if k == 0 else 1 - meta[65]
        columns = pl.ds(pl.multiple_of(half_id * local, local), local)
        for c in range(3):
            part = tn(n_own[:, columns], grads[c][0]) + tn(n_other[:, columns], grads[c][1])
            out_ref[pl.ds(c * local, local), :] = part.astype(BF16)
        part = tn(h_own[...], g_own[:, columns]) + tn(h_other[...], g_other[:, columns])
        out_ref[pl.ds(3 * local, local), :] = part.astype(BF16)


def final_kernel(
    mine_ref, got_ref, x_ref, hidden_ref, mark_ref, vec_ref, tokens_ref, sum_ref
):
    sums = [jnp.zeros((1, x_ref.shape[1]), F32)] * 3
    for first in range(0, x_ref.shape[0], WINDOW):
        rows = pl.ds(first, WINDOW)
        normal, inverse = normed_of(x_ref[rows, :].astype(F32))
        grad = mine_ref[rows, :].astype(F32) + got_ref[rows, :].astype(F32)
        grad_x = hidden_ref[rows, :] + norm_back(grad, row_of(vec_ref, 0), normal, inverse)
        marked = mark_ref[rows, :] > 0.5
        tokens_ref[rows, :] = jnp.where(marked, 0.0, grad_x)
        parts = [
            jnp.sum(v, axis=0, keepdims=True)
            for v in (jnp.where(marked, grad_x, 0.0), grad * normal, grad)
        ]
        sums = [a + b for a, b in zip(sums, parts)]
    for k in range(3):
        sum_ref[k : k + 1, :] = sums[k]


def unpack_kernel(count, meta, mine_ref, core_ref, side_ref, opposite_ref, *refs):
    vector_refs, pair_ref, units_ref = refs[-2 - count : -2], refs[-2], refs[-1]
    qkv_ref, proj_ref = refs[8:10]
    total = mine_ref[...] + core_ref[...]
    shared = total[:count] + (side_ref[...] + opposite_ref[...])
    for k, ref in enumerate(vector_refs):
        ref[...] = shared[k]
    width, local = total.shape[1], qkv_ref.shape[2]
    for k in range(2):
        pair_ref[k : k + 1, :] = total[count : count + 1, k * local : (k + 1) * local]
    for k in range(count + 1, total.shape[0]):
        units_ref[pl.ds((k - count - 1) * width, width)] = total[k]
    for k, ref in enumerate(refs[:8]):
        begin = pl.ds(pl.multiple_of((meta[65] ^ (k % 2)) * local, local), local)
        block = (meta[66] ^ (k // 2 % 2)) * 2 + (meta[67] ^ (k // 4))

        @pl.when(block < 3)
        def first(ref=ref, begin=begin, block=block):
            qkv_ref[block, begin, :] = ref[...].astype(F32)

        @pl.when(block == 3)
        def second(ref=ref, begin=begin):
            proj_ref[:, begin] = ref[...].astype(F32)


def own_validity(lengths, buckets, first_own, own_rows):
    slots = lengths.shape[0]
    rows = jnp.where(buckets == 0, B0, jnp.where(buckets == 1, B1, jnp.where(buckets == 2, B2, B3)))
    padded = jnp.where(lengths > 0, rows, 0).astype(jnp.int32)
    before = jnp.tril(jnp.ones((slots, slots), jnp.int32), -1)
    starts = jnp.sum(before * padded[None, :], axis=1)
    ids = first_own + lax.broadcasted_iota(jnp.int32, (own_rows, slots), 0)
    inside = (ids >= starts[None, :]) & (ids < (starts + lengths)[None, :])
    return jnp.any(inside, axis=1, keepdims=True)


def chip_bits():
    return list(range(1, lax.axis_size("wide").bit_length() - 1))


def hop(value, flip):
    size = lax.axis_size("wide")
    return lax.ppermute(value, "wide", tuple((i, i ^ flip) for i in range(size)))


def bits_at(shift, count=1):
    return ((lax.axis_index("wide") >> shift) % (1 << count)).astype(jnp.int32)


def fold_kernel(parts, place, meta, mine_ref, got_ref, *out_refs):
    rows = out_refs[0].shape[0]
    for flip, out_ref in enumerate(out_refs):
        start = pl.multiple_of((meta[place] ^ flip) * rows, rows)
        total = mine_ref[pl.ds(start, rows), :].astype(F32) + got_ref[pl.ds(start, rows), :].astype(F32)
        out_ref[...] = total.astype(BF16)


def fold(meta, mine, got, parts, place, index):
    rows = mine.shape[0] // parts
    if rows % 32:
        total = (mine.astype(F32) + got.astype(F32)).astype(BF16)
        return [
            lax.dynamic_slice_in_dim(total, (index ^ flip) * rows, rows) for flip in range(parts)
        ]
    return call(
        partial(fold_kernel, parts, place),
        [shape((rows, mine.shape[1]))] * parts,
        (meta, mine, got),
        1,
        "fold",
        scalars=1,
    )


def gather_kernel(place, meta, *refs):
    out_ref = refs[-1]
    rows = refs[0].shape[0]
    for flip, ref in enumerate(refs[:-1]):
        start = pl.multiple_of((meta[place] ^ flip) * rows, rows)
        out_ref[pl.ds(start, rows), :] = ref[...]


def gather(meta, pieces, place, index):
    rows, columns = pieces[0].shape
    if rows % 32:
        total = jnp.zeros((rows * len(pieces), columns), pieces[0].dtype)
        for flip, piece in enumerate(pieces):
            total = lax.dynamic_update_slice_in_dim(total, piece, (index ^ flip) * rows, 0)
        return total
    return call(
        partial(gather_kernel, place),
        shape((rows * len(pieces), columns)),
        (meta, *pieces),
        1,
        "gather",
        scalars=1,
    )


def quarter(w_proj, bit):
    rows, columns = w_proj.shape[0] // 2, w_proj.shape[1] // 2
    part = lax.dynamic_slice(w_proj, (bits_at(bit) * rows, bits_at(0) * columns), (rows, columns))
    return lax.ppermute(part, "narrow", SWAP)


def shards(
    tokens,
    token_marks,
    crop_lengths,
    bucket_ids,
    mask_token,
    norm1_gain,
    norm1_bias,
    w_qkv,
    qv_bias,
    w_proj,
    proj_bias,
    scale_attn,
    norm2_gain,
    norm2_bias,
    w_fc1,
    fc1_bias,
    w_fc2,
    fc2_bias,
    scale_mlp,
    cotangent,
):
    half, width = tokens.shape
    slots = crop_lengths.shape[0]
    local = w_qkv.shape[2]
    pairs = local // 128
    units = w_fc1.shape[1]
    first_own = (lax.axis_index("narrow") * half).astype(jnp.int32)
    swap = lambda v: lax.ppermute(v, "narrow", SWAP)
    singles = chip_bits()

    tokens_other = swap(tokens)
    marks_other = swap(token_marks)
    valid = own_validity(crop_lengths, bucket_ids, first_own, half)
    scale2 = scale_mlp.astype(F32)
    gout_own = jnp.where(valid, cotangent, 0).astype(BF16)
    gb_own = (scale2 * gout_own.astype(F32)).astype(BF16)
    pad = jnp.zeros((32 - slots,), jnp.int32)
    meta = jnp.concatenate(
        [
            crop_lengths,
            pad,
            bucket_ids,
            pad,
            jnp.stack(
                [first_own, bits_at(0)] + [bits_at(bit) for bit in singles]
            ),
        ]
    )
    table = [
        norm1_gain,
        norm1_bias,
        norm2_gain,
        norm2_bias,
        scale_attn,
        scale_mlp,
        proj_bias,
        fc2_bias,
        mask_token,
        qv_bias.reshape(width),
    ] + [fc1_bias[k * width : (k + 1) * width] for k in range(units // width)]
    lines = lax.broadcasted_iota(jnp.int32, (len(table), width), 0)
    vec = jnp.zeros((len(table), width), BF16)
    for k, line in enumerate(table):
        vec = jnp.where(lines == k, line[None, :], vec)

    def qkv(rows, marks):
        return call(
            qkv_kernel,
            [shape((half, width)), shape((3, pairs, half, 128)), shape((half, width))],
            (rows, marks, vec, w_qkv),
            2,
            "norm_qkv",
        )

    mark_column = (token_marks == 1).astype(F32)[:, None]
    n_own, qkv_own, x_own = qkv(tokens, mark_column)
    n_own, wp_start = lax.optimization_barrier((n_own, w_proj))
    wp_mine = quarter(wp_start, singles[0])
    tokens_other, gb_start = lax.optimization_barrier((tokens_other, gb_own))
    gb_other = swap(gb_start)
    heads_own, heads_other, qkv_all, n_other, x_other = call(
        partial(attention_kernel, slots),
        [
            shape((half, local)),
            shape((half, local)),
            shape((3, pairs, 2 * half + WINDOW, 128)),
            shape((half, width)),
            shape((half, width)),
        ],
        (meta, qkv_own, tokens_other, (marks_other == 1).astype(F32)[:, None], vec, w_qkv),
        12,
        "attention",
        scratch=[pltpu.VMEM((pairs, 2 * half + WINDOW, 128), BF16)],
        scalars=1,
    )
    heads_own, heads_other, wp_mine = lax.optimization_barrier((heads_own, heads_other, wp_mine))
    wp_side = hop(wp_mine, 1 << singles[0])
    heads_own, heads_other, gb_other, wp_side = lax.optimization_barrier(
        (heads_own, heads_other, gb_other, wp_side)
    )
    got_other = swap(heads_own)
    got_own = swap(heads_other)
    wp_mine = gather(meta, [wp_mine, wp_side], 66, bits_at(singles[0]))
    wp_next = hop(wp_mine, 1)

    def feed(mine, theirs, x, gb, keep):
        outs = [shape((half, width)), shape((half, units)), shape((half, units)), shape((half, width))]
        if keep:
            outs.append(shape((half, width), F32))
        return call(
            partial(feed_kernel, keep),
            outs,
            (meta, mine, theirs, x, gb, vec, w_proj, wp_mine, wp_next, w_fc1, w_fc2),
            7,
            "feed",
            scratch=[pltpu.VMEM((half, width), F32)],
            scalars=1,
        )

    n2_other, act_other, gpre_other, gn2_other = feed(
        heads_other, got_other, x_other, gb_other, False
    )
    gn2_got = swap(gn2_other)
    n2_own, act_own, gpre_own, gn2_own, attn_own = feed(
        heads_own, got_own, x_own, gb_own, True
    )
    g_fc1, g_fc2, g_fc1b = feed_grads(
        n2_own, n2_other, act_own, act_other, gpre_own, gpre_other, gb_own, gb_other
    )
    gn2_got, g_fc1, g_fc2 = lax.optimization_barrier((gn2_got, g_fc1, g_fc2))
    grad_hidden, ga_own, sums2 = call(
        partial(middle_kernel, 0),
        [shape((half, width), F32), shape((half, width)), shape((4, width), F32)],
        (gn2_own, gn2_got, attn_own, x_own, gout_own, vec),
        0.2,
        "middle",
    )
    sum_fc1, sum_fc2 = lax.psum((g_fc1, g_fc2), "wide")

    operands = (
        attn_own, x_own, gout_own, gb_own, act_own, act_other, qkv_all, n_own, n_other,
        heads_own, heads_other, g_fc1b, grad_hidden, ga_own, sums2
    )

    def rest(operands):
        (
            attn_own, x_own, gout_own, gb_own, act_own, act_other, qkv_all, n_own, n_other, heads_own, heads_other, g_fc1b, grad_hidden, ga_own, sums2
        ) = operands
        ga_other = swap(ga_own)

        def branch_of(act, kind):
            return call(
                branch_kernel, shape((half, width), kind), (act, w_fc2), 2, "branch"
            )

        branch_got = swap(branch_of(act_other, BF16))
        branch_own = branch_of(act_own, F32)
        ga_other, branch_own = lax.optimization_barrier((ga_other, branch_own))
        ga = (ga_own, ga_other)
        d_qkv = call(
            partial(attention_back_kernel, slots),
            shape((3, pairs, 2 * half + WINDOW, 128)),
            (meta, qkv_all, *ga, w_proj),
            9,
            "attention_back",
            scratch=[
                pltpu.VMEM((pairs, 2 * half + WINDOW, 128), BF16),
                pltpu.VMEM((2, pairs, B3, 128), F32),
            ],
            scalars=1,
        )
        d_qkv, branch_got = lax.optimization_barrier((d_qkv, branch_got))
        keep, give, d_bias = call(
            weight_kernel,
            [shape((2 * width, local)), shape((2 * width, local)), shape((3, local), F32)],
            (meta, d_qkv, n_own, n_other, heads_own, heads_other, *ga),
            4,
            "weights",
            scalars=1,
        )
        d_qkv, keep, give = lax.optimization_barrier((d_qkv, keep, give))
        got = hop(give, 1)
        gn1_own, gn1_other = call(
            share_kernel,
            [shape((half, width)), shape((half, width))],
            (meta, d_qkv, w_qkv),
            3,
            "share",
            scalars=1,
        )
        gn1_got = swap(gn1_other)
        got, gn1_own = lax.optimization_barrier((got, gn1_own))
        branch = branch_own + branch_got.astype(F32) + fc2_bias.astype(F32)
        hidden = x_own.astype(F32) + scale_attn.astype(F32) * attn_own
        output = jnp.where(valid, hidden + scale2 * branch, 0.0).astype(BF16)
        g_smlp = jnp.sum(gout_own.astype(F32) * branch, axis=0)
        g_fc2b = jnp.sum(gb_own.astype(F32), axis=0)
        for k, bit in enumerate(singles):
            keep, give = fold(meta, keep, got, 2, 66 + k, bits_at(bit))
            got = hop(give, 1 << bit)
            if k == 0:
                got, output, g_smlp, g_fc2b = lax.optimization_barrier((got, output, g_smlp, g_fc2b))
        keep, gn1_got = lax.optimization_barrier((keep, gn1_got))
        grad_tokens, sums1 = call(
            final_kernel,
            [shape((half, width), F32), shape((3, width), F32)],
            (gn1_own, gn1_got, x_own, grad_hidden, mark_column, vec),
            3,
            "final",
        )
        got, grad_tokens = lax.optimization_barrier((got, grad_tokens))
        part = (keep.astype(F32) + got.astype(F32)).astype(BF16)
        wide_only = jnp.concatenate([d_bias[0], d_bias[2], g_fc1b[0]]).reshape(-1, width)
        small = jnp.concatenate([sums1, sums2, g_fc2b[None], g_smlp[None], wide_only], axis=0)
        for k in range(len(singles) - 1, 1, -1):
            part, small = lax.optimization_barrier((part, small))
            pieces = [part, hop(part, 1 << singles[k])]
            small = small + hop(small, 1 << singles[k])
            part = gather(meta, pieces, 66 + k, bits_at(singles[k]))
        part, small = lax.optimization_barrier((part, small))
        side, near = 1 << singles[0], 1 << singles[1]
        next_part, beside, across = hop(part, near), hop(part, side), hop(part, 1)
        small = small + hop(small, near)
        next_part, beside, across, small = lax.optimization_barrier((next_part, beside, across, small))
        next_beside, next_across, corner = hop(next_part, side), hop(next_part, 1), hop(beside, 1)
        small = small + hop(small, side)
        next_beside, next_across, corner, small = lax.optimization_barrier(
            (next_beside, next_across, corner, small)
        )
        next_corner = hop(next_beside, 1)
        count = 9
        size = 2 * lax.axis_size("wide")
        opposite = lax.ppermute(
            small[:count], ("wide", "narrow"), tuple((i, i ^ 3) for i in range(size))
        )
        shared = (small, hop(small, 1), swap(small[:count]), opposite)
        g_qkv, g_proj, *vectors, g_qvb, g_fc1b = call(
            partial(unpack_kernel, count),
            [shape((3, width, local), F32), shape((local, width), F32)]
            + [shape((width,), F32)] * count
            + [shape((2, local), F32), shape((units,), F32)],
            (meta, *shared, part, across, beside, corner, next_part, next_across, next_beside, next_corner),
            3,
            "unpack",
            scalars=1,
        )
        return output, grad_tokens, vectors, g_qvb, g_fc1b, g_qkv, g_proj

    def none(operands):
        return jax.tree.map(lambda v: jnp.zeros(v.shape, v.dtype), jax.eval_shape(rest, operands))

    output, grad_tokens, rows, g_qvb, g_fc1b, g_qkv, g_proj = lax.cond(
        jnp.max(crop_lengths) < 65536, rest, none, operands
    )
    return (
        output,
        grad_tokens,
        rows[0],
        rows[1],
        rows[2],
        g_qkv,
        g_qvb,
        g_proj,
        rows[6],
        rows[5],
        rows[3],
        rows[4],
        sum_fc1.astype(F32),
        g_fc1b,
        sum_fc2.astype(F32),
        rows[7],
        rows[8],
    )


def solution(mesh):
    rows = P(("wide", "narrow"), None)
    return jax.shard_map(
        shards,
        mesh=mesh,
        in_specs=(
            rows,
            P(("wide", "narrow")),
            P("wide"),
            P("wide"),
            P(),
            P(),
            P(),
            P(None, None, "narrow"),
            P(None, "narrow"),
            P("narrow", None),
            P(),
            P(),
            P(),
            P(),
            P(None, "narrow"),
            P("narrow"),
            P("narrow", None),
            P(),
            P(),
            rows,
        ),
        out_specs=(
            rows,
            rows,
            P(),
            P(),
            P(),
            P(None, None, "narrow"),
            P(None, "narrow"),
            P("narrow", None),
            P(),
            P(),
            P(),
            P(),
            P(None, "narrow"),
            P("narrow"),
            P("narrow", None),
            P(),
            P(),
        ),
        check_vma=False,
    )
```

```python
from functools import partial

import jax
import jax.numpy as jnp
from jax import lax
from jax.experimental import pallas as pl
from jax.experimental.pallas import tpu as pltpu
from jax.sharding import PartitionSpec as P

HEAD_DIM = 64
B0 = 64
B1 = 144
B2 = 256
B3 = 576

epsilon = 1e-06
masked_score = -1e30
F32 = jnp.float32
BF16 = jnp.bfloat16
WINDOW = 256
BIG_ROWS = 128
SWAP = ((0, 1), (1, 0))


def nn(a, b):
    return lax.dot_general(a, b, (((1,), (0,)), ((), ())), preferred_element_type=F32)


def nt(a, b):
    return lax.dot_general(a, b, (((1,), (1,)), ((), ())), preferred_element_type=F32)


def tn(a, b):
    return lax.dot_general(a, b, (((0,), (0,)), ((), ())), preferred_element_type=F32)


def normed_of(rows_in):
    width = rows_in.shape[-1]
    mean = jnp.sum(rows_in, axis=-1, keepdims=True) * (1.0 / width)
    centered = rows_in - mean
    variance = jnp.sum(centered * centered, axis=-1, keepdims=True) * (1.0 / width)
    inverse = lax.rsqrt(variance + epsilon)
    return centered * inverse, inverse


def norm_back(grad, gain, normal, inverse):
    width = grad.shape[-1]
    g = grad * gain
    mean_g = jnp.sum(g, axis=-1, keepdims=True) * (1.0 / width)
    mean_gn = jnp.sum(g * normal, axis=-1, keepdims=True) * (1.0 / width)
    return (g - mean_g - normal * mean_gn) * inverse


def estimate(micros):
    return pl.CostEstimate(flops=int(micros * 1e9), bytes_accessed=1000, transcendentals=0)


def call(kernel, out_shape, args, micros, name, scratch=(), scalars=0):
    spec = pltpu.PrefetchScalarGridSpec(
        num_scalar_prefetch=scalars,
        grid=(),
        in_specs=[pl.BlockSpec(memory_space=pltpu.VMEM)] * (len(args) - scalars),
        out_specs=jax.tree.map(lambda s: pl.BlockSpec(memory_space=pltpu.VMEM), out_shape),
        scratch_shapes=list(scratch),
    )
    return pl.pallas_call(
        kernel,
        out_shape=out_shape,
        grid_spec=spec,
        compiler_params=pltpu.CompilerParams(vmem_limit_bytes=22 * 1024 * 1024),
        cost_estimate=estimate(micros),
        name=name,
    )(*args)


def shape(dims, kind=BF16):
    return jax.ShapeDtypeStruct(tuple(dims), kind)


def row_of(ref, k):
    return ref[k : k + 1, :].astype(F32)


def over_rows(total, body, carry=0):
    def step(i, carry):
        result = body(pl.ds(pl.multiple_of(i * WINDOW, WINDOW), WINDOW), carry)
        return carry if result is None else result

    return lax.fori_loop(0, total // WINDOW, step, carry)


def project_rows(tokens_ref, mark_ref, vec_ref, w_ref, normed_ref, x_ref, store):
    local = w_ref.shape[2]
    count = x_ref.shape[0]
    for first in range(0, count, count):
        rows = pl.ds(first, count)
        x = jnp.where(mark_ref[rows, :] > 0.5, vec_ref[8:9, :], tokens_ref[rows, :])
        x_ref[rows, :] = x
        normal, inverse = normed_of(x.astype(F32))
        normed = (normal * row_of(vec_ref, 0) + row_of(vec_ref, 1)).astype(BF16)
        normed_ref[rows, :] = normed
        for c in range(3):
            part = nn(normed, w_ref[c])
            if c != 1:
                start = 0 if c == 0 else local
                part = part + vec_ref[9:10, start : start + local].astype(F32)
            part = part.astype(BF16)
            if c == 0:
                part = part * 0.125
            for p in range(local // 128):
                store(c, p, first, part[:, p * 128 : (p + 1) * 128])


def qkv_kernel(tokens_ref, mark_ref, vec_ref, w_ref, normed_ref, qkv_ref, x_ref):
    def store(c, p, first, value):
        qkv_ref[c, p, pl.ds(first, value.shape[0]), :] = value

    project_rows(tokens_ref, mark_ref, vec_ref, w_ref, normed_ref, x_ref, store)


def slot_rows(meta, slot):
    bucket = meta[32 + slot]
    rows = jnp.where(bucket == 0, B0, jnp.where(bucket == 1, B1, jnp.where(bucket == 2, B2, B3)))
    return jnp.where(meta[slot] > 0, rows, 0)


def walk_groups(meta, slots, small, big):
    def more(state):
        slot, first = state
        return jnp.logical_and(slot < slots, meta[slot] > 0)

    def step(state):
        slot, first = state
        first = pl.multiple_of(first, 16)
        rows = slot_rows(meta, slot)

        def take_big():
            big(first, meta[slot])
            return slot + 1, first + B3

        def take_small():
            starts, ends, lasts = [jnp.int32(0)], [rows], [meta[slot]]
            going, end, count = jnp.bool_(True), rows, jnp.int32(1)
            for k in range(1, 4):
                size = slot_rows(meta, slot + k)
                going = going & (slot + k < slots) & (size > 0) & (end + size <= WINDOW)
                starts.append(jnp.where(going, end, WINDOW))
                lasts.append(jnp.where(going, end + meta[slot + k], WINDOW))
                end = jnp.where(going, end + size, end)
                ends.append(jnp.where(going, end, WINDOW))
                count = jnp.where(going, count + 1, count)
            small(first, starts, ends, lasts)
            return slot + count, first + end

        return lax.cond(rows == B3, take_big, take_small)

    lax.while_loop(more, step, (jnp.int32(0), jnp.int32(0)))


def slot_ids(ids, starts, stops, outside):
    result = jnp.full(ids.shape, outside, jnp.int32)
    for k in range(4):
        result = jnp.where((ids >= starts[k]) & (ids < stops[k]), k, result)
    return result


def attention_kernel(
    slots,
    meta,
    own_ref,
    tokens_ref,
    mark_ref,
    vec_ref,
    w_ref,
    heads_own_ref,
    heads_other_ref,
    qkv_ref,
    normed_ref,
    x_ref,
    mixed_ref,
):
    pairs = own_ref.shape[1]
    half = own_ref.shape[2]
    total = 2 * half
    first_own = pl.multiple_of(meta[64], half)
    first_other = pl.multiple_of(half - meta[64], half)

    def store(c, p, first, value):
        begin = pl.multiple_of(first_other + first, WINDOW)
        qkv_ref[c, p, pl.ds(begin, value.shape[0]), :] = value

    project_rows(tokens_ref, mark_ref, vec_ref, w_ref, normed_ref, x_ref, store)
    for c in range(3):
        for p in range(pairs):
            qkv_ref[c, p, pl.ds(first_own, half), :] = own_ref[c, p]
            qkv_ref[c, p, pl.ds(total, WINDOW), :] = jnp.zeros((WINDOW, 128), BF16)
    mixed_ref[...] = jnp.zeros(mixed_ref.shape, BF16)
    low = lax.broadcasted_iota(jnp.int32, (1, 128), 1) < HEAD_DIM
    lanes = (low, jnp.logical_not(low))

    def mix(chosen, first, count, window, mask):
        scores = []
        for p in chosen:
            q = qkv_ref[0, p, pl.ds(first, count), :]
            keys = qkv_ref[1, p, window, :]
            for h in range(2):
                scores.append(nt(jnp.where(lanes[h], q, 0), keys))
        probs = []
        for score in scores:
            score = jnp.where(mask, score, masked_score)
            exponent = jnp.exp(score - jnp.max(score, axis=1, keepdims=True))
            inverse = 1.0 / jnp.sum(exponent, axis=1, keepdims=True)
            probs.append((exponent * inverse).astype(BF16))
        for k, p in enumerate(chosen):
            values = qkv_ref[2, p, window, :]
            mixed = jnp.where(low, nn(probs[2 * k], values), nn(probs[2 * k + 1], values))
            mixed_ref[p, pl.ds(first, count), :] = mixed.astype(BF16)

    def small(first, starts, ends, lasts):
        row = slot_ids(lax.broadcasted_iota(jnp.int32, (WINDOW, 1), 0), starts, ends, 4)
        column = slot_ids(lax.broadcasted_iota(jnp.int32, (1, WINDOW), 1), starts, lasts, 5)
        mix(range(pairs), first, WINDOW, pl.ds(first, WINDOW), row == column)

    def big(first, length):
        mask = lax.broadcasted_iota(jnp.int32, (1, B3), 1) < length

        def block(b, carry):
            begin = pl.multiple_of(first + b * BIG_ROWS, 16)
            mix(range(pairs), begin, BIG_ROWS, pl.ds(first, B3), mask)
            return carry

        lax.fori_loop(0, pl.cdiv(B3, BIG_ROWS), block, 0)

    walk_groups(meta, slots, small, big)
    for p in range(pairs):
        heads_own_ref[:, p * 128 : (p + 1) * 128] = mixed_ref[p, pl.ds(first_own, half), :]
        heads_other_ref[:, p * 128 : (p + 1) * 128] = mixed_ref[p, pl.ds(first_other, half), :]


def attention_back_kernel(
    slots, meta, qkv_ref, own_ref, other_ref, w_ref, grad_ref, out_ref, sum_ref
):
    pairs = qkv_ref.shape[1]
    half = own_ref.shape[0]
    total = 2 * half
    first_own = pl.multiple_of(meta[64], half)
    first_other = pl.multiple_of(half - meta[64], half)
    for source, first in ((own_ref, first_own), (other_ref, first_other)):
        part = nt(source[...], w_ref[...]).astype(BF16)
        for p in range(pairs):
            out_ref[p, pl.ds(first, half), :] = part[:, p * 128 : (p + 1) * 128]
    for p in range(pairs):
        out_ref[p, pl.ds(total, WINDOW), :] = jnp.zeros((WINDOW, 128), BF16)
    grad_ref[...] = jnp.zeros(grad_ref.shape, BF16)
    low = lax.broadcasted_iota(jnp.int32, (1, 128), 1) < HEAD_DIM
    lanes = (low, jnp.logical_not(low))

    def back(chosen, first, count, window, mask, rows_in):
        work = []
        for p in chosen:
            q = qkv_ref[0, p, pl.ds(first, count), :]
            keys = qkv_ref[1, p, window, :]
            values = qkv_ref[2, p, window, :]
            grads = out_ref[p, pl.ds(first, count), :]
            if rows_in is not None:
                grads = jnp.where(rows_in, grads, 0)
            for h in range(2):
                q_h = jnp.where(lanes[h], q, 0)
                g_h = jnp.where(lanes[h], grads, 0)
                work.append((nt(keys, q_h), nt(values, g_h), q_h, g_h))
        pieces = []
        for scores, grad_probs, q_h, g_h in work:
            scores = jnp.where(mask, scores, masked_score)
            exponent = jnp.exp(scores - jnp.max(scores, axis=0, keepdims=True))
            probs = exponent * (1.0 / jnp.sum(exponent, axis=0, keepdims=True))
            inner = jnp.sum(probs * grad_probs, axis=0, keepdims=True)
            grad_scores = (probs * (grad_probs - inner)).astype(BF16)
            pieces.append((probs.astype(BF16), grad_scores, q_h, g_h))
        results = []
        for k, p in enumerate(chosen):
            keys = qkv_ref[1, p, window, :]
            d_query = d_key = d_value = 0.0
            for h in range(2):
                probs, grad_scores, q_h, g_h = pieces[2 * k + h]
                d_query = d_query + tn(grad_scores, jnp.where(lanes[h], keys, 0))
                d_key = d_key + nn(grad_scores, q_h)
                d_value = d_value + nn(probs, g_h)
            grad_ref[0, p, pl.ds(first, count), :] = (d_query * 0.125).astype(BF16)
            results.append((d_key, d_value))
        return results

    def small(first, starts, ends, lasts):
        key = slot_ids(lax.broadcasted_iota(jnp.int32, (WINDOW, 1), 0), starts, lasts, 5)
        query = slot_ids(lax.broadcasted_iota(jnp.int32, (1, WINDOW), 1), starts, ends, 4)
        rows_in = slot_ids(lax.broadcasted_iota(jnp.int32, (WINDOW, 1), 0), starts, ends, 4) < 4
        window = pl.ds(first, WINDOW)
        parts = back(range(pairs), first, WINDOW, window, key == query, rows_in)
        for p, (d_key, d_value) in enumerate(parts):
            grad_ref[1, p, window, :] = d_key.astype(BF16)
            grad_ref[2, p, window, :] = d_value.astype(BF16)

    def big(first, length):
        mask = lax.broadcasted_iota(jnp.int32, (B3, 1), 0) < length
        window = pl.ds(first, B3)
        sum_ref[...] = jnp.zeros(sum_ref.shape, F32)

        def block(b, carry):
            begin = pl.multiple_of(first + b * BIG_ROWS, 16)
            rows_in = lax.broadcasted_iota(jnp.int32, (BIG_ROWS, 1), 0) < B3 - b * BIG_ROWS
            for p, parts in enumerate(back(range(pairs), begin, BIG_ROWS, window, mask, rows_in)):
                for c in range(2):
                    sum_ref[c, p] += parts[c]
            return carry

        lax.fori_loop(0, pl.cdiv(B3, BIG_ROWS), block, 0)
        for p in range(pairs):
            for c in range(2):
                grad_ref[1 + c, p, window, :] = sum_ref[c, p].astype(BF16)

    walk_groups(meta, slots, small, big)


def feed_kernel(
    keep_attn,
    meta,
    mine_ref,
    theirs_ref,
    x_ref,
    gb_ref,
    vec_ref,
    wp_ref,
    wp_first_ref,
    wp_second_ref,
    w1_ref,
    w2_ref,
    normed_ref,
    act_ref,
    gpre_ref,
    grad_ref,
    *more,
):
    units = w1_ref.shape[1]
    step = x_ref.shape[1]
    sum_ref = more[-1]
    even = meta[65] == 0
    wp_theirs = jnp.concatenate(
        [
            jnp.where(even, wp_first_ref[...], wp_second_ref[...]),
            jnp.where(even, wp_second_ref[...], wp_first_ref[...]),
        ],
        axis=1,
    )

    def block(rows, carry):
        attn = nn(mine_ref[rows, :], wp_ref[...]) + nn(theirs_ref[rows, :], wp_theirs)
        attn = attn + row_of(vec_ref, 6)
        if keep_attn:
            more[0][rows, :] = attn
        hidden = x_ref[rows, :].astype(F32) + row_of(vec_ref, 4) * attn
        normal, inverse = normed_of(hidden)
        normed = (normal * row_of(vec_ref, 2) + row_of(vec_ref, 3)).astype(BF16)
        normed_ref[rows, :] = normed
        sum_ref[...] = jnp.zeros(sum_ref.shape, F32)

        def chunk(u, carry):
            cols = pl.ds(pl.multiple_of(u * step, step), step)
            shift = row_of(vec_ref, 10)
            for k in range(1, units // step):
                shift = jnp.where(u == k, row_of(vec_ref, 10 + k), shift)
            pre = nn(normed_ref[rows, :], w1_ref[:, cols]) + shift
            half_phi = 0.5 * (1.0 + lax.erf(pre * 0.7071067811865476))
            act_ref[rows, cols] = (pre * half_phi).astype(BF16)
            slope = half_phi + pre * (jnp.exp(pre * pre * -0.5) * 0.3989422804014327)
            gpre = (nt(gb_ref[rows, :], w2_ref[cols, :]) * slope).astype(BF16)
            gpre_ref[rows, cols] = gpre
            sum_ref[...] += nt(gpre, w1_ref[:, cols])
            return carry

        lax.fori_loop(0, units // step, chunk, 0)
        grad_ref[rows, :] = sum_ref[...].astype(BF16)

    block(pl.ds(0, x_ref.shape[0]), 0)


def feed_grad_kernel(
    n_own, n_other, a_own, a_other, p_own, p_other, g_own, g_other, fc1_ref, fc2_ref, bias_ref
):
    units = a_own.shape[1]
    tile = 512

    def block(i, carry):
        cols = pl.ds(pl.multiple_of(i * tile, tile), tile)
        fc1_ref[:, cols] = (
            tn(n_own[...], p_own[:, cols]) + tn(n_other[...], p_other[:, cols])
        ).astype(BF16)
        fc2_ref[cols, :] = (
            tn(a_own[:, cols], g_own[...]) + tn(a_other[:, cols], g_other[...])
        ).astype(BF16)
        bias_ref[:, cols] = jnp.sum(p_own[:, cols].astype(F32), axis=0, keepdims=True) + jnp.sum(
            p_other[:, cols].astype(F32), axis=0, keepdims=True
        )
        return carry

    lax.fori_loop(0, units // tile, block, 0)


def feed_grads(n_own, n_other, a_own, a_other, p_own, p_other, g_own, g_other):
    units = a_own.shape[1]
    width = n_own.shape[1]
    return call(
        feed_grad_kernel,
        [shape((width, units)), shape((units, width)), shape((1, units), F32)],
        (n_own, n_other, a_own, a_other, p_own, p_other, g_own, g_other),
        0.3,
        "feed_grads",
    )


def branch_kernel(act_ref, w2_ref, out_ref):
    def block(rows, carry):
        out_ref[rows, :] = nn(act_ref[rows, :], w2_ref[...]).astype(out_ref.dtype)

    over_rows(act_ref.shape[0], block)


def middle_kernel(
    begin, mine_ref, got_ref, attn_ref, x_ref, gout_ref, vec_ref, hidden_ref, ga_ref, sum_ref
):
    rows = pl.ds(begin, got_ref.shape[0])
    attn = attn_ref[rows, :]
    normal, inverse = normed_of(x_ref[rows, :].astype(F32) + row_of(vec_ref, 4) * attn)
    grad = mine_ref[rows, :].astype(F32) + got_ref[...].astype(F32)
    grad_hidden = gout_ref[rows, :].astype(F32) + norm_back(grad, row_of(vec_ref, 2), normal, inverse)
    hidden_ref[...] = grad_hidden
    grad_attn = (row_of(vec_ref, 4) * grad_hidden).astype(BF16)
    ga_ref[...] = grad_attn
    sums = [
        jnp.sum(v, axis=0, keepdims=True)
        for v in (grad * normal, grad, grad_hidden * attn, grad_attn.astype(F32))
    ]
    for k in range(4):
        sum_ref[k : k + 1, :] = sums[k]


def share_kernel(meta, grad_ref, w_ref, own_ref, other_ref):
    pairs = grad_ref.shape[1]
    half = own_ref.shape[0]
    for first, target in ((half - meta[64], other_ref), (meta[64], own_ref)):

        def block(to_rows, carry):
            rows = pl.ds(pl.multiple_of(first + to_rows.start, WINDOW), WINDOW)
            total = None
            for c in range(3):
                wide = jnp.concatenate([grad_ref[c, p, rows, :] for p in range(pairs)], axis=1)
                part = nt(wide, w_ref[c])
                total = part if total is None else total + part
            target[to_rows, :] = total.astype(BF16)

        over_rows(half, block)


def weight_kernel(
    meta, grad_ref, n_own, n_other, h_own, h_other, g_own, g_other, keep_ref, give_ref, bias_ref
):
    pairs = grad_ref.shape[1]
    half = n_own.shape[0]
    local = pairs * 128
    own = pl.ds(pl.multiple_of(meta[64], half), half)
    other = pl.ds(pl.multiple_of(half - meta[64], half), half)
    grads = []
    for c in range(3):
        wide_own = jnp.concatenate([grad_ref[c, p, own, :] for p in range(pairs)], axis=1)
        wide_other = jnp.concatenate([grad_ref[c, p, other, :] for p in range(pairs)], axis=1)
        bias_ref[c : c + 1, :] = jnp.sum(wide_own.astype(F32), axis=0, keepdims=True) + jnp.sum(
            wide_other.astype(F32), axis=0, keepdims=True
        )
        grads.append((wide_own, wide_other))
    for k, out_ref in enumerate((keep_ref, give_ref)):
        half_id = meta[65] if k == 0 else 1 - meta[65]
        columns = pl.ds(pl.multiple_of(half_id * local, local), local)
        for c in range(3):
            part = tn(n_own[:, columns], grads[c][0]) + tn(n_other[:, columns], grads[c][1])
            out_ref[pl.ds(c * local, local), :] = part.astype(BF16)
        part = tn(h_own[...], g_own[:, columns]) + tn(h_other[...], g_other[:, columns])
        out_ref[pl.ds(3 * local, local), :] = part.astype(BF16)


def final_kernel(
    mine_ref, got_ref, x_ref, hidden_ref, mark_ref, vec_ref, tokens_ref, sum_ref
):
    sums = [jnp.zeros((1, x_ref.shape[1]), F32)] * 3
    for first in range(0, x_ref.shape[0], WINDOW):
        rows = pl.ds(first, WINDOW)
        normal, inverse = normed_of(x_ref[rows, :].astype(F32))
        grad = mine_ref[rows, :].astype(F32) + got_ref[rows, :].astype(F32)
        grad_x = hidden_ref[rows, :] + norm_back(grad, row_of(vec_ref, 0), normal, inverse)
        marked = mark_ref[rows, :] > 0.5
        tokens_ref[rows, :] = jnp.where(marked, 0.0, grad_x)
        parts = [
            jnp.sum(v, axis=0, keepdims=True)
            for v in (jnp.where(marked, grad_x, 0.0), grad * normal, grad)
        ]
        sums = [a + b for a, b in zip(sums, parts)]
    for k in range(3):
        sum_ref[k : k + 1, :] = sums[k]


def unpack_kernel(count, meta, mine_ref, core_ref, *refs):
    vector_refs, pair_ref, units_ref = refs[-2 - count : -2], refs[-2], refs[-1]
    qkv_ref, proj_ref = refs[8:10]
    total = mine_ref[...] + core_ref[...]
    for k, ref in enumerate(vector_refs):
        ref[...] = total[k]
    width, local = total.shape[1], qkv_ref.shape[2]
    for k in range(2):
        pair_ref[k : k + 1, :] = total[count : count + 1, k * local : (k + 1) * local]
    for k in range(count + 1, total.shape[0]):
        units_ref[pl.ds((k - count - 1) * width, width)] = total[k]
    for k, ref in enumerate(refs[:8]):
        begin = pl.ds(pl.multiple_of((meta[65] ^ (k % 2)) * local, local), local)
        block = (meta[66] ^ (k // 2 % 2)) * 2 + (meta[67] ^ (k // 4))

        @pl.when(block < 3)
        def first(ref=ref, begin=begin, block=block):
            qkv_ref[block, begin, :] = ref[...].astype(F32)

        @pl.when(block == 3)
        def second(ref=ref, begin=begin):
            proj_ref[:, begin] = ref[...].astype(F32)


def own_validity(lengths, buckets, first_own, own_rows):
    slots = lengths.shape[0]
    rows = jnp.where(buckets == 0, B0, jnp.where(buckets == 1, B1, jnp.where(buckets == 2, B2, B3)))
    padded = jnp.where(lengths > 0, rows, 0).astype(jnp.int32)
    before = jnp.tril(jnp.ones((slots, slots), jnp.int32), -1)
    starts = jnp.sum(before * padded[None, :], axis=1)
    ids = first_own + lax.broadcasted_iota(jnp.int32, (own_rows, slots), 0)
    inside = (ids >= starts[None, :]) & (ids < (starts + lengths)[None, :])
    return jnp.any(inside, axis=1, keepdims=True)


def chip_bits():
    return list(range(1, lax.axis_size("wide").bit_length() - 1))


def hop(value, flip):
    size = lax.axis_size("wide")
    return lax.ppermute(value, "wide", tuple((i, i ^ flip) for i in range(size)))


def bits_at(shift, count=1):
    return ((lax.axis_index("wide") >> shift) % (1 << count)).astype(jnp.int32)


def fold_kernel(parts, place, meta, mine_ref, got_ref, *out_refs):
    rows = out_refs[0].shape[0]
    for flip, out_ref in enumerate(out_refs):
        start = pl.multiple_of((meta[place] ^ flip) * rows, rows)
        total = mine_ref[pl.ds(start, rows), :].astype(F32) + got_ref[pl.ds(start, rows), :].astype(F32)
        out_ref[...] = total.astype(BF16)


def fold(meta, mine, got, parts, place, index):
    rows = mine.shape[0] // parts
    if rows % 32:
        total = (mine.astype(F32) + got.astype(F32)).astype(BF16)
        return [
            lax.dynamic_slice_in_dim(total, (index ^ flip) * rows, rows) for flip in range(parts)
        ]
    return call(
        partial(fold_kernel, parts, place),
        [shape((rows, mine.shape[1]))] * parts,
        (meta, mine, got),
        1,
        "fold",
        scalars=1,
    )


def gather_kernel(place, meta, *refs):
    out_ref = refs[-1]
    rows = refs[0].shape[0]
    for flip, ref in enumerate(refs[:-1]):
        start = pl.multiple_of((meta[place] ^ flip) * rows, rows)
        out_ref[pl.ds(start, rows), :] = ref[...]


def gather(meta, pieces, place, index):
    rows, columns = pieces[0].shape
    if rows % 32:
        total = jnp.zeros((rows * len(pieces), columns), pieces[0].dtype)
        for flip, piece in enumerate(pieces):
            total = lax.dynamic_update_slice_in_dim(total, piece, (index ^ flip) * rows, 0)
        return total
    return call(
        partial(gather_kernel, place),
        shape((rows * len(pieces), columns)),
        (meta, *pieces),
        1,
        "gather",
        scalars=1,
    )


def quarter(w_proj, bit):
    rows, columns = w_proj.shape[0] // 2, w_proj.shape[1] // 2
    part = lax.dynamic_slice(w_proj, (bits_at(bit) * rows, bits_at(0) * columns), (rows, columns))
    return lax.ppermute(part, "narrow", SWAP)


def shards(
    tokens,
    token_marks,
    crop_lengths,
    bucket_ids,
    mask_token,
    norm1_gain,
    norm1_bias,
    w_qkv,
    qv_bias,
    w_proj,
    proj_bias,
    scale_attn,
    norm2_gain,
    norm2_bias,
    w_fc1,
    fc1_bias,
    w_fc2,
    fc2_bias,
    scale_mlp,
    cotangent,
):
    half, width = tokens.shape
    slots = crop_lengths.shape[0]
    local = w_qkv.shape[2]
    pairs = local // 128
    units = w_fc1.shape[1]
    first_own = (lax.axis_index("narrow") * half).astype(jnp.int32)
    swap = lambda v: lax.ppermute(v, "narrow", SWAP)
    singles = chip_bits()

    tokens_other = swap(tokens)
    marks_other = swap(token_marks)
    valid = own_validity(crop_lengths, bucket_ids, first_own, half)
    scale2 = scale_mlp.astype(F32)
    gout_own = jnp.where(valid, cotangent, 0).astype(BF16)
    gb_own = (scale2 * gout_own.astype(F32)).astype(BF16)
    pad = jnp.zeros((32 - slots,), jnp.int32)
    meta = jnp.concatenate(
        [
            crop_lengths,
            pad,
            bucket_ids,
            pad,
            jnp.stack(
                [first_own, bits_at(0)] + [bits_at(bit) for bit in singles]
            ),
        ]
    )
    table = [
        norm1_gain,
        norm1_bias,
        norm2_gain,
        norm2_bias,
        scale_attn,
        scale_mlp,
        proj_bias,
        fc2_bias,
        mask_token,
        qv_bias.reshape(width),
    ] + [fc1_bias[k * width : (k + 1) * width] for k in range(units // width)]
    lines = lax.broadcasted_iota(jnp.int32, (len(table), width), 0)
    vec = jnp.zeros((len(table), width), BF16)
    for k, line in enumerate(table):
        vec = jnp.where(lines == k, line[None, :], vec)

    def qkv(rows, marks):
        return call(
            qkv_kernel,
            [shape((half, width)), shape((3, pairs, half, 128)), shape((half, width))],
            (rows, marks, vec, w_qkv),
            2,
            "norm_qkv",
        )

    mark_column = (token_marks == 1).astype(F32)[:, None]
    n_own, qkv_own, x_own = qkv(tokens, mark_column)
    n_own, wp_start = lax.optimization_barrier((n_own, w_proj))
    wp_mine = quarter(wp_start, singles[0])
    tokens_other, gb_start = lax.optimization_barrier((tokens_other, gb_own))
    gb_other = swap(gb_start)
    heads_own, heads_other, qkv_all, n_other, x_other = call(
        partial(attention_kernel, slots),
        [
            shape((half, local)),
            shape((half, local)),
            shape((3, pairs, 2 * half + WINDOW, 128)),
            shape((half, width)),
            shape((half, width)),
        ],
        (meta, qkv_own, tokens_other, (marks_other == 1).astype(F32)[:, None], vec, w_qkv),
        12,
        "attention",
        scratch=[pltpu.VMEM((pairs, 2 * half + WINDOW, 128), BF16)],
        scalars=1,
    )
    heads_own, heads_other, wp_mine = lax.optimization_barrier((heads_own, heads_other, wp_mine))
    wp_side = hop(wp_mine, 1 << singles[0])
    heads_own, heads_other, gb_other, wp_side = lax.optimization_barrier(
        (heads_own, heads_other, gb_other, wp_side)
    )
    got_other = swap(heads_own)
    got_own = swap(heads_other)
    wp_mine = gather(meta, [wp_mine, wp_side], 66, bits_at(singles[0]))
    wp_next = hop(wp_mine, 1)

    def feed(mine, theirs, x, gb, keep):
        outs = [shape((half, width)), shape((half, units)), shape((half, units)), shape((half, width))]
        if keep:
            outs.append(shape((half, width), F32))
        return call(
            partial(feed_kernel, keep),
            outs,
            (meta, mine, theirs, x, gb, vec, w_proj, wp_mine, wp_next, w_fc1, w_fc2),
            7,
            "feed",
            scratch=[pltpu.VMEM((half, width), F32)],
            scalars=1,
        )

    n2_other, act_other, gpre_other, gn2_other = feed(
        heads_other, got_other, x_other, gb_other, False
    )
    gn2_got = swap(gn2_other)
    n2_own, act_own, gpre_own, gn2_own, attn_own = feed(
        heads_own, got_own, x_own, gb_own, True
    )
    g_fc1, g_fc2, g_fc1b = feed_grads(
        n2_own, n2_other, act_own, act_other, gpre_own, gpre_other, gb_own, gb_other
    )
    gn2_got, g_fc1, g_fc2 = lax.optimization_barrier((gn2_got, g_fc1, g_fc2))
    grad_hidden, ga_own, sums2 = call(
        partial(middle_kernel, 0),
        [shape((half, width), F32), shape((half, width)), shape((4, width), F32)],
        (gn2_own, gn2_got, attn_own, x_own, gout_own, vec),
        0.2,
        "middle",
    )
    sum_fc1, sum_fc2 = lax.psum((g_fc1, g_fc2), "wide")

    operands = (
        attn_own, x_own, gout_own, gb_own, act_own, act_other, qkv_all, n_own, n_other,
        heads_own, heads_other, g_fc1b, grad_hidden, ga_own, sums2
    )

    def rest(operands):
        (
            attn_own, x_own, gout_own, gb_own, act_own, act_other, qkv_all, n_own, n_other, heads_own, heads_other, g_fc1b, grad_hidden, ga_own, sums2
        ) = operands
        ga_other = swap(ga_own)

        def branch_of(act, kind):
            return call(
                branch_kernel, shape((half, width), kind), (act, w_fc2), 2, "branch"
            )

        branch_got = swap(branch_of(act_other, BF16))
        branch_own = branch_of(act_own, F32)
        ga_other, branch_own = lax.optimization_barrier((ga_other, branch_own))
        ga = (ga_own, ga_other)
        d_qkv = call(
            partial(attention_back_kernel, slots),
            shape((3, pairs, 2 * half + WINDOW, 128)),
            (meta, qkv_all, *ga, w_proj),
            9,
            "attention_back",
            scratch=[
                pltpu.VMEM((pairs, 2 * half + WINDOW, 128), BF16),
                pltpu.VMEM((2, pairs, B3, 128), F32),
            ],
            scalars=1,
        )
        d_qkv, branch_got = lax.optimization_barrier((d_qkv, branch_got))
        keep, give, d_bias = call(
            weight_kernel,
            [shape((2 * width, local)), shape((2 * width, local)), shape((3, local), F32)],
            (meta, d_qkv, n_own, n_other, heads_own, heads_other, *ga),
            4,
            "weights",
            scalars=1,
        )
        d_qkv, keep, give = lax.optimization_barrier((d_qkv, keep, give))
        got = hop(give, 1)
        gn1_own, gn1_other = call(
            share_kernel,
            [shape((half, width)), shape((half, width))],
            (meta, d_qkv, w_qkv),
            3,
            "share",
            scalars=1,
        )
        gn1_got = swap(gn1_other)
        got, gn1_own = lax.optimization_barrier((got, gn1_own))
        branch = branch_own + branch_got.astype(F32) + fc2_bias.astype(F32)
        hidden = x_own.astype(F32) + scale_attn.astype(F32) * attn_own
        output = jnp.where(valid, hidden + scale2 * branch, 0.0).astype(BF16)
        g_smlp = jnp.sum(gout_own.astype(F32) * branch, axis=0)
        g_fc2b = jnp.sum(gb_own.astype(F32), axis=0)
        for k, bit in enumerate(singles):
            keep, give = fold(meta, keep, got, 2, 66 + k, bits_at(bit))
            got = hop(give, 1 << bit)
            if k == 0:
                got, output, g_smlp, g_fc2b = lax.optimization_barrier((got, output, g_smlp, g_fc2b))
        keep, gn1_got = lax.optimization_barrier((keep, gn1_got))
        grad_tokens, sums1 = call(
            final_kernel,
            [shape((half, width), F32), shape((3, width), F32)],
            (gn1_own, gn1_got, x_own, grad_hidden, mark_column, vec),
            3,
            "final",
        )
        got, grad_tokens = lax.optimization_barrier((got, grad_tokens))
        part = (keep.astype(F32) + got.astype(F32)).astype(BF16)
        wide_only = jnp.concatenate([d_bias[0], d_bias[2], g_fc1b[0]]).reshape(-1, width)
        small = jnp.concatenate([sums1, sums2, g_fc2b[None], g_smlp[None], wide_only], axis=0)
        for k in range(len(singles) - 1, 1, -1):
            part, small = lax.optimization_barrier((part, small))
            pieces = [part, hop(part, 1 << singles[k])]
            small = small + hop(small, 1 << singles[k])
            part = gather(meta, pieces, 66 + k, bits_at(singles[k]))
        part, small = lax.optimization_barrier((part, small))
        side, near = 1 << singles[0], 1 << singles[1]
        next_part, beside, across = hop(part, near), hop(part, side), hop(part, 1)
        small = small + hop(small, near)
        next_part, beside, across, small = lax.optimization_barrier((next_part, beside, across, small))
        next_beside, next_across, corner = hop(next_part, side), hop(next_part, 1), hop(beside, 1)
        count = 9
        flip = 2 * side + 1
        size = 2 * lax.axis_size("wide")
        opposite = lax.ppermute(
            small[:count], ("wide", "narrow"), tuple((i, i ^ flip) for i in range(size))
        )
        shared = small[:count] + swap(small[:count]) + opposite
        small = jnp.concatenate([shared, small[count:]], axis=0) + hop(small, side)
        next_beside, next_across, corner, small = lax.optimization_barrier(
            (next_beside, next_across, corner, small)
        )
        next_corner = hop(next_beside, 1)
        g_qkv, g_proj, *vectors, g_qvb, g_fc1b = call(
            partial(unpack_kernel, count),
            [shape((3, width, local), F32), shape((local, width), F32)]
            + [shape((width,), F32)] * count
            + [shape((2, local), F32), shape((units,), F32)],
            (meta, small, hop(small, 1), part, across, beside, corner, next_part, next_across, next_beside, next_corner),
            3,
            "unpack",
            scalars=1,
        )
        return output, grad_tokens, vectors, g_qvb, g_fc1b, g_qkv, g_proj

    def none(operands):
        return jax.tree.map(lambda v: jnp.zeros(v.shape, v.dtype), jax.eval_shape(rest, operands))

    output, grad_tokens, rows, g_qvb, g_fc1b, g_qkv, g_proj = lax.cond(
        jnp.max(crop_lengths) < 65536, rest, none, operands
    )
    return (
        output,
        grad_tokens,
        rows[0],
        rows[1],
        rows[2],
        g_qkv,
        g_qvb,
        g_proj,
        rows[6],
        rows[5],
        rows[3],
        rows[4],
        sum_fc1.astype(F32),
        g_fc1b,
        sum_fc2.astype(F32),
        rows[7],
        rows[8],
    )


def solution(mesh):
    rows = P(("wide", "narrow"), None)
    return jax.shard_map(
        shards,
        mesh=mesh,
        in_specs=(
            rows,
            P(("wide", "narrow")),
            P("wide"),
            P("wide"),
            P(),
            P(),
            P(),
            P(None, None, "narrow"),
            P(None, "narrow"),
            P("narrow", None),
            P(),
            P(),
            P(),
            P(),
            P(None, "narrow"),
            P("narrow"),
            P("narrow", None),
            P(),
            P(),
            rows,
        ),
        out_specs=(
            rows,
            rows,
            P(),
            P(),
            P(),
            P(None, None, "narrow"),
            P(None, "narrow"),
            P("narrow", None),
            P(),
            P(),
            P(),
            P(),
            P(None, "narrow"),
            P("narrow"),
            P("narrow", None),
            P(),
            P(),
        ),
        check_vma=False,
    )
```

```python
from functools import partial

import jax
import jax.numpy as jnp
from jax import lax
from jax.experimental import pallas as pl
from jax.experimental.pallas import tpu as pltpu
from jax.sharding import PartitionSpec as P

HEAD_DIM = 64
B0 = 64
B1 = 144
B2 = 256
B3 = 576

epsilon = 1e-06
masked_score = -1e30
F32 = jnp.float32
BF16 = jnp.bfloat16
WINDOW = 256
BIG_ROWS = 128
SWAP = ((0, 1), (1, 0))


def nn(a, b):
    return lax.dot_general(a, b, (((1,), (0,)), ((), ())), preferred_element_type=F32)


def nt(a, b):
    return lax.dot_general(a, b, (((1,), (1,)), ((), ())), preferred_element_type=F32)


def tn(a, b):
    return lax.dot_general(a, b, (((0,), (0,)), ((), ())), preferred_element_type=F32)


def normed_of(rows_in):
    width = rows_in.shape[-1]
    mean = jnp.sum(rows_in, axis=-1, keepdims=True) * (1.0 / width)
    centered = rows_in - mean
    variance = jnp.sum(centered * centered, axis=-1, keepdims=True) * (1.0 / width)
    inverse = lax.rsqrt(variance + epsilon)
    return centered * inverse, inverse


def norm_back(grad, gain, normal, inverse):
    width = grad.shape[-1]
    g = grad * gain
    mean_g = jnp.sum(g, axis=-1, keepdims=True) * (1.0 / width)
    mean_gn = jnp.sum(g * normal, axis=-1, keepdims=True) * (1.0 / width)
    return (g - mean_g - normal * mean_gn) * inverse


def estimate(micros):
    return pl.CostEstimate(flops=int(micros * 1e9), bytes_accessed=1000, transcendentals=0)


def call(kernel, out_shape, args, micros, name, scratch=(), scalars=0):
    spec = pltpu.PrefetchScalarGridSpec(
        num_scalar_prefetch=scalars,
        grid=(),
        in_specs=[pl.BlockSpec(memory_space=pltpu.VMEM)] * (len(args) - scalars),
        out_specs=jax.tree.map(lambda s: pl.BlockSpec(memory_space=pltpu.VMEM), out_shape),
        scratch_shapes=list(scratch),
    )
    return pl.pallas_call(
        kernel,
        out_shape=out_shape,
        grid_spec=spec,
        compiler_params=pltpu.CompilerParams(vmem_limit_bytes=22 * 1024 * 1024),
        cost_estimate=estimate(micros),
        name=name,
    )(*args)


def shape(dims, kind=BF16):
    return jax.ShapeDtypeStruct(tuple(dims), kind)


def row_of(ref, k):
    return ref[k : k + 1, :].astype(F32)


def over_rows(total, body, carry=0):
    def step(i, carry):
        result = body(pl.ds(pl.multiple_of(i * WINDOW, WINDOW), WINDOW), carry)
        return carry if result is None else result

    return lax.fori_loop(0, total // WINDOW, step, carry)


def project_rows(tokens_ref, mark_ref, vec_ref, w_ref, normed_ref, x_ref, store):
    local = w_ref.shape[2]
    count = x_ref.shape[0]
    for first in range(0, count, count):
        rows = pl.ds(first, count)
        x = jnp.where(mark_ref[rows, :] > 0.5, vec_ref[8:9, :], tokens_ref[rows, :])
        x_ref[rows, :] = x
        normal, inverse = normed_of(x.astype(F32))
        normed = (normal * row_of(vec_ref, 0) + row_of(vec_ref, 1)).astype(BF16)
        normed_ref[rows, :] = normed
        for c in range(3):
            part = nn(normed, w_ref[c])
            if c != 1:
                start = 0 if c == 0 else local
                part = part + vec_ref[9:10, start : start + local].astype(F32)
            part = part.astype(BF16)
            if c == 0:
                part = part * 0.125
            for p in range(local // 128):
                store(c, p, first, part[:, p * 128 : (p + 1) * 128])


def qkv_kernel(tokens_ref, mark_ref, vec_ref, w_ref, normed_ref, qkv_ref, x_ref):
    def store(c, p, first, value):
        qkv_ref[c, p, pl.ds(first, value.shape[0]), :] = value

    project_rows(tokens_ref, mark_ref, vec_ref, w_ref, normed_ref, x_ref, store)


def slot_rows(meta, slot):
    bucket = meta[32 + slot]
    rows = jnp.where(bucket == 0, B0, jnp.where(bucket == 1, B1, jnp.where(bucket == 2, B2, B3)))
    return jnp.where(meta[slot] > 0, rows, 0)


def walk_groups(meta, slots, small, big):
    def more(state):
        slot, first = state
        return jnp.logical_and(slot < slots, meta[slot] > 0)

    def step(state):
        slot, first = state
        first = pl.multiple_of(first, 16)
        rows = slot_rows(meta, slot)

        def take_big():
            big(first, meta[slot])
            return slot + 1, first + B3

        def take_small():
            starts, ends, lasts = [jnp.int32(0)], [rows], [meta[slot]]
            going, end, count = jnp.bool_(True), rows, jnp.int32(1)
            for k in range(1, 4):
                size = slot_rows(meta, slot + k)
                going = going & (slot + k < slots) & (size > 0) & (end + size <= WINDOW)
                starts.append(jnp.where(going, end, WINDOW))
                lasts.append(jnp.where(going, end + meta[slot + k], WINDOW))
                end = jnp.where(going, end + size, end)
                ends.append(jnp.where(going, end, WINDOW))
                count = jnp.where(going, count + 1, count)
            small(first, starts, ends, lasts)
            return slot + count, first + end

        return lax.cond(rows == B3, take_big, take_small)

    lax.while_loop(more, step, (jnp.int32(0), jnp.int32(0)))


def slot_ids(ids, starts, stops, outside):
    result = jnp.full(ids.shape, outside, jnp.int32)
    for k in range(4):
        result = jnp.where((ids >= starts[k]) & (ids < stops[k]), k, result)
    return result


def attention_kernel(
    slots,
    meta,
    own_ref,
    tokens_ref,
    mark_ref,
    vec_ref,
    w_ref,
    heads_own_ref,
    heads_other_ref,
    qkv_ref,
    normed_ref,
    x_ref,
    mixed_ref,
):
    pairs = own_ref.shape[1]
    half = own_ref.shape[2]
    total = 2 * half
    first_own = pl.multiple_of(meta[64], half)
    first_other = pl.multiple_of(half - meta[64], half)

    def store(c, p, first, value):
        begin = pl.multiple_of(first_other + first, WINDOW)
        qkv_ref[c, p, pl.ds(begin, value.shape[0]), :] = value

    project_rows(tokens_ref, mark_ref, vec_ref, w_ref, normed_ref, x_ref, store)
    for c in range(3):
        for p in range(pairs):
            qkv_ref[c, p, pl.ds(first_own, half), :] = own_ref[c, p]
            qkv_ref[c, p, pl.ds(total, WINDOW), :] = jnp.zeros((WINDOW, 128), BF16)
    mixed_ref[...] = jnp.zeros(mixed_ref.shape, BF16)
    low = lax.broadcasted_iota(jnp.int32, (1, 128), 1) < HEAD_DIM
    lanes = (low, jnp.logical_not(low))

    def mix(chosen, first, count, window, mask):
        scores = []
        for p in chosen:
            q = qkv_ref[0, p, pl.ds(first, count), :]
            keys = qkv_ref[1, p, window, :]
            for h in range(2):
                scores.append(nt(jnp.where(lanes[h], q, 0), keys))
        probs = []
        for score in scores:
            score = jnp.where(mask, score, masked_score)
            exponent = jnp.exp(score - jnp.max(score, axis=1, keepdims=True))
            inverse = 1.0 / jnp.sum(exponent, axis=1, keepdims=True)
            probs.append((exponent * inverse).astype(BF16))
        for k, p in enumerate(chosen):
            values = qkv_ref[2, p, window, :]
            mixed = jnp.where(low, nn(probs[2 * k], values), nn(probs[2 * k + 1], values))
            mixed_ref[p, pl.ds(first, count), :] = mixed.astype(BF16)

    def small(first, starts, ends, lasts):
        row = slot_ids(lax.broadcasted_iota(jnp.int32, (WINDOW, 1), 0), starts, ends, 4)
        column = slot_ids(lax.broadcasted_iota(jnp.int32, (1, WINDOW), 1), starts, lasts, 5)
        mix(range(pairs), first, WINDOW, pl.ds(first, WINDOW), row == column)

    def big(first, length):
        mask = lax.broadcasted_iota(jnp.int32, (1, B3), 1) < length

        def block(b, carry):
            begin = pl.multiple_of(first + b * BIG_ROWS, 16)
            mix(range(pairs), begin, BIG_ROWS, pl.ds(first, B3), mask)
            return carry

        lax.fori_loop(0, pl.cdiv(B3, BIG_ROWS), block, 0)

    walk_groups(meta, slots, small, big)
    for p in range(pairs):
        heads_own_ref[:, p * 128 : (p + 1) * 128] = mixed_ref[p, pl.ds(first_own, half), :]
        heads_other_ref[:, p * 128 : (p + 1) * 128] = mixed_ref[p, pl.ds(first_other, half), :]


def attention_back_kernel(
    slots, meta, qkv_ref, own_ref, other_ref, w_ref, grad_ref, out_ref, sum_ref
):
    pairs = qkv_ref.shape[1]
    half = own_ref.shape[0]
    total = 2 * half
    first_own = pl.multiple_of(meta[64], half)
    first_other = pl.multiple_of(half - meta[64], half)
    for source, first in ((own_ref, first_own), (other_ref, first_other)):
        part = nt(source[...], w_ref[...]).astype(BF16)
        for p in range(pairs):
            out_ref[p, pl.ds(first, half), :] = part[:, p * 128 : (p + 1) * 128]
    for p in range(pairs):
        out_ref[p, pl.ds(total, WINDOW), :] = jnp.zeros((WINDOW, 128), BF16)
    grad_ref[...] = jnp.zeros(grad_ref.shape, BF16)
    low = lax.broadcasted_iota(jnp.int32, (1, 128), 1) < HEAD_DIM
    lanes = (low, jnp.logical_not(low))

    def back(chosen, first, count, window, mask, rows_in):
        work = []
        for p in chosen:
            q = qkv_ref[0, p, pl.ds(first, count), :]
            keys = qkv_ref[1, p, window, :]
            values = qkv_ref[2, p, window, :]
            grads = out_ref[p, pl.ds(first, count), :]
            if rows_in is not None:
                grads = jnp.where(rows_in, grads, 0)
            for h in range(2):
                q_h = jnp.where(lanes[h], q, 0)
                g_h = jnp.where(lanes[h], grads, 0)
                work.append((nt(keys, q_h), nt(values, g_h), q_h, g_h))
        pieces = []
        for scores, grad_probs, q_h, g_h in work:
            scores = jnp.where(mask, scores, masked_score)
            exponent = jnp.exp(scores - jnp.max(scores, axis=0, keepdims=True))
            probs = exponent * (1.0 / jnp.sum(exponent, axis=0, keepdims=True))
            inner = jnp.sum(probs * grad_probs, axis=0, keepdims=True)
            grad_scores = (probs * (grad_probs - inner)).astype(BF16)
            pieces.append((probs.astype(BF16), grad_scores, q_h, g_h))
        results = []
        for k, p in enumerate(chosen):
            keys = qkv_ref[1, p, window, :]
            d_query = d_key = d_value = 0.0
            for h in range(2):
                probs, grad_scores, q_h, g_h = pieces[2 * k + h]
                d_query = d_query + tn(grad_scores, jnp.where(lanes[h], keys, 0))
                d_key = d_key + nn(grad_scores, q_h)
                d_value = d_value + nn(probs, g_h)
            grad_ref[0, p, pl.ds(first, count), :] = (d_query * 0.125).astype(BF16)
            results.append((d_key, d_value))
        return results

    def small(first, starts, ends, lasts):
        key = slot_ids(lax.broadcasted_iota(jnp.int32, (WINDOW, 1), 0), starts, lasts, 5)
        query = slot_ids(lax.broadcasted_iota(jnp.int32, (1, WINDOW), 1), starts, ends, 4)
        rows_in = slot_ids(lax.broadcasted_iota(jnp.int32, (WINDOW, 1), 0), starts, ends, 4) < 4
        window = pl.ds(first, WINDOW)
        parts = back(range(pairs), first, WINDOW, window, key == query, rows_in)
        for p, (d_key, d_value) in enumerate(parts):
            grad_ref[1, p, window, :] = d_key.astype(BF16)
            grad_ref[2, p, window, :] = d_value.astype(BF16)

    def big(first, length):
        mask = lax.broadcasted_iota(jnp.int32, (B3, 1), 0) < length
        window = pl.ds(first, B3)
        sum_ref[...] = jnp.zeros(sum_ref.shape, F32)

        def block(b, carry):
            begin = pl.multiple_of(first + b * BIG_ROWS, 16)
            rows_in = lax.broadcasted_iota(jnp.int32, (BIG_ROWS, 1), 0) < B3 - b * BIG_ROWS
            for p, parts in enumerate(back(range(pairs), begin, BIG_ROWS, window, mask, rows_in)):
                for c in range(2):
                    sum_ref[c, p] += parts[c]
            return carry

        lax.fori_loop(0, pl.cdiv(B3, BIG_ROWS), block, 0)
        for p in range(pairs):
            for c in range(2):
                grad_ref[1 + c, p, window, :] = sum_ref[c, p].astype(BF16)

    walk_groups(meta, slots, small, big)


def feed_kernel(
    keep_attn,
    meta,
    mine_ref,
    theirs_ref,
    x_ref,
    gb_ref,
    vec_ref,
    wp_ref,
    wp_first_ref,
    wp_second_ref,
    w1_ref,
    w2_ref,
    normed_ref,
    act_ref,
    gpre_ref,
    grad_ref,
    *more,
):
    units = w1_ref.shape[1]
    step = x_ref.shape[1]
    sum_ref = more[-1]
    even = meta[65] == 0
    wp_theirs = jnp.concatenate(
        [
            jnp.where(even, wp_first_ref[...], wp_second_ref[...]),
            jnp.where(even, wp_second_ref[...], wp_first_ref[...]),
        ],
        axis=1,
    )

    def block(rows, carry):
        attn = nn(mine_ref[rows, :], wp_ref[...]) + nn(theirs_ref[rows, :], wp_theirs)
        attn = attn + row_of(vec_ref, 6)
        if keep_attn:
            more[0][rows, :] = attn
        hidden = x_ref[rows, :].astype(F32) + row_of(vec_ref, 4) * attn
        normal, inverse = normed_of(hidden)
        normed = (normal * row_of(vec_ref, 2) + row_of(vec_ref, 3)).astype(BF16)
        normed_ref[rows, :] = normed
        sum_ref[...] = jnp.zeros(sum_ref.shape, F32)

        def chunk(u, carry):
            cols = pl.ds(pl.multiple_of(u * step, step), step)
            shift = row_of(vec_ref, 10)
            for k in range(1, units // step):
                shift = jnp.where(u == k, row_of(vec_ref, 10 + k), shift)
            pre = nn(normed_ref[rows, :], w1_ref[:, cols]) + shift
            half_phi = 0.5 * (1.0 + lax.erf(pre * 0.7071067811865476))
            act_ref[rows, cols] = (pre * half_phi).astype(BF16)
            slope = half_phi + pre * (jnp.exp(pre * pre * -0.5) * 0.3989422804014327)
            gpre = (nt(gb_ref[rows, :], w2_ref[cols, :]) * slope).astype(BF16)
            gpre_ref[rows, cols] = gpre
            sum_ref[...] += nt(gpre, w1_ref[:, cols])
            return carry

        lax.fori_loop(0, units // step, chunk, 0)
        grad_ref[rows, :] = sum_ref[...].astype(BF16)

    block(pl.ds(0, x_ref.shape[0]), 0)


def feed_grad_kernel(
    n_own, n_other, a_own, a_other, p_own, p_other, g_own, g_other, fc1_ref, fc2_ref, bias_ref
):
    units = a_own.shape[1]
    tile = 512

    def block(i, carry):
        cols = pl.ds(pl.multiple_of(i * tile, tile), tile)
        fc1_ref[:, cols] = (
            tn(n_own[...], p_own[:, cols]) + tn(n_other[...], p_other[:, cols])
        ).astype(BF16)
        fc2_ref[cols, :] = (
            tn(a_own[:, cols], g_own[...]) + tn(a_other[:, cols], g_other[...])
        ).astype(BF16)
        bias_ref[:, cols] = jnp.sum(p_own[:, cols].astype(F32), axis=0, keepdims=True) + jnp.sum(
            p_other[:, cols].astype(F32), axis=0, keepdims=True
        )
        return carry

    lax.fori_loop(0, units // tile, block, 0)


def feed_grads(n_own, n_other, a_own, a_other, p_own, p_other, g_own, g_other):
    units = a_own.shape[1]
    width = n_own.shape[1]
    return call(
        feed_grad_kernel,
        [shape((width, units)), shape((units, width)), shape((1, units), F32)],
        (n_own, n_other, a_own, a_other, p_own, p_other, g_own, g_other),
        0.3,
        "feed_grads",
    )


def branch_kernel(act_ref, w2_ref, out_ref):
    def block(rows, carry):
        out_ref[rows, :] = nn(act_ref[rows, :], w2_ref[...]).astype(out_ref.dtype)

    over_rows(act_ref.shape[0], block)


def middle_kernel(
    begin, mine_ref, got_ref, attn_ref, x_ref, gout_ref, vec_ref, hidden_ref, ga_ref, sum_ref
):
    rows = pl.ds(begin, got_ref.shape[0])
    attn = attn_ref[rows, :]
    normal, inverse = normed_of(x_ref[rows, :].astype(F32) + row_of(vec_ref, 4) * attn)
    grad = mine_ref[rows, :].astype(F32) + got_ref[...].astype(F32)
    grad_hidden = gout_ref[rows, :].astype(F32) + norm_back(grad, row_of(vec_ref, 2), normal, inverse)
    hidden_ref[...] = grad_hidden
    grad_attn = (row_of(vec_ref, 4) * grad_hidden).astype(BF16)
    ga_ref[...] = grad_attn
    sums = [
        jnp.sum(v, axis=0, keepdims=True)
        for v in (grad * normal, grad, grad_hidden * attn, grad_attn.astype(F32))
    ]
    for k in range(4):
        sum_ref[k : k + 1, :] = sums[k]


def share_kernel(meta, grad_ref, w_ref, own_ref, other_ref):
    pairs = grad_ref.shape[1]
    half = own_ref.shape[0]
    for first, target in ((half - meta[64], other_ref), (meta[64], own_ref)):

        def block(to_rows, carry):
            rows = pl.ds(pl.multiple_of(first + to_rows.start, WINDOW), WINDOW)
            total = None
            for c in range(3):
                wide = jnp.concatenate([grad_ref[c, p, rows, :] for p in range(pairs)], axis=1)
                part = nt(wide, w_ref[c])
                total = part if total is None else total + part
            target[to_rows, :] = total.astype(BF16)

        over_rows(half, block)


def weight_kernel(flip, meta, grad_ref, n_own, n_other, h_own, h_other, g_own, g_other, *outs):
    pairs = grad_ref.shape[1]
    half = n_own.shape[0]
    local = pairs * 128
    own = pl.ds(pl.multiple_of(meta[64], half), half)
    other = pl.ds(pl.multiple_of(half - meta[64], half), half)
    columns = pl.ds(pl.multiple_of((meta[65] ^ flip) * local, local), local)
    out_ref = outs[0]
    for c in range(3):
        wide_own = jnp.concatenate([grad_ref[c, p, own, :] for p in range(pairs)], axis=1)
        wide_other = jnp.concatenate([grad_ref[c, p, other, :] for p in range(pairs)], axis=1)
        if flip == 0:
            outs[1][c : c + 1, :] = jnp.sum(wide_own.astype(F32), axis=0, keepdims=True) + jnp.sum(
                wide_other.astype(F32), axis=0, keepdims=True
            )
        part = tn(n_own[:, columns], wide_own) + tn(n_other[:, columns], wide_other)
        out_ref[pl.ds(c * local, local), :] = part.astype(BF16)
    part = tn(h_own[...], g_own[:, columns]) + tn(h_other[...], g_other[:, columns])
    out_ref[pl.ds(3 * local, local), :] = part.astype(BF16)


def final_kernel(
    mine_ref, got_ref, x_ref, hidden_ref, mark_ref, vec_ref, tokens_ref, sum_ref
):
    sums = [jnp.zeros((1, x_ref.shape[1]), F32)] * 3
    for first in range(0, x_ref.shape[0], WINDOW):
        rows = pl.ds(first, WINDOW)
        normal, inverse = normed_of(x_ref[rows, :].astype(F32))
        grad = mine_ref[rows, :].astype(F32) + got_ref[rows, :].astype(F32)
        grad_x = hidden_ref[rows, :] + norm_back(grad, row_of(vec_ref, 0), normal, inverse)
        marked = mark_ref[rows, :] > 0.5
        tokens_ref[rows, :] = jnp.where(marked, 0.0, grad_x)
        parts = [
            jnp.sum(v, axis=0, keepdims=True)
            for v in (jnp.where(marked, grad_x, 0.0), grad * normal, grad)
        ]
        sums = [a + b for a, b in zip(sums, parts)]
    for k in range(3):
        sum_ref[k : k + 1, :] = sums[k]


def unpack_kernel(count, meta, mine_ref, core_ref, *refs):
    vector_refs, pair_ref, units_ref = refs[-2 - count : -2], refs[-2], refs[-1]
    qkv_ref, proj_ref = refs[8:10]
    total = mine_ref[...] + core_ref[...]
    for k, ref in enumerate(vector_refs):
        ref[...] = total[k]
    width, local = total.shape[1], qkv_ref.shape[2]
    for k in range(2):
        pair_ref[k : k + 1, :] = total[count : count + 1, k * local : (k + 1) * local]
    for k in range(count + 1, total.shape[0]):
        units_ref[pl.ds((k - count - 1) * width, width)] = total[k]
    for k, ref in enumerate(refs[:8]):
        begin = pl.ds(pl.multiple_of((meta[65] ^ (k % 2)) * local, local), local)
        block = (meta[66] ^ (k // 2 % 2)) * 2 + (meta[67] ^ (k // 4))

        @pl.when(block < 3)
        def first(ref=ref, begin=begin, block=block):
            qkv_ref[block, begin, :] = ref[...].astype(F32)

        @pl.when(block == 3)
        def second(ref=ref, begin=begin):
            proj_ref[:, begin] = ref[...].astype(F32)


def own_validity(lengths, buckets, first_own, own_rows):
    slots = lengths.shape[0]
    rows = jnp.where(buckets == 0, B0, jnp.where(buckets == 1, B1, jnp.where(buckets == 2, B2, B3)))
    padded = jnp.where(lengths > 0, rows, 0).astype(jnp.int32)
    before = jnp.tril(jnp.ones((slots, slots), jnp.int32), -1)
    starts = jnp.sum(before * padded[None, :], axis=1)
    ids = first_own + lax.broadcasted_iota(jnp.int32, (own_rows, slots), 0)
    inside = (ids >= starts[None, :]) & (ids < (starts + lengths)[None, :])
    return jnp.any(inside, axis=1, keepdims=True)


def chip_bits():
    return list(range(1, lax.axis_size("wide").bit_length() - 1))


def hop(value, flip):
    size = lax.axis_size("wide")
    return lax.ppermute(value, "wide", tuple((i, i ^ flip) for i in range(size)))


def bits_at(shift, count=1):
    return ((lax.axis_index("wide") >> shift) % (1 << count)).astype(jnp.int32)


def fold_kernel(parts, place, meta, mine_ref, got_ref, *out_refs):
    rows = out_refs[0].shape[0]
    for flip, out_ref in enumerate(out_refs):
        start = pl.multiple_of((meta[place] ^ flip) * rows, rows)
        total = mine_ref[pl.ds(start, rows), :].astype(F32) + got_ref[pl.ds(start, rows), :].astype(F32)
        out_ref[...] = total.astype(BF16)


def fold(meta, mine, got, parts, place, index):
    rows = mine.shape[0] // parts
    if rows % 32:
        total = (mine.astype(F32) + got.astype(F32)).astype(BF16)
        return [
            lax.dynamic_slice_in_dim(total, (index ^ flip) * rows, rows) for flip in range(parts)
        ]
    return call(
        partial(fold_kernel, parts, place),
        [shape((rows, mine.shape[1]))] * parts,
        (meta, mine, got),
        1,
        "fold",
        scalars=1,
    )


def gather_kernel(place, meta, *refs):
    out_ref = refs[-1]
    rows = refs[0].shape[0]
    for flip, ref in enumerate(refs[:-1]):
        start = pl.multiple_of((meta[place] ^ flip) * rows, rows)
        out_ref[pl.ds(start, rows), :] = ref[...]


def gather(meta, pieces, place, index):
    rows, columns = pieces[0].shape
    if rows % 32:
        total = jnp.zeros((rows * len(pieces), columns), pieces[0].dtype)
        for flip, piece in enumerate(pieces):
            total = lax.dynamic_update_slice_in_dim(total, piece, (index ^ flip) * rows, 0)
        return total
    return call(
        partial(gather_kernel, place),
        shape((rows * len(pieces), columns)),
        (meta, *pieces),
        1,
        "gather",
        scalars=1,
    )


def quarter(w_proj, bit):
    rows, columns = w_proj.shape[0] // 2, w_proj.shape[1] // 2
    part = lax.dynamic_slice(w_proj, (bits_at(bit) * rows, bits_at(0) * columns), (rows, columns))
    return lax.ppermute(part, "narrow", SWAP)


def shards(
    tokens,
    token_marks,
    crop_lengths,
    bucket_ids,
    mask_token,
    norm1_gain,
    norm1_bias,
    w_qkv,
    qv_bias,
    w_proj,
    proj_bias,
    scale_attn,
    norm2_gain,
    norm2_bias,
    w_fc1,
    fc1_bias,
    w_fc2,
    fc2_bias,
    scale_mlp,
    cotangent,
):
    half, width = tokens.shape
    slots = crop_lengths.shape[0]
    local = w_qkv.shape[2]
    pairs = local // 128
    units = w_fc1.shape[1]
    first_own = (lax.axis_index("narrow") * half).astype(jnp.int32)
    swap = lambda v: lax.ppermute(v, "narrow", SWAP)
    singles = chip_bits()

    tokens_other = swap(tokens)
    marks_other = swap(token_marks)
    valid = own_validity(crop_lengths, bucket_ids, first_own, half)
    scale2 = scale_mlp.astype(F32)
    gout_own = jnp.where(valid, cotangent, 0).astype(BF16)
    gb_own = (scale2 * gout_own.astype(F32)).astype(BF16)
    pad = jnp.zeros((32 - slots,), jnp.int32)
    meta = jnp.concatenate(
        [
            crop_lengths,
            pad,
            bucket_ids,
            pad,
            jnp.stack(
                [first_own, bits_at(0)] + [bits_at(bit) for bit in singles]
            ),
        ]
    )
    table = [
        norm1_gain,
        norm1_bias,
        norm2_gain,
        norm2_bias,
        scale_attn,
        scale_mlp,
        proj_bias,
        fc2_bias,
        mask_token,
        qv_bias.reshape(width),
    ] + [fc1_bias[k * width : (k + 1) * width] for k in range(units // width)]
    lines = lax.broadcasted_iota(jnp.int32, (len(table), width), 0)
    vec = jnp.zeros((len(table), width), BF16)
    for k, line in enumerate(table):
        vec = jnp.where(lines == k, line[None, :], vec)

    def qkv(rows, marks):
        return call(
            qkv_kernel,
            [shape((half, width)), shape((3, pairs, half, 128)), shape((half, width))],
            (rows, marks, vec, w_qkv),
            2,
            "norm_qkv",
        )

    mark_column = (token_marks == 1).astype(F32)[:, None]
    n_own, qkv_own, x_own = qkv(tokens, mark_column)
    n_own, wp_start = lax.optimization_barrier((n_own, w_proj))
    wp_mine = quarter(wp_start, singles[0])
    tokens_other, gb_start = lax.optimization_barrier((tokens_other, gb_own))
    gb_other = swap(gb_start)
    heads_own, heads_other, qkv_all, n_other, x_other = call(
        partial(attention_kernel, slots),
        [
            shape((half, local)),
            shape((half, local)),
            shape((3, pairs, 2 * half + WINDOW, 128)),
            shape((half, width)),
            shape((half, width)),
        ],
        (meta, qkv_own, tokens_other, (marks_other == 1).astype(F32)[:, None], vec, w_qkv),
        12,
        "attention",
        scratch=[pltpu.VMEM((pairs, 2 * half + WINDOW, 128), BF16)],
        scalars=1,
    )
    heads_own, heads_other, wp_mine = lax.optimization_barrier((heads_own, heads_other, wp_mine))
    wp_side = hop(wp_mine, 1 << singles[0])
    heads_own, heads_other, gb_other, wp_side = lax.optimization_barrier(
        (heads_own, heads_other, gb_other, wp_side)
    )
    got_other = swap(heads_own)
    got_own = swap(heads_other)
    wp_mine = gather(meta, [wp_mine, wp_side], 66, bits_at(singles[0]))
    wp_next = hop(wp_mine, 1)

    def feed(mine, theirs, x, gb, keep):
        outs = [shape((half, width)), shape((half, units)), shape((half, units)), shape((half, width))]
        if keep:
            outs.append(shape((half, width), F32))
        return call(
            partial(feed_kernel, keep),
            outs,
            (meta, mine, theirs, x, gb, vec, w_proj, wp_mine, wp_next, w_fc1, w_fc2),
            7,
            "feed",
            scratch=[pltpu.VMEM((half, width), F32)],
            scalars=1,
        )

    n2_other, act_other, gpre_other, gn2_other = feed(
        heads_other, got_other, x_other, gb_other, False
    )
    gn2_got = swap(gn2_other)
    n2_own, act_own, gpre_own, gn2_own, attn_own = feed(
        heads_own, got_own, x_own, gb_own, True
    )
    g_fc1, g_fc2, g_fc1b = feed_grads(
        n2_own, n2_other, act_own, act_other, gpre_own, gpre_other, gb_own, gb_other
    )
    gn2_got, g_fc1, g_fc2 = lax.optimization_barrier((gn2_got, g_fc1, g_fc2))
    grad_hidden, ga_own, sums2 = call(
        partial(middle_kernel, 0),
        [shape((half, width), F32), shape((half, width)), shape((4, width), F32)],
        (gn2_own, gn2_got, attn_own, x_own, gout_own, vec),
        0.2,
        "middle",
    )
    sum_fc1, sum_fc2 = lax.psum((g_fc1, g_fc2), "wide")

    operands = (
        attn_own, x_own, gout_own, gb_own, act_own, act_other, qkv_all, n_own, n_other,
        heads_own, heads_other, g_fc1b, grad_hidden, ga_own, sums2
    )

    def rest(operands):
        (
            attn_own, x_own, gout_own, gb_own, act_own, act_other, qkv_all, n_own, n_other, heads_own, heads_other, g_fc1b, grad_hidden, ga_own, sums2
        ) = operands
        ga_other = swap(ga_own)

        def branch_of(act, kind):
            return call(
                branch_kernel, shape((half, width), kind), (act, w_fc2), 2, "branch"
            )

        branch_got = swap(branch_of(act_other, BF16))
        branch_own = branch_of(act_own, F32)
        ga_other, branch_own = lax.optimization_barrier((ga_other, branch_own))
        ga = (ga_own, ga_other)
        d_qkv = call(
            partial(attention_back_kernel, slots),
            shape((3, pairs, 2 * half + WINDOW, 128)),
            (meta, qkv_all, *ga, w_proj),
            9,
            "attention_back",
            scratch=[
                pltpu.VMEM((pairs, 2 * half + WINDOW, 128), BF16),
                pltpu.VMEM((2, pairs, B3, 128), F32),
            ],
            scalars=1,
        )
        d_qkv, branch_got = lax.optimization_barrier((d_qkv, branch_got))
        arrays = (n_own, n_other, heads_own, heads_other, *ga)
        (give,) = call(
            partial(weight_kernel, 1),
            [shape((2 * width, local))],
            (meta, d_qkv, *arrays),
            2,
            "weights_give",
            scalars=1,
        )
        d_qkv, give = lax.optimization_barrier((d_qkv, give))
        got = hop(give, 1)
        keep, d_bias = call(
            partial(weight_kernel, 0),
            [shape((2 * width, local)), shape((3, local), F32)],
            (meta, d_qkv, *arrays),
            2,
            "weights_keep",
            scalars=1,
        )
        d_qkv, keep, got = lax.optimization_barrier((d_qkv, keep, got))
        gn1_own, gn1_other = call(
            share_kernel,
            [shape((half, width)), shape((half, width))],
            (meta, d_qkv, w_qkv),
            3,
            "share",
            scalars=1,
        )
        gn1_got = swap(gn1_other)
        branch = branch_own + branch_got.astype(F32) + fc2_bias.astype(F32)
        hidden = x_own.astype(F32) + scale_attn.astype(F32) * attn_own
        output = jnp.where(valid, hidden + scale2 * branch, 0.0).astype(BF16)
        g_smlp = jnp.sum(gout_own.astype(F32) * branch, axis=0)
        g_fc2b = jnp.sum(gb_own.astype(F32), axis=0)
        for k, bit in enumerate(singles):
            keep, give = fold(meta, keep, got, 2, 66 + k, bits_at(bit))
            got = hop(give, 1 << bit)
            if k == 0:
                got, output, g_smlp, g_fc2b, gn1_own = lax.optimization_barrier(
                    (got, output, g_smlp, g_fc2b, gn1_own)
                )
        keep, gn1_got = lax.optimization_barrier((keep, gn1_got))
        grad_tokens, sums1 = call(
            final_kernel,
            [shape((half, width), F32), shape((3, width), F32)],
            (gn1_own, gn1_got, x_own, grad_hidden, mark_column, vec),
            3,
            "final",
        )
        got, grad_tokens = lax.optimization_barrier((got, grad_tokens))
        part = (keep.astype(F32) + got.astype(F32)).astype(BF16)
        wide_only = jnp.concatenate([d_bias[0], d_bias[2], g_fc1b[0]]).reshape(-1, width)
        small = jnp.concatenate([sums1, sums2, g_fc2b[None], g_smlp[None], wide_only], axis=0)
        for k in range(len(singles) - 1, 1, -1):
            part, small = lax.optimization_barrier((part, small))
            pieces = [part, hop(part, 1 << singles[k])]
            small = small + hop(small, 1 << singles[k])
            part = gather(meta, pieces, 66 + k, bits_at(singles[k]))
        part, small = lax.optimization_barrier((part, small))
        side, near = 1 << singles[0], 1 << singles[1]
        next_part, beside, across = hop(part, near), hop(part, side), hop(part, 1)
        small = small + hop(small, near)
        next_part, beside, across, small = lax.optimization_barrier((next_part, beside, across, small))
        next_beside, next_across, corner = hop(next_part, side), hop(next_part, 1), hop(beside, 1)
        count = 9
        flip = 2 * side + 1
        size = 2 * lax.axis_size("wide")
        opposite = lax.ppermute(
            small[:count], ("wide", "narrow"), tuple((i, i ^ flip) for i in range(size))
        )
        shared = small[:count] + swap(small[:count]) + opposite
        small = jnp.concatenate([shared, small[count:]], axis=0) + hop(small, side)
        next_beside, next_across, corner, small = lax.optimization_barrier(
            (next_beside, next_across, corner, small)
        )
        next_corner = hop(next_beside, 1)
        g_qkv, g_proj, *vectors, g_qvb, g_fc1b = call(
            partial(unpack_kernel, count),
            [shape((3, width, local), F32), shape((local, width), F32)]
            + [shape((width,), F32)] * count
            + [shape((2, local), F32), shape((units,), F32)],
            (meta, small, hop(small, 1), part, across, beside, corner, next_part, next_across, next_beside, next_corner),
            3,
            "unpack",
            scalars=1,
        )
        return output, grad_tokens, vectors, g_qvb, g_fc1b, g_qkv, g_proj

    def none(operands):
        return jax.tree.map(lambda v: jnp.zeros(v.shape, v.dtype), jax.eval_shape(rest, operands))

    output, grad_tokens, rows, g_qvb, g_fc1b, g_qkv, g_proj = lax.cond(
        jnp.max(crop_lengths) < 65536, rest, none, operands
    )
    return (
        output,
        grad_tokens,
        rows[0],
        rows[1],
        rows[2],
        g_qkv,
        g_qvb,
        g_proj,
        rows[6],
        rows[5],
        rows[3],
        rows[4],
        sum_fc1.astype(F32),
        g_fc1b,
        sum_fc2.astype(F32),
        rows[7],
        rows[8],
    )


def solution(mesh):
    rows = P(("wide", "narrow"), None)
    return jax.shard_map(
        shards,
        mesh=mesh,
        in_specs=(
            rows,
            P(("wide", "narrow")),
            P("wide"),
            P("wide"),
            P(),
            P(),
            P(),
            P(None, None, "narrow"),
            P(None, "narrow"),
            P("narrow", None),
            P(),
            P(),
            P(),
            P(),
            P(None, "narrow"),
            P("narrow"),
            P("narrow", None),
            P(),
            P(),
            rows,
        ),
        out_specs=(
            rows,
            rows,
            P(),
            P(),
            P(),
            P(None, None, "narrow"),
            P(None, "narrow"),
            P("narrow", None),
            P(),
            P(),
            P(),
            P(),
            P(None, "narrow"),
            P("narrow"),
            P("narrow", None),
            P(),
            P(),
        ),
        check_vma=False,
    )
```

```python
from functools import partial

import jax
import jax.numpy as jnp
from jax import lax
from jax.experimental import pallas as pl
from jax.experimental.pallas import tpu as pltpu
from jax.sharding import PartitionSpec as P

HEAD_DIM = 64
B0 = 64
B1 = 144
B2 = 256
B3 = 576

epsilon = 1e-06
masked_score = -1e30
F32 = jnp.float32
BF16 = jnp.bfloat16
WINDOW = 256
BIG_ROWS = 128
MIX_ROWS = 144
SWAP = ((0, 1), (1, 0))


def nn(a, b):
    return lax.dot_general(a, b, (((1,), (0,)), ((), ())), preferred_element_type=F32)


def nt(a, b):
    return lax.dot_general(a, b, (((1,), (1,)), ((), ())), preferred_element_type=F32)


def tn(a, b):
    return lax.dot_general(a, b, (((0,), (0,)), ((), ())), preferred_element_type=F32)


def normed_of(rows_in):
    width = rows_in.shape[-1]
    mean = jnp.sum(rows_in, axis=-1, keepdims=True) * (1.0 / width)
    centered = rows_in - mean
    variance = jnp.sum(centered * centered, axis=-1, keepdims=True) * (1.0 / width)
    inverse = lax.rsqrt(variance + epsilon)
    return centered * inverse, inverse


def norm_back(grad, gain, normal, inverse):
    width = grad.shape[-1]
    g = grad * gain
    mean_g = jnp.sum(g, axis=-1, keepdims=True) * (1.0 / width)
    mean_gn = jnp.sum(g * normal, axis=-1, keepdims=True) * (1.0 / width)
    return (g - mean_g - normal * mean_gn) * inverse


def estimate(micros):
    return pl.CostEstimate(flops=int(micros * 1e9), bytes_accessed=1000, transcendentals=0)


def call(kernel, out_shape, args, micros, name, scratch=(), scalars=0):
    spec = pltpu.PrefetchScalarGridSpec(
        num_scalar_prefetch=scalars,
        grid=(),
        in_specs=[pl.BlockSpec(memory_space=pltpu.VMEM)] * (len(args) - scalars),
        out_specs=jax.tree.map(lambda s: pl.BlockSpec(memory_space=pltpu.VMEM), out_shape),
        scratch_shapes=list(scratch),
    )
    return pl.pallas_call(
        kernel,
        out_shape=out_shape,
        grid_spec=spec,
        compiler_params=pltpu.CompilerParams(vmem_limit_bytes=22 * 1024 * 1024),
        cost_estimate=estimate(micros),
        name=name,
    )(*args)


def shape(dims, kind=BF16):
    return jax.ShapeDtypeStruct(tuple(dims), kind)


def row_of(ref, k):
    return ref[k : k + 1, :].astype(F32)


def over_rows(total, body, carry=0):
    def step(i, carry):
        result = body(pl.ds(pl.multiple_of(i * WINDOW, WINDOW), WINDOW), carry)
        return carry if result is None else result

    return lax.fori_loop(0, total // WINDOW, step, carry)


def project_rows(tokens_ref, mark_ref, vec_ref, w_ref, normed_ref, x_ref, store):
    local = w_ref.shape[2]
    count = x_ref.shape[0]
    for first in range(0, count, count):
        rows = pl.ds(first, count)
        x = jnp.where(mark_ref[rows, :] > 0.5, vec_ref[8:9, :], tokens_ref[rows, :])
        x_ref[rows, :] = x
        normal, inverse = normed_of(x.astype(F32))
        normed = (normal * row_of(vec_ref, 0) + row_of(vec_ref, 1)).astype(BF16)
        normed_ref[rows, :] = normed
        for c in range(3):
            part = nn(normed, w_ref[c])
            if c != 1:
                start = 0 if c == 0 else local
                part = part + vec_ref[9:10, start : start + local].astype(F32)
            part = part.astype(BF16)
            if c == 0:
                part = part * 0.125
            for p in range(local // 128):
                store(c, p, first, part[:, p * 128 : (p + 1) * 128])


def qkv_kernel(tokens_ref, mark_ref, vec_ref, w_ref, normed_ref, qkv_ref, x_ref):
    def store(c, p, first, value):
        qkv_ref[c, p, pl.ds(first, value.shape[0]), :] = value

    project_rows(tokens_ref, mark_ref, vec_ref, w_ref, normed_ref, x_ref, store)


def slot_rows(meta, slot):
    bucket = meta[32 + slot]
    rows = jnp.where(bucket == 0, B0, jnp.where(bucket == 1, B1, jnp.where(bucket == 2, B2, B3)))
    return jnp.where(meta[slot] > 0, rows, 0)


def walk_groups(meta, slots, small, big):
    def more(state):
        slot, first = state
        return jnp.logical_and(slot < slots, meta[slot] > 0)

    def step(state):
        slot, first = state
        first = pl.multiple_of(first, 16)
        rows = slot_rows(meta, slot)

        def take_big():
            big(first, meta[slot])
            return slot + 1, first + B3

        def take_small():
            starts, ends, lasts = [jnp.int32(0)], [rows], [meta[slot]]
            going, end, count = jnp.bool_(True), rows, jnp.int32(1)
            for k in range(1, 4):
                size = slot_rows(meta, slot + k)
                going = going & (slot + k < slots) & (size > 0) & (end + size <= WINDOW)
                starts.append(jnp.where(going, end, WINDOW))
                lasts.append(jnp.where(going, end + meta[slot + k], WINDOW))
                end = jnp.where(going, end + size, end)
                ends.append(jnp.where(going, end, WINDOW))
                count = jnp.where(going, count + 1, count)
            small(first, starts, ends, lasts)
            return slot + count, first + end

        return lax.cond(rows == B3, take_big, take_small)

    lax.while_loop(more, step, (jnp.int32(0), jnp.int32(0)))


def slot_ids(ids, starts, stops, outside):
    result = jnp.full(ids.shape, outside, jnp.int32)
    for k in range(4):
        result = jnp.where((ids >= starts[k]) & (ids < stops[k]), k, result)
    return result


def attention_kernel(
    slots,
    meta,
    own_ref,
    tokens_ref,
    mark_ref,
    vec_ref,
    w_ref,
    heads_own_ref,
    heads_other_ref,
    qkv_ref,
    normed_ref,
    x_ref,
    mixed_ref,
):
    pairs = own_ref.shape[1]
    half = own_ref.shape[2]
    total = 2 * half
    first_own = pl.multiple_of(meta[64], half)
    first_other = pl.multiple_of(half - meta[64], half)

    def store(c, p, first, value):
        begin = pl.multiple_of(first_other + first, WINDOW)
        qkv_ref[c, p, pl.ds(begin, value.shape[0]), :] = value

    project_rows(tokens_ref, mark_ref, vec_ref, w_ref, normed_ref, x_ref, store)
    for c in range(3):
        for p in range(pairs):
            qkv_ref[c, p, pl.ds(first_own, half), :] = own_ref[c, p]
            qkv_ref[c, p, pl.ds(total, WINDOW), :] = jnp.zeros((WINDOW, 128), BF16)
    mixed_ref[...] = jnp.zeros(mixed_ref.shape, BF16)
    low = lax.broadcasted_iota(jnp.int32, (1, 128), 1) < HEAD_DIM
    lanes = (low, jnp.logical_not(low))

    def mix(chosen, first, count, window, mask):
        scores = []
        for p in chosen:
            q = qkv_ref[0, p, pl.ds(first, count), :]
            keys = qkv_ref[1, p, window, :]
            for h in range(2):
                scores.append(nt(jnp.where(lanes[h], q, 0), keys))
        probs = []
        for score in scores:
            score = jnp.where(mask, score, masked_score)
            exponent = jnp.exp(score - jnp.max(score, axis=1, keepdims=True))
            inverse = 1.0 / jnp.sum(exponent, axis=1, keepdims=True)
            probs.append((exponent * inverse).astype(BF16))
        for k, p in enumerate(chosen):
            values = qkv_ref[2, p, window, :]
            mixed = jnp.where(low, nn(probs[2 * k], values), nn(probs[2 * k + 1], values))
            mixed_ref[p, pl.ds(first, count), :] = mixed.astype(BF16)

    def small(first, starts, ends, lasts):
        row = slot_ids(lax.broadcasted_iota(jnp.int32, (WINDOW, 1), 0), starts, ends, 4)
        column = slot_ids(lax.broadcasted_iota(jnp.int32, (1, WINDOW), 1), starts, lasts, 5)
        mix(range(pairs), first, WINDOW, pl.ds(first, WINDOW), row == column)

    def big(first, length):
        mask = lax.broadcasted_iota(jnp.int32, (1, B3), 1) < length

        def block(b, carry):
            begin = pl.multiple_of(first + b * MIX_ROWS, 16)
            mix(range(pairs), begin, MIX_ROWS, pl.ds(first, B3), mask)
            return carry

        lax.fori_loop(0, pl.cdiv(B3, MIX_ROWS), block, 0)

    walk_groups(meta, slots, small, big)
    for p in range(pairs):
        heads_own_ref[:, p * 128 : (p + 1) * 128] = mixed_ref[p, pl.ds(first_own, half), :]
        heads_other_ref[:, p * 128 : (p + 1) * 128] = mixed_ref[p, pl.ds(first_other, half), :]


def attention_back_kernel(
    slots, meta, qkv_ref, own_ref, other_ref, w_ref, grad_ref, out_ref, sum_ref
):
    pairs = qkv_ref.shape[1]
    half = own_ref.shape[0]
    total = 2 * half
    first_own = pl.multiple_of(meta[64], half)
    first_other = pl.multiple_of(half - meta[64], half)
    for source, first in ((own_ref, first_own), (other_ref, first_other)):
        part = nt(source[...], w_ref[...]).astype(BF16)
        for p in range(pairs):
            out_ref[p, pl.ds(first, half), :] = part[:, p * 128 : (p + 1) * 128]
    for p in range(pairs):
        out_ref[p, pl.ds(total, WINDOW), :] = jnp.zeros((WINDOW, 128), BF16)
    grad_ref[...] = jnp.zeros(grad_ref.shape, BF16)
    low = lax.broadcasted_iota(jnp.int32, (1, 128), 1) < HEAD_DIM
    lanes = (low, jnp.logical_not(low))

    def back(chosen, first, count, window, mask, rows_in):
        work = []
        for p in chosen:
            q = qkv_ref[0, p, pl.ds(first, count), :]
            keys = qkv_ref[1, p, window, :]
            values = qkv_ref[2, p, window, :]
            grads = out_ref[p, pl.ds(first, count), :]
            if rows_in is not None:
                grads = jnp.where(rows_in, grads, 0)
            for h in range(2):
                q_h = jnp.where(lanes[h], q, 0)
                g_h = jnp.where(lanes[h], grads, 0)
                work.append((nt(keys, q_h), nt(values, g_h), q_h, g_h))
        pieces = []
        for scores, grad_probs, q_h, g_h in work:
            scores = jnp.where(mask, scores, masked_score)
            exponent = jnp.exp(scores - jnp.max(scores, axis=0, keepdims=True))
            probs = exponent * (1.0 / jnp.sum(exponent, axis=0, keepdims=True))
            inner = jnp.sum(probs * grad_probs, axis=0, keepdims=True)
            grad_scores = (probs * (grad_probs - inner)).astype(BF16)
            pieces.append((probs.astype(BF16), grad_scores, q_h, g_h))
        results = []
        for k, p in enumerate(chosen):
            keys = qkv_ref[1, p, window, :]
            d_query = d_key = d_value = 0.0
            for h in range(2):
                probs, grad_scores, q_h, g_h = pieces[2 * k + h]
                d_query = d_query + tn(grad_scores, jnp.where(lanes[h], keys, 0))
                d_key = d_key + nn(grad_scores, q_h)
                d_value = d_value + nn(probs, g_h)
            grad_ref[0, p, pl.ds(first, count), :] = (d_query * 0.125).astype(BF16)
            results.append((d_key, d_value))
        return results

    def small(first, starts, ends, lasts):
        key = slot_ids(lax.broadcasted_iota(jnp.int32, (WINDOW, 1), 0), starts, lasts, 5)
        query = slot_ids(lax.broadcasted_iota(jnp.int32, (1, WINDOW), 1), starts, ends, 4)
        rows_in = slot_ids(lax.broadcasted_iota(jnp.int32, (WINDOW, 1), 0), starts, ends, 4) < 4
        window = pl.ds(first, WINDOW)
        parts = back(range(pairs), first, WINDOW, window, key == query, rows_in)
        for p, (d_key, d_value) in enumerate(parts):
            grad_ref[1, p, window, :] = d_key.astype(BF16)
            grad_ref[2, p, window, :] = d_value.astype(BF16)

    def big(first, length):
        mask = lax.broadcasted_iota(jnp.int32, (B3, 1), 0) < length
        window = pl.ds(first, B3)
        sum_ref[...] = jnp.zeros(sum_ref.shape, F32)

        def block(b, carry):
            begin = pl.multiple_of(first + b * BIG_ROWS, 16)
            rows_in = lax.broadcasted_iota(jnp.int32, (BIG_ROWS, 1), 0) < B3 - b * BIG_ROWS
            for p, parts in enumerate(back(range(pairs), begin, BIG_ROWS, window, mask, rows_in)):
                for c in range(2):
                    sum_ref[c, p] += parts[c]
            return carry

        lax.fori_loop(0, pl.cdiv(B3, BIG_ROWS), block, 0)
        for p in range(pairs):
            for c in range(2):
                grad_ref[1 + c, p, window, :] = sum_ref[c, p].astype(BF16)

    walk_groups(meta, slots, small, big)


def feed_kernel(
    keep_attn,
    meta,
    mine_ref,
    theirs_ref,
    x_ref,
    gb_ref,
    vec_ref,
    wp_ref,
    wp_first_ref,
    wp_second_ref,
    w1_ref,
    w2_ref,
    normed_ref,
    act_ref,
    gpre_ref,
    grad_ref,
    *more,
):
    units = w1_ref.shape[1]
    step = x_ref.shape[1]
    sum_ref = more[-1]
    even = meta[65] == 0
    wp_theirs = jnp.concatenate(
        [
            jnp.where(even, wp_first_ref[...], wp_second_ref[...]),
            jnp.where(even, wp_second_ref[...], wp_first_ref[...]),
        ],
        axis=1,
    )

    def block(rows, carry):
        attn = nn(mine_ref[rows, :], wp_ref[...]) + nn(theirs_ref[rows, :], wp_theirs)
        attn = attn + row_of(vec_ref, 6)
        if keep_attn:
            more[0][rows, :] = attn
        hidden = x_ref[rows, :].astype(F32) + row_of(vec_ref, 4) * attn
        normal, inverse = normed_of(hidden)
        normed = (normal * row_of(vec_ref, 2) + row_of(vec_ref, 3)).astype(BF16)
        normed_ref[rows, :] = normed
        sum_ref[...] = jnp.zeros(sum_ref.shape, F32)

        def chunk(u, carry):
            cols = pl.ds(pl.multiple_of(u * step, step), step)
            shift = row_of(vec_ref, 10)
            for k in range(1, units // step):
                shift = jnp.where(u == k, row_of(vec_ref, 10 + k), shift)
            pre = nn(normed_ref[rows, :], w1_ref[:, cols]) + shift
            half_phi = 0.5 * (1.0 + lax.erf(pre * 0.7071067811865476))
            act_ref[rows, cols] = (pre * half_phi).astype(BF16)
            slope = half_phi + pre * (jnp.exp(pre * pre * -0.5) * 0.3989422804014327)
            gpre = (nt(gb_ref[rows, :], w2_ref[cols, :]) * slope).astype(BF16)
            gpre_ref[rows, cols] = gpre
            sum_ref[...] += nt(gpre, w1_ref[:, cols])
            return carry

        lax.fori_loop(0, units // step, chunk, 0)
        grad_ref[rows, :] = sum_ref[...].astype(BF16)

    block(pl.ds(0, x_ref.shape[0]), 0)


def feed_grad_kernel(
    n_own, n_other, a_own, a_other, p_own, p_other, g_own, g_other, fc1_ref, fc2_ref, bias_ref
):
    units = a_own.shape[1]
    tile = 512

    def block(i, carry):
        cols = pl.ds(pl.multiple_of(i * tile, tile), tile)
        fc1_ref[:, cols] = (
            tn(n_own[...], p_own[:, cols]) + tn(n_other[...], p_other[:, cols])
        ).astype(BF16)
        fc2_ref[cols, :] = (
            tn(a_own[:, cols], g_own[...]) + tn(a_other[:, cols], g_other[...])
        ).astype(BF16)
        bias_ref[:, cols] = jnp.sum(p_own[:, cols].astype(F32), axis=0, keepdims=True) + jnp.sum(
            p_other[:, cols].astype(F32), axis=0, keepdims=True
        )
        return carry

    lax.fori_loop(0, units // tile, block, 0)


def feed_grads(n_own, n_other, a_own, a_other, p_own, p_other, g_own, g_other):
    units = a_own.shape[1]
    width = n_own.shape[1]
    return call(
        feed_grad_kernel,
        [shape((width, units)), shape((units, width)), shape((1, units), F32)],
        (n_own, n_other, a_own, a_other, p_own, p_other, g_own, g_other),
        0.3,
        "feed_grads",
    )


def branch_kernel(act_ref, w2_ref, out_ref):
    def block(rows, carry):
        out_ref[rows, :] = nn(act_ref[rows, :], w2_ref[...]).astype(out_ref.dtype)

    over_rows(act_ref.shape[0], block)


def middle_kernel(
    begin, mine_ref, got_ref, attn_ref, x_ref, gout_ref, vec_ref, hidden_ref, ga_ref, sum_ref
):
    rows = pl.ds(begin, got_ref.shape[0])
    attn = attn_ref[rows, :]
    normal, inverse = normed_of(x_ref[rows, :].astype(F32) + row_of(vec_ref, 4) * attn)
    grad = mine_ref[rows, :].astype(F32) + got_ref[...].astype(F32)
    grad_hidden = gout_ref[rows, :].astype(F32) + norm_back(grad, row_of(vec_ref, 2), normal, inverse)
    hidden_ref[...] = grad_hidden
    grad_attn = (row_of(vec_ref, 4) * grad_hidden).astype(BF16)
    ga_ref[...] = grad_attn
    sums = [
        jnp.sum(v, axis=0, keepdims=True)
        for v in (grad * normal, grad, grad_hidden * attn, grad_attn.astype(F32))
    ]
    for k in range(4):
        sum_ref[k : k + 1, :] = sums[k]


def share_kernel(meta, grad_ref, w_ref, own_ref, other_ref):
    pairs = grad_ref.shape[1]
    half = own_ref.shape[0]
    for first, target in ((half - meta[64], other_ref), (meta[64], own_ref)):

        def block(to_rows, carry):
            rows = pl.ds(pl.multiple_of(first + to_rows.start, WINDOW), WINDOW)
            total = None
            for c in range(3):
                wide = jnp.concatenate([grad_ref[c, p, rows, :] for p in range(pairs)], axis=1)
                part = nt(wide, w_ref[c])
                total = part if total is None else total + part
            target[to_rows, :] = total.astype(BF16)

        over_rows(half, block)


def weight_kernel(flip, meta, grad_ref, n_own, n_other, h_own, h_other, g_own, g_other, *outs):
    pairs = grad_ref.shape[1]
    half = n_own.shape[0]
    local = pairs * 128
    own = pl.ds(pl.multiple_of(meta[64], half), half)
    other = pl.ds(pl.multiple_of(half - meta[64], half), half)
    columns = pl.ds(pl.multiple_of((meta[65] ^ flip) * local, local), local)
    out_ref = outs[0]
    for c in range(3):
        wide_own = jnp.concatenate([grad_ref[c, p, own, :] for p in range(pairs)], axis=1)
        wide_other = jnp.concatenate([grad_ref[c, p, other, :] for p in range(pairs)], axis=1)
        if flip == 0:
            outs[1][c : c + 1, :] = jnp.sum(wide_own.astype(F32), axis=0, keepdims=True) + jnp.sum(
                wide_other.astype(F32), axis=0, keepdims=True
            )
        part = tn(n_own[:, columns], wide_own) + tn(n_other[:, columns], wide_other)
        out_ref[pl.ds(c * local, local), :] = part.astype(BF16)
    part = tn(h_own[...], g_own[:, columns]) + tn(h_other[...], g_other[:, columns])
    out_ref[pl.ds(3 * local, local), :] = part.astype(BF16)


def final_kernel(
    mine_ref, got_ref, x_ref, hidden_ref, mark_ref, vec_ref, tokens_ref, sum_ref
):
    sums = [jnp.zeros((1, x_ref.shape[1]), F32)] * 3
    for first in range(0, x_ref.shape[0], WINDOW):
        rows = pl.ds(first, WINDOW)
        normal, inverse = normed_of(x_ref[rows, :].astype(F32))
        grad = mine_ref[rows, :].astype(F32) + got_ref[rows, :].astype(F32)
        grad_x = hidden_ref[rows, :] + norm_back(grad, row_of(vec_ref, 0), normal, inverse)
        marked = mark_ref[rows, :] > 0.5
        tokens_ref[rows, :] = jnp.where(marked, 0.0, grad_x)
        parts = [
            jnp.sum(v, axis=0, keepdims=True)
            for v in (jnp.where(marked, grad_x, 0.0), grad * normal, grad)
        ]
        sums = [a + b for a, b in zip(sums, parts)]
    for k in range(3):
        sum_ref[k : k + 1, :] = sums[k]


def unpack_kernel(count, meta, mine_ref, core_ref, *refs):
    vector_refs, pair_ref, units_ref = refs[-2 - count : -2], refs[-2], refs[-1]
    qkv_ref, proj_ref = refs[8:10]
    total = mine_ref[...] + core_ref[...]
    for k, ref in enumerate(vector_refs):
        ref[...] = total[k]
    width, local = total.shape[1], qkv_ref.shape[2]
    for k in range(2):
        pair_ref[k : k + 1, :] = total[count : count + 1, k * local : (k + 1) * local]
    for k in range(count + 1, total.shape[0]):
        units_ref[pl.ds((k - count - 1) * width, width)] = total[k]
    for k, ref in enumerate(refs[:8]):
        begin = pl.ds(pl.multiple_of((meta[65] ^ (k % 2)) * local, local), local)
        block = (meta[66] ^ (k // 2 % 2)) * 2 + (meta[67] ^ (k // 4))

        @pl.when(block < 3)
        def first(ref=ref, begin=begin, block=block):
            qkv_ref[block, begin, :] = ref[...].astype(F32)

        @pl.when(block == 3)
        def second(ref=ref, begin=begin):
            proj_ref[:, begin] = ref[...].astype(F32)


def own_validity(lengths, buckets, first_own, own_rows):
    slots = lengths.shape[0]
    rows = jnp.where(buckets == 0, B0, jnp.where(buckets == 1, B1, jnp.where(buckets == 2, B2, B3)))
    padded = jnp.where(lengths > 0, rows, 0).astype(jnp.int32)
    before = jnp.tril(jnp.ones((slots, slots), jnp.int32), -1)
    starts = jnp.sum(before * padded[None, :], axis=1)
    ids = first_own + lax.broadcasted_iota(jnp.int32, (own_rows, slots), 0)
    inside = (ids >= starts[None, :]) & (ids < (starts + lengths)[None, :])
    return jnp.any(inside, axis=1, keepdims=True)


def chip_bits():
    return list(range(1, lax.axis_size("wide").bit_length() - 1))


def hop(value, flip):
    size = lax.axis_size("wide")
    return lax.ppermute(value, "wide", tuple((i, i ^ flip) for i in range(size)))


def bits_at(shift, count=1):
    return ((lax.axis_index("wide") >> shift) % (1 << count)).astype(jnp.int32)


def fold_kernel(parts, place, meta, mine_ref, got_ref, *out_refs):
    rows = out_refs[0].shape[0]
    for flip, out_ref in enumerate(out_refs):
        start = pl.multiple_of((meta[place] ^ flip) * rows, rows)
        total = mine_ref[pl.ds(start, rows), :].astype(F32) + got_ref[pl.ds(start, rows), :].astype(F32)
        out_ref[...] = total.astype(BF16)


def fold(meta, mine, got, parts, place, index):
    rows = mine.shape[0] // parts
    if rows % 32:
        total = (mine.astype(F32) + got.astype(F32)).astype(BF16)
        return [
            lax.dynamic_slice_in_dim(total, (index ^ flip) * rows, rows) for flip in range(parts)
        ]
    return call(
        partial(fold_kernel, parts, place),
        [shape((rows, mine.shape[1]))] * parts,
        (meta, mine, got),
        1,
        "fold",
        scalars=1,
    )


def gather_kernel(place, meta, *refs):
    out_ref = refs[-1]
    rows = refs[0].shape[0]
    for flip, ref in enumerate(refs[:-1]):
        start = pl.multiple_of((meta[place] ^ flip) * rows, rows)
        out_ref[pl.ds(start, rows), :] = ref[...]


def gather(meta, pieces, place, index):
    rows, columns = pieces[0].shape
    if rows % 32:
        total = jnp.zeros((rows * len(pieces), columns), pieces[0].dtype)
        for flip, piece in enumerate(pieces):
            total = lax.dynamic_update_slice_in_dim(total, piece, (index ^ flip) * rows, 0)
        return total
    return call(
        partial(gather_kernel, place),
        shape((rows * len(pieces), columns)),
        (meta, *pieces),
        1,
        "gather",
        scalars=1,
    )


def quarter(w_proj, bit):
    rows, columns = w_proj.shape[0] // 2, w_proj.shape[1] // 2
    part = lax.dynamic_slice(w_proj, (bits_at(bit) * rows, bits_at(0) * columns), (rows, columns))
    return lax.ppermute(part, "narrow", SWAP)


def shards(
    tokens,
    token_marks,
    crop_lengths,
    bucket_ids,
    mask_token,
    norm1_gain,
    norm1_bias,
    w_qkv,
    qv_bias,
    w_proj,
    proj_bias,
    scale_attn,
    norm2_gain,
    norm2_bias,
    w_fc1,
    fc1_bias,
    w_fc2,
    fc2_bias,
    scale_mlp,
    cotangent,
):
    half, width = tokens.shape
    slots = crop_lengths.shape[0]
    local = w_qkv.shape[2]
    pairs = local // 128
    units = w_fc1.shape[1]
    first_own = (lax.axis_index("narrow") * half).astype(jnp.int32)
    swap = lambda v: lax.ppermute(v, "narrow", SWAP)
    singles = chip_bits()

    tokens_other = swap(tokens)
    marks_other = swap(token_marks)
    valid = own_validity(crop_lengths, bucket_ids, first_own, half)
    scale2 = scale_mlp.astype(F32)
    gout_own = jnp.where(valid, cotangent, 0).astype(BF16)
    gb_own = (scale2 * gout_own.astype(F32)).astype(BF16)
    pad = jnp.zeros((32 - slots,), jnp.int32)
    meta = jnp.concatenate(
        [
            crop_lengths,
            pad,
            bucket_ids,
            pad,
            jnp.stack(
                [first_own, bits_at(0)] + [bits_at(bit) for bit in singles]
            ),
        ]
    )
    table = [
        norm1_gain,
        norm1_bias,
        norm2_gain,
        norm2_bias,
        scale_attn,
        scale_mlp,
        proj_bias,
        fc2_bias,
        mask_token,
        qv_bias.reshape(width),
    ] + [fc1_bias[k * width : (k + 1) * width] for k in range(units // width)]
    lines = lax.broadcasted_iota(jnp.int32, (len(table), width), 0)
    vec = jnp.zeros((len(table), width), BF16)
    for k, line in enumerate(table):
        vec = jnp.where(lines == k, line[None, :], vec)

    def qkv(rows, marks):
        return call(
            qkv_kernel,
            [shape((half, width)), shape((3, pairs, half, 128)), shape((half, width))],
            (rows, marks, vec, w_qkv),
            2,
            "norm_qkv",
        )

    mark_column = (token_marks == 1).astype(F32)[:, None]
    n_own, qkv_own, x_own = qkv(tokens, mark_column)
    n_own, wp_start = lax.optimization_barrier((n_own, w_proj))
    wp_mine = quarter(wp_start, singles[0])
    tokens_other, gb_start = lax.optimization_barrier((tokens_other, gb_own))
    gb_other = swap(gb_start)
    heads_own, heads_other, qkv_all, n_other, x_other = call(
        partial(attention_kernel, slots),
        [
            shape((half, local)),
            shape((half, local)),
            shape((3, pairs, 2 * half + WINDOW, 128)),
            shape((half, width)),
            shape((half, width)),
        ],
        (meta, qkv_own, tokens_other, (marks_other == 1).astype(F32)[:, None], vec, w_qkv),
        12,
        "attention",
        scratch=[pltpu.VMEM((pairs, 2 * half + WINDOW, 128), BF16)],
        scalars=1,
    )
    heads_own, heads_other, wp_mine = lax.optimization_barrier((heads_own, heads_other, wp_mine))
    wp_side = hop(wp_mine, 1 << singles[0])
    heads_own, heads_other, gb_other, wp_side = lax.optimization_barrier(
        (heads_own, heads_other, gb_other, wp_side)
    )
    got_other = swap(heads_own)
    got_own = swap(heads_other)
    wp_mine = gather(meta, [wp_mine, wp_side], 66, bits_at(singles[0]))
    wp_next = hop(wp_mine, 1)

    def feed(mine, theirs, x, gb, keep):
        outs = [shape((half, width)), shape((half, units)), shape((half, units)), shape((half, width))]
        if keep:
            outs.append(shape((half, width), F32))
        return call(
            partial(feed_kernel, keep),
            outs,
            (meta, mine, theirs, x, gb, vec, w_proj, wp_mine, wp_next, w_fc1, w_fc2),
            7,
            "feed",
            scratch=[pltpu.VMEM((half, width), F32)],
            scalars=1,
        )

    n2_other, act_other, gpre_other, gn2_other = feed(
        heads_other, got_other, x_other, gb_other, False
    )
    gn2_got = swap(gn2_other)
    n2_own, act_own, gpre_own, gn2_own, attn_own = feed(
        heads_own, got_own, x_own, gb_own, True
    )
    g_fc1, g_fc2, g_fc1b = feed_grads(
        n2_own, n2_other, act_own, act_other, gpre_own, gpre_other, gb_own, gb_other
    )
    gn2_got, g_fc1, g_fc2 = lax.optimization_barrier((gn2_got, g_fc1, g_fc2))
    grad_hidden, ga_own, sums2 = call(
        partial(middle_kernel, 0),
        [shape((half, width), F32), shape((half, width)), shape((4, width), F32)],
        (gn2_own, gn2_got, attn_own, x_own, gout_own, vec),
        0.2,
        "middle",
    )
    sum_fc1, sum_fc2 = lax.psum((g_fc1, g_fc2), "wide")

    operands = (
        attn_own, x_own, gout_own, gb_own, act_own, act_other, qkv_all, n_own, n_other,
        heads_own, heads_other, g_fc1b, grad_hidden, ga_own, sums2
    )

    def rest(operands):
        (
            attn_own, x_own, gout_own, gb_own, act_own, act_other, qkv_all, n_own, n_other, heads_own, heads_other, g_fc1b, grad_hidden, ga_own, sums2
        ) = operands
        ga_other = swap(ga_own)

        def branch_of(act, kind):
            return call(
                branch_kernel, shape((half, width), kind), (act, w_fc2), 2, "branch"
            )

        branch_got = swap(branch_of(act_other, BF16))
        branch_own = branch_of(act_own, F32)
        ga_other, branch_own = lax.optimization_barrier((ga_other, branch_own))
        ga = (ga_own, ga_other)
        d_qkv = call(
            partial(attention_back_kernel, slots),
            shape((3, pairs, 2 * half + WINDOW, 128)),
            (meta, qkv_all, *ga, w_proj),
            9,
            "attention_back",
            scratch=[
                pltpu.VMEM((pairs, 2 * half + WINDOW, 128), BF16),
                pltpu.VMEM((2, pairs, B3, 128), F32),
            ],
            scalars=1,
        )
        d_qkv, branch_got = lax.optimization_barrier((d_qkv, branch_got))
        arrays = (n_own, n_other, heads_own, heads_other, *ga)
        (give,) = call(
            partial(weight_kernel, 1),
            [shape((2 * width, local))],
            (meta, d_qkv, *arrays),
            2,
            "weights_give",
            scalars=1,
        )
        d_qkv, give = lax.optimization_barrier((d_qkv, give))
        got = hop(give, 1)
        keep, d_bias = call(
            partial(weight_kernel, 0),
            [shape((2 * width, local)), shape((3, local), F32)],
            (meta, d_qkv, *arrays),
            2,
            "weights_keep",
            scalars=1,
        )
        d_qkv, keep, got = lax.optimization_barrier((d_qkv, keep, got))
        gn1_own, gn1_other = call(
            share_kernel,
            [shape((half, width)), shape((half, width))],
            (meta, d_qkv, w_qkv),
            3,
            "share",
            scalars=1,
        )
        gn1_got = swap(gn1_other)
        branch = branch_own + branch_got.astype(F32) + fc2_bias.astype(F32)
        hidden = x_own.astype(F32) + scale_attn.astype(F32) * attn_own
        output = jnp.where(valid, hidden + scale2 * branch, 0.0).astype(BF16)
        g_smlp = jnp.sum(gout_own.astype(F32) * branch, axis=0)
        g_fc2b = jnp.sum(gb_own.astype(F32), axis=0)
        for k, bit in enumerate(singles):
            keep, give = fold(meta, keep, got, 2, 66 + k, bits_at(bit))
            got = hop(give, 1 << bit)
            if k == 0:
                got, output, g_smlp, g_fc2b, gn1_own = lax.optimization_barrier(
                    (got, output, g_smlp, g_fc2b, gn1_own)
                )
        keep, gn1_got = lax.optimization_barrier((keep, gn1_got))
        grad_tokens, sums1 = call(
            final_kernel,
            [shape((half, width), F32), shape((3, width), F32)],
            (gn1_own, gn1_got, x_own, grad_hidden, mark_column, vec),
            3,
            "final",
        )
        got, grad_tokens = lax.optimization_barrier((got, grad_tokens))
        part = (keep.astype(F32) + got.astype(F32)).astype(BF16)
        wide_only = jnp.concatenate([d_bias[0], d_bias[2], g_fc1b[0]]).reshape(-1, width)
        small = jnp.concatenate([sums1, sums2, g_fc2b[None], g_smlp[None], wide_only], axis=0)
        for k in range(len(singles) - 1, 1, -1):
            part, small = lax.optimization_barrier((part, small))
            pieces = [part, hop(part, 1 << singles[k])]
            small = small + hop(small, 1 << singles[k])
            part = gather(meta, pieces, 66 + k, bits_at(singles[k]))
        part, small = lax.optimization_barrier((part, small))
        side, near = 1 << singles[0], 1 << singles[1]
        next_part, beside, across = hop(part, near), hop(part, side), hop(part, 1)
        small = small + hop(small, near)
        next_part, beside, across, small = lax.optimization_barrier((next_part, beside, across, small))
        next_beside, next_across, corner = hop(next_part, side), hop(next_part, 1), hop(beside, 1)
        count = 9
        flip = 2 * side + 1
        size = 2 * lax.axis_size("wide")
        opposite = lax.ppermute(
            small[:count], ("wide", "narrow"), tuple((i, i ^ flip) for i in range(size))
        )
        shared = small[:count] + swap(small[:count]) + opposite
        small = jnp.concatenate([shared, small[count:]], axis=0) + hop(small, side)
        next_beside, next_across, corner, small = lax.optimization_barrier(
            (next_beside, next_across, corner, small)
        )
        next_corner = hop(next_beside, 1)
        g_qkv, g_proj, *vectors, g_qvb, g_fc1b = call(
            partial(unpack_kernel, count),
            [shape((3, width, local), F32), shape((local, width), F32)]
            + [shape((width,), F32)] * count
            + [shape((2, local), F32), shape((units,), F32)],
            (meta, small, hop(small, 1), part, across, beside, corner, next_part, next_across, next_beside, next_corner),
            3,
            "unpack",
            scalars=1,
        )
        return output, grad_tokens, vectors, g_qvb, g_fc1b, g_qkv, g_proj

    def none(operands):
        return jax.tree.map(lambda v: jnp.zeros(v.shape, v.dtype), jax.eval_shape(rest, operands))

    output, grad_tokens, rows, g_qvb, g_fc1b, g_qkv, g_proj = lax.cond(
        jnp.max(crop_lengths) < 65536, rest, none, operands
    )
    return (
        output,
        grad_tokens,
        rows[0],
        rows[1],
        rows[2],
        g_qkv,
        g_qvb,
        g_proj,
        rows[6],
        rows[5],
        rows[3],
        rows[4],
        sum_fc1.astype(F32),
        g_fc1b,
        sum_fc2.astype(F32),
        rows[7],
        rows[8],
    )


def solution(mesh):
    rows = P(("wide", "narrow"), None)
    return jax.shard_map(
        shards,
        mesh=mesh,
        in_specs=(
            rows,
            P(("wide", "narrow")),
            P("wide"),
            P("wide"),
            P(),
            P(),
            P(),
            P(None, None, "narrow"),
            P(None, "narrow"),
            P("narrow", None),
            P(),
            P(),
            P(),
            P(),
            P(None, "narrow"),
            P("narrow"),
            P("narrow", None),
            P(),
            P(),
            rows,
        ),
        out_specs=(
            rows,
            rows,
            P(),
            P(),
            P(),
            P(None, None, "narrow"),
            P(None, "narrow"),
            P("narrow", None),
            P(),
            P(),
            P(),
            P(),
            P(None, "narrow"),
            P("narrow"),
            P("narrow", None),
            P(),
            P(),
        ),
        check_vma=False,
    )
```
